512 devices in a mesh: gx: 16 (over z), gy: 8 (over y, core), gz: 4 (over x).
Axes of the slice: x: 4, y: 4, z: 16, core: 2. Of those that a mesh axis runs over, the one named last changes fastest.
Arguments:
- right_side: float32 [256, 128, 512], P('gx', 'gy', 'gz'), may hold values from -6 to 6
- conductivity: float32 [256, 128, 512], P('gx', 'gy', 'gz'), may hold values from 0.3 to 3
Outputs:
- solution_field: float32 [256, 128, 512], P('gx', 'gy', 'gz')
The draws below stay inside these ranges and needn't reach their ends.
All inputs are finite; a program needn't handle non-finite values.
Results may differ from the reference program's by a relative error of at most 0.0001.
Values sent between devices are 32-bit elements; how exact they have to be, the bound alone decides.
No kernel may reach another device: no remote copies, remote signals or barrier semaphores. Data moves between devices by JAX's collectives and lax.ppermute only.
A program may use at most 64 MiB of HBM per device.

```python
import math
import jax
import jax.numpy as jnp
from jax import lax

LEVELS = 4
SWEEPS = 2
COARSE_SWEEPS = 8
NX = 256
NY = 128
NZ = 512


def draw_right_side(key, part):
    return jnp.clip(jax.random.normal(key, (NX, NY, NZ), jnp.float32), -6.0, 6.0)


def steps_of(key, dims, split, smallest, top_value):
    level = 1.0
    for dim, blocks in split:
        draws = jax.random.uniform(jax.random.fold_in(jax.random.fold_in(key, 6), dim), (blocks,), jnp.float32, smallest / len(split), top_value / len(split))
        level = level * jnp.repeat(jnp.exp(draws), dims[dim] // blocks).reshape((-1,) + (1,) * (len(dims) - 1 - dim))
    return level


def setup_inputs(seed: int = 0) -> dict:
    streams_of = jax.random.split(jax.random.key(seed), 3)
    return {
        "right_side": draw_right_side(jax.random.fold_in(streams_of[2], 71), 0),
        "conductivity": jnp.clip(jnp.exp(math.log(3.0) - 2.3025851 * jax.random.uniform(streams_of[1], (NX, NY, NZ), jnp.float32) ** steps_of(streams_of[1], (NX, NY, NZ), ((0, 16), (1, 8), (2, 4)), -0.2, 0.2)), 0.3, 3.0),
    }


def pad_zero(field):
    return jnp.pad(field, 1)


def face_values(conduct, padder):
    padded = padder(conduct)
    face_first = 0.5 * (padded[:-1, 1:-1, 1:-1] + padded[1:, 1:-1, 1:-1])
    face_second = 0.5 * (padded[1:-1, :-1, 1:-1] + padded[1:-1, 1:, 1:-1])
    face_third = 0.5 * (padded[1:-1, 1:-1, :-1] + padded[1:-1, 1:-1, 1:])
    return face_first, face_second, face_third


def apply_operator(field, face_terms, factor, padder):
    face_first, face_second, face_third = face_terms
    padded = padder(field)
    total = face_first[:-1] * (field - padded[:-2, 1:-1, 1:-1]) + face_first[1:] * (field - padded[2:, 1:-1, 1:-1])
    total = total + face_second[:, :-1] * (field - padded[1:-1, :-2, 1:-1]) + face_second[:, 1:] * (field - padded[1:-1, 2:, 1:-1])
    total = total + face_third[:, :, :-1] * (field - padded[1:-1, 1:-1, :-2]) + face_third[:, :, 1:] * (field - padded[1:-1, 1:-1, 2:])
    return factor * total


def diagonal_of(face_terms, factor):
    face_first, face_second, face_third = face_terms
    total = face_first[:-1] + face_first[1:] + face_second[:, :-1] + face_second[:, 1:]
    total = total + face_third[:, :, :-1] + face_third[:, :, 1:]
    return factor * total


def red_cells(extent):
    index_x = lax.broadcasted_iota(jnp.int32, extent, 0)
    index_y = lax.broadcasted_iota(jnp.int32, extent, 1)
    index_z = lax.broadcasted_iota(jnp.int32, extent, 2)
    return (index_x + index_y + index_z) % 2 == 0


def smooth(source, face_terms, factor, count, padder):
    inverse = 1.0 / diagonal_of(face_terms, factor)
    red = red_cells(source.shape)
    iterate = jnp.zeros(source.shape, jnp.float32)
    for sweep in range(count):
        for chosen in (red, jnp.logical_not(red)):
            update = iterate + (source - apply_operator(iterate, face_terms, factor, padder)) * inverse
            iterate = jnp.where(chosen, update, iterate)
    return iterate


def restrict(field):
    size_x, size_y, size_z = field.shape
    blocks = field.reshape(size_x // 2, 2, size_y // 2, 2, size_z // 2, 2)
    return jnp.sum(blocks, axis=(1, 3, 5)) * 0.125


def prolong(field):
    size_x, size_y, size_z = field.shape
    spread = jnp.broadcast_to(field[:, None, :, None, :, None], (size_x, 2, size_y, 2, size_z, 2))
    return spread.reshape(size_x * 2, size_y * 2, size_z * 2)


def descend(source, conduct, level, padder):
    factor = 0.25 ** level
    face_terms = face_values(conduct, padder)
    iterate = smooth(source, face_terms, factor, SWEEPS, padder)
    residual = source - apply_operator(iterate, face_terms, factor, padder)
    return restrict(residual), restrict(conduct), iterate


def reference(right_side, conductivity):
    source, conduct = right_side, conductivity
    stored = []
    for level in range(LEVELS):
        source, conduct, iterate = descend(source, conduct, level, pad_zero)
        stored.append(iterate)
    face_terms = face_values(conduct, pad_zero)
    iterate = smooth(source, face_terms, 0.25 ** LEVELS, COARSE_SWEEPS, pad_zero)
    for level in reversed(range(LEVELS)):
        iterate = stored[level] + prolong(iterate)
    return iterate
```

```python
import jax
import jax.numpy as jnp
from jax import lax
from jax.experimental import pallas as pl
from jax.experimental.pallas import tpu as pltpu
from jax.sharding import PartitionSpec as P

F_HALO = 12
B_HALO = 13
BLOCK = 16
F_PLANES = BLOCK + 2 * F_HALO
B_PLANES = BLOCK + 2 * B_HALO
PLANES = F_PLANES + B_PLANES
GROUPS = -(-PLANES // 8)
F_GROUPS = F_PLANES // 8
ROWS = 48
LANES = 256
COARSE_SWEEPS = 8
F32 = jnp.float32


def iota(shape, dim):
    return lax.broadcasted_iota(jnp.int32, shape, dim)


def split_matmul(value, selector):
    high = value.astype(jnp.bfloat16)
    low = (value - high.astype(F32)).astype(jnp.bfloat16)
    return jnp.dot(high, selector, preferred_element_type=F32) + jnp.dot(
        low, selector, preferred_element_type=F32
    )


def selector_of(condition):
    return jnp.where(condition, 1.0, 0.0).astype(jnp.bfloat16)


def pair_selector(source_lanes, first, out_lanes, offset, count):
    source = iota((source_lanes, out_lanes), 0) - first
    target = iota((source_lanes, out_lanes), 1) - offset
    return selector_of(
        (source >= 0) & (source < 2 * count) & ((source >> 1) == target)
    )


def spread_selector(first, offset, count):
    source = iota((128, 128), 0) - first
    target = iota((128, 128), 1) - offset
    return selector_of((source >= 0) & (source < count) & ((target >> 1) == source))


def ring_sum(value):
    rows, lanes = value.shape
    return (
        pltpu.roll(value, 1, 0)
        + pltpu.roll(value, rows - 1, 0)
        + pltpu.roll(value, 1, 1)
        + pltpu.roll(value, lanes - 1, 1)
    )


def stencil(v_ref, b_ref, g_ref, plane):
    v = v_ref[plane]
    v_low, v_high = v_ref[plane - 1], v_ref[plane + 1]
    b = b_ref[plane]
    near_v = v_low + v_high + ring_sum(v)
    near_w = b_ref[plane - 1] * v_low + b_ref[plane + 1] * v_high + ring_sum(b * v)
    return v, g_ref[plane] + b * near_v + near_w


def diagonal(b_ref, plane):
    b = b_ref[plane]
    total = 6.0 * b + b_ref[plane - 1] + b_ref[plane + 1] + ring_sum(b)
    return total, jnp.where(b > 0.0, 1.0 / jnp.where(b > 0.0, total, 1.0), 0.0)


def parity_of(rows, lanes):
    return (iota((rows, lanes), 0) + iota((rows, lanes), 1)) & 1


def ring_level(b_ref, g_ref, v_ref, d_ref, i_ref, first, last, shift, parity):
    @pl.loop(first, last)
    def _(plane):
        total, inverse = diagonal(b_ref, plane)
        d_ref[plane] = total
        i_ref[plane] = inverse
        red = parity == ((plane + shift) & 1)
        v_ref[plane] = jnp.where(red, g_ref[plane] * inverse, 0.0)

    for colour in (1, 0, 1):

        @pl.loop(first, last)
        def _(plane):
            v, total = stencil(v_ref, b_ref, g_ref, plane)
            chosen = parity == ((plane + shift + colour) & 1)
            v_ref[plane] = jnp.where(chosen, total * i_ref[plane], v)


def pack_kernel(f_ref, b_ref, low_ref, high_ref, main_ref, left_ref, right_ref):
    lane = iota((BLOCK, 128), 1)

    def source(index):
        if index < F_HALO:
            return low_ref[index]
        if index < F_HALO + BLOCK:
            return f_ref[index - F_HALO]
        if index < F_PLANES:
            return high_ref[index - F_HALO - BLOCK]
        index -= F_PLANES
        if index < B_HALO:
            return low_ref[F_HALO + index]
        if index < B_HALO + BLOCK:
            return b_ref[index - B_HALO]
        return high_ref[F_HALO + index - B_HALO - BLOCK]

    for group in range(GROUPS):
        left = jnp.zeros((BLOCK, 128), F32)
        right = jnp.zeros((BLOCK, 128), F32)
        for slot in range(8):
            index = group * 8 + slot
            if index >= PLANES:
                break
            plane = source(index)
            main_ref[index] = plane
            here = (lane >> 4) == slot
            first = pltpu.roll(plane, 16 * slot, 1) if slot else plane
            final = pltpu.roll(plane, 16 * slot + 16, 1) if slot < 7 else plane
            left = jnp.where(here, first, left)
            right = jnp.where(here, final, right)
        left_ref[group] = left
        right_ref[group] = right


def fine_kernel(
    low_ref, own_ref, high_ref,
    u0_ref, u1_ref, coarse_ref,
    b0, g0, v0, d0, i0, pair_a, pair_b, stack_g, stack_b,
    b1, g1, v1, d1, i1, pair_1, collect,
):
    lane = iota((BLOCK, 128), 1)

    def place(target, plane, scale, index, group, slot):
        for part, source in enumerate((low_ref, own_ref, high_ref)):
            rows = slice(BLOCK * part, BLOCK * part + BLOCK)
            right = source[PLANES + group]
            left = source[PLANES + GROUPS + group]
            if slot:
                right = pltpu.roll(right, 128 - 16 * slot, 1)
            if slot < 7:
                left = pltpu.roll(left, 112 - 16 * slot, 1)
            side = jnp.where(lane < 16, right, jnp.where(lane >= 112, left, 0.0))
            target[plane, rows, 0:128] = source[index] * scale
            target[plane, rows, 128:256] = side * scale

    @pl.loop(0, F_GROUPS)
    def _(group):
        for slot in range(8):
            index = group * 8 + slot
            place(g0, index + 1, 2.0, index, group, slot)

    @pl.loop(F_GROUPS, GROUPS - 1)
    def _(group):
        for slot in range(8):
            index = group * 8 + slot
            place(b0, index - F_PLANES, 1.0, index, group, slot)

    for slot in range(PLANES - 8 * (GROUPS - 1)):
        index = 8 * (GROUPS - 1) + slot
        place(b0, index - F_PLANES, 1.0, index, GROUPS - 1, slot)

    zero = jnp.zeros((ROWS, LANES), F32)
    v0[0] = zero
    v0[B_PLANES - 1] = zero

    parity = parity_of(ROWS, LANES)
    ring_level(b0, g0, v0, d0, i0, 1, B_PLANES - 1, 1, parity)
    for plane in range(BLOCK):
        u0_ref[plane] = v0[plane + B_HALO, BLOCK : 2 * BLOCK, 0:128]

    stack_g[...] = jnp.zeros((20, 24, LANES), F32)

    def pair_rows(value, stack, index):
        pair_a[...] = value[:, 0:128]
        pair_b[...] = value[:, 128:256]
        for pair, lanes in ((pair_a, slice(0, 128)), (pair_b, slice(128, 256))):
            stack[index, :, lanes] = (
                pair[pl.ds(0, 24, stride=2), :] + pair[pl.ds(1, 24, stride=2), :]
            )

    @pl.loop(2, 18)
    def _(index):
        total = zero
        for plane in (2 * index + 1, 2 * index + 2):
            v, value = stencil(v0, b0, g0, plane)
            rest = value - d0[plane] * v
            total = total + jnp.where(b0[plane] > 0.0, rest, 0.0)
        pair_rows(total, stack_g, index)

    @pl.loop(0, 20)
    def _(index):
        pair_rows(b0[2 * index + 1] + b0[2 * index + 2], stack_b, index)

    halve = pair_selector(256, 0, 128, 0, 128)
    g1[...] = 0.5 * split_matmul(stack_g[...].reshape(480, 256), halve).reshape(20, 24, 128)
    b1[...] = 0.125 * split_matmul(stack_b[...].reshape(480, 256), halve).reshape(20, 24, 128)

    small = jnp.zeros((24, 128), F32)
    v1[1] = small
    v1[18] = small
    ring_level(b1, g1, v1, d1, i1, 2, 18, 0, parity_of(24, 128))
    for plane in range(8):
        u1_ref[plane] = v1[plane + 6, 8:16]

    collect[...] = jnp.zeros((4, 16, 128), F32)

    def pack_rows(value, row):
        pair_1[...] = value
        four = pair_1[pl.ds(8, 4, stride=2), :] + pair_1[pl.ds(9, 4, stride=2), :]
        for part in range(4):
            collect[part, row : row + 1, :] = four[part : part + 1]

    for index in range(4):
        total = small
        for plane in (2 * index + 6, 2 * index + 7):
            v, value = stencil(v1, b1, g1, plane)
            total = total + (value - d1[plane] * v)
        pack_rows(0.5 * total, index)
    for index in range(6):
        pack_rows(0.125 * (b1[2 * index + 4] + b1[2 * index + 5]), 4 + index)
    out = jnp.zeros((16, 128), F32)
    for part in range(4):
        out = out + split_matmul(collect[part], pair_selector(128, 0, 128, 32 * part, 32))
    coarse_ref[...] = out


def slab_kernel(gathered_ref, u2_ref, coarse_ref, b2, g2, v2, d2, i2, pair_2):
    row = iota((4, 8, 128), 1)
    lane = iota((4, 8, 128), 2)
    group = lane >> 5
    turn = (group - row) & 3

    def exchange(value):
        value = value.reshape(4, 8, 128)
        out = value
        for d in (1, 2, 3):
            moved = pltpu.roll(value, 32 * d, 2)
            near = pltpu.roll(moved, 8 - d, 1)
            far = pltpu.roll(moved, 4 - d, 1)
            out = jnp.where(turn == d, jnp.where(group >= d, near, far), out)
        return out.reshape(32, 128)

    zero = jnp.zeros((32, 128), F32)
    for plane in range(12):
        g2[plane + 1] = exchange(gathered_ref[pl.ds(plane, 32, stride=32), :])
    for plane in range(14):
        b2[plane] = exchange(gathered_ref[pl.ds(plane + 12, 32, stride=32), :])
    for plane in (0, 13):
        v2[plane] = zero

    row = iota((32, 128), 0)
    lane = iota((32, 128), 1)
    parity = (row + lane) & 1

    def edge_sum(value):
        return (
            jnp.where(row > 0, pltpu.roll(value, 1, 0), 0.0)
            + jnp.where(row < 31, pltpu.roll(value, 31, 0), 0.0)
            + jnp.where(lane > 0, pltpu.roll(value, 1, 1), 0.0)
            + jnp.where(lane < 127, pltpu.roll(value, 127, 1), 0.0)
        )

    def value_of(plane):
        v, v_low, v_high = v2[plane], v2[plane - 1], v2[plane + 1]
        b = b2[plane]
        near_v = v_low + v_high + edge_sum(v)
        near_w = b2[plane - 1] * v_low + b2[plane + 1] * v_high + edge_sum(b * v)
        return v, g2[plane] + b * near_v + near_w

    @pl.loop(1, 13)
    def _(plane):
        b = b2[plane]
        total = 6.0 * b + b2[plane - 1] + b2[plane + 1] + edge_sum(b)
        inverse = jnp.where(b > 0.0, 1.0 / jnp.where(b > 0.0, total, 1.0), 0.0)
        d2[plane] = total
        i2[plane] = inverse
        v2[plane] = jnp.where(parity == ((plane + 1) & 1), g2[plane] * inverse, 0.0)

    for colour in (1, 0, 1):

        @pl.loop(1, 13)
        def _(plane):
            v, value = value_of(plane)
            chosen = parity == ((plane + 1 + colour) & 1)
            v2[plane] = jnp.where(chosen, value * i2[plane], v)

    for plane in range(4):
        u2_ref[plane] = v2[plane + 5]
    g_out = jnp.zeros((16, 128), F32)
    b_out = jnp.zeros((16, 128), F32)
    for part in range(2):
        halve = pair_selector(128, 0, 128, 64 * part, 64)
        total = zero
        for plane in (5 + 2 * part, 6 + 2 * part):
            v, value = value_of(plane)
            total = total + (value - d2[plane] * v)
        pair_2[...] = total
        rows = pair_2[pl.ds(0, 16, stride=2), :] + pair_2[pl.ds(1, 16, stride=2), :]
        g_out = g_out + split_matmul(0.5 * rows, halve)
        pair_2[...] = b2[5 + 2 * part] + b2[6 + 2 * part]
        rows = pair_2[pl.ds(0, 16, stride=2), :] + pair_2[pl.ds(1, 16, stride=2), :]
        b_out = b_out + split_matmul(0.125 * rows, halve)
    coarse_ref[0:16] = g_out
    coarse_ref[16:32] = b_out


def smooth_whole(b, g, near, red, sweeps):
    total = 6.0 * b + near(b)
    inverse = jnp.where(b > 0.0, 1.0 / jnp.where(b > 0.0, total, 1.0), 0.0)

    def value_of(v):
        return g + b * near(v) + near(b * v)

    v = jnp.where(red, g * inverse, 0.0)
    v = jnp.where(red, v, value_of(v) * inverse)

    def sweep(_, v):
        v = jnp.where(red, value_of(v) * inverse, v)
        return jnp.where(red, v, value_of(v) * inverse)

    v = lax.fori_loop(1, sweeps, sweep, v)
    return v, value_of(v) - total * v


def beside(value):
    edge = jnp.zeros_like(value[:1])
    return (
        jnp.concatenate([edge, value[:-1]], axis=0),
        jnp.concatenate([value[1:], edge], axis=0),
    )


def coarse_kernel(
    gathered_ref, u0_ref, u1_ref, u2_ref, out_ref,
    v3, u4, pair_3, twice_3, twice_2, twice_1, twice_0, level_1,
):
    at_x = lax.axis_index("gx")
    at_y = lax.axis_index("gy")
    at_z = lax.axis_index("gz")

    shape = (16, 16, 128)
    row, lane = iota(shape, 1), iota(shape, 2)
    cell = lane & 63

    def near_3(value):
        swapped = pltpu.roll(value, 64, 2)
        low, high = beside(swapped)
        return (
            swapped
            + jnp.where(lane < 64, low, high)
            + jnp.where(row > 0, pltpu.roll(value, 1, 1), 0.0)
            + jnp.where(row < 15, pltpu.roll(value, 15, 1), 0.0)
            + jnp.where(cell > 0, pltpu.roll(value, 1, 2), 0.0)
            + jnp.where(cell < 63, pltpu.roll(value, 127, 2), 0.0)
        )

    g3 = gathered_ref[:, 0:16]
    b3 = gathered_ref[:, 16:32]
    red = (((lane >> 6) + row + cell) & 1) == 0
    v, rest = smooth_whole(b3, g3, near_3, red, 2)
    v3[...] = v
    halve = pair_selector(128, 0, 128, 0, 32)

    def restrict_3(value):
        value = value + pltpu.roll(value, 64, 2)
        pair_3[...] = value.reshape(256, 128)
        rows = pair_3[pl.ds(0, 128, stride=2), :] + pair_3[pl.ds(1, 128, stride=2), :]
        return split_matmul(rows, halve).reshape(16, 8, 128)

    g4 = 0.5 * restrict_3(rest)
    b4 = 0.125 * restrict_3(b3)

    shape = (16, 8, 128)
    plane, row, lane = iota(shape, 0), iota(shape, 1), iota(shape, 2)

    def near_4(value):
        low, high = beside(value)
        return (
            low
            + high
            + jnp.where(row > 0, pltpu.roll(value, 1, 1), 0.0)
            + jnp.where(row < 7, pltpu.roll(value, 7, 1), 0.0)
            + pltpu.roll(value, 1, 2)
            + pltpu.roll(value, 127, 2)
        )

    red = ((plane + row + lane) & 1) == 0
    v, _ = smooth_whole(b4, g4, near_4, red, COARSE_SWEEPS)
    u4[...] = v

    lane = iota((128, 128), 0)
    wide = iota((128, 128), 1)
    spread = selector_of((lane < 32) & (((wide & 63) >> 1) == lane))
    value = split_matmul(u4[at_x], spread)
    twice_3[pl.ds(0, 8, stride=2), :] = value
    twice_3[pl.ds(1, 8, stride=2), :] = value
    value = v3[at_x] + twice_3[...]
    value = pltpu.roll(value, lax.rem(16 - 2 * at_y, 16), 0)
    value = pltpu.roll(value, lax.rem(128 - 16 * at_z, 128), 1)
    level_2 = []
    for part in range(2):
        fine = split_matmul(value, spread_selector(64 * part, 0, 16))[0:8]
        twice_2[pl.ds(0, 8, stride=2), :] = fine
        twice_2[pl.ds(1, 8, stride=2), :] = fine
        for index in range(2):
            own = u2_ref[2 * part + index]
            own = pltpu.roll(own, lax.rem(32 - 4 * at_y, 32), 0)
            own = pltpu.roll(own, lax.rem(128 - 32 * at_z, 128), 1)
            level_2.append(own[0:8] + twice_2[0:8])
    fine = split_matmul(jnp.concatenate(level_2, axis=0), spread_selector(0, 0, 32))
    twice_1[pl.ds(0, 32, stride=2), :] = fine
    twice_1[pl.ds(1, 32, stride=2), :] = fine
    for index in range(8):
        start = 16 * (index // 2)
        level_1[8 * index : 8 * index + 8] = u1_ref[index] + twice_1[start : start + 8]
    fine = split_matmul(level_1[...], spread_selector(0, 0, 64))
    twice_0[pl.ds(0, 64, stride=2), :] = fine
    twice_0[pl.ds(1, 64, stride=2), :] = fine
    for index in range(16):
        start = 16 * (index // 2)
        out_ref[index] = u0_ref[index] + twice_0[start : start + 16]


def call(kernel, outs, scratch, *operands):
    whole = pl.BlockSpec(memory_space=pltpu.VMEM)
    return pl.pallas_call(
        kernel,
        out_shape=[jax.ShapeDtypeStruct(shape, F32) for shape in outs],
        in_specs=[whole] * len(operands),
        out_specs=[whole] * len(outs),
        scratch_shapes=[pltpu.VMEM(shape, F32) for shape in scratch],
        compiler_params=pltpu.CompilerParams(vmem_limit_bytes=60000 * 1024),
    )(*operands)


def shift(value, axis, step):
    count = lax.axis_size(axis)
    pairs = [(i, i + step) for i in range(count) if 0 <= i + step < count]
    return lax.ppermute(value, axis, pairs)


def on_device(right_side, conductivity):
    f, b = right_side, conductivity
    upper = jnp.concatenate([f[BLOCK - F_HALO :], b[BLOCK - B_HALO :]], axis=0)
    lower = jnp.concatenate([f[:F_HALO], b[:B_HALO]], axis=0)
    low, high = shift(upper, "gx", 1), shift(lower, "gx", -1)

    strip = (GROUPS, BLOCK, 128)
    main, left, right = call(
        pack_kernel, [(PLANES, BLOCK, 128), strip, strip], [], f, b, low, high
    )
    beyond, before = shift(left, "gz", -1), shift(right, "gz", 1)
    own = jnp.concatenate([main, beyond, before], axis=0)
    low, high = shift(own, "gy", 1), shift(own, "gy", -1)

    large = (B_PLANES, ROWS, LANES)
    level_1 = (20, 24, 128)
    u0, u1, coarse = call(
        fine_kernel,
        [(BLOCK, BLOCK, 128), (8, 8, 128), (16, 128)],
        [large] * 5
        + [(ROWS, 128)] * 2
        + [(20, 24, LANES)] * 2
        + [level_1] * 5
        + [(24, 128), (4, 16, 128)],
        low, own, high,
    )

    low, high = shift(coarse, "gx", 1), shift(coarse, "gx", -1)
    slab = jnp.concatenate(
        [
            low[0:4], coarse[0:4], high[0:4],
            low[4:9], coarse[5:9], high[5:10],
            jnp.zeros((6, 128), F32),
        ],
        axis=0,
    )
    slab = lax.all_to_all(
        jnp.broadcast_to(slab[None], (32, 32, 128)), ("gy", "gz"), 0, 0, tiled=True
    )
    wide = (14, 32, 128)
    u2, coarse = call(
        slab_kernel,
        [(4, 32, 128), (32, 128)],
        [wide] * 5 + [(32, 128)],
        slab.reshape(1024, 128),
    )

    whole = lax.all_to_all(
        jnp.broadcast_to(coarse[None], (16, 32, 128)), "gx", 0, 0, tiled=True
    )
    (out,) = call(
        coarse_kernel,
        [(BLOCK, BLOCK, 128)],
        [
            (16, 16, 128), (16, 8, 128), (256, 128), (16, 128), (16, 128),
            (64, 128), (128, 128), (64, 128),
        ],
        whole, u0, u1, u2,
    )
    return out


def solution(mesh):
    spec = P("gx", "gy", "gz")
    return jax.shard_map(
        on_device, mesh=mesh, in_specs=(spec, spec), out_specs=spec, check_vma=False
    )
```

```python
import jax
import jax.numpy as jnp
from jax import lax
from jax.experimental import pallas as pl
from jax.experimental.pallas import tpu as pltpu
from jax.sharding import PartitionSpec as P

F_HALO = 12
B_HALO = 13
BLOCK = 16
F_PLANES = BLOCK + 2 * F_HALO
B_PLANES = BLOCK + 2 * B_HALO
PLANES = F_PLANES + B_PLANES
GROUPS = -(-PLANES // 8)
F_GROUPS = F_PLANES // 8
ROWS = 48
COARSE_SWEEPS = 8
F32 = jnp.float32


def iota(shape, dim):
    return lax.broadcasted_iota(jnp.int32, shape, dim)


def split_matmul(value, selector):
    high = value.astype(jnp.bfloat16)
    low = (value - high.astype(F32)).astype(jnp.bfloat16)
    return jnp.dot(high, selector, preferred_element_type=F32) + jnp.dot(
        low, selector, preferred_element_type=F32
    )


def selector_of(condition):
    return jnp.where(condition, 1.0, 0.0).astype(jnp.bfloat16)


def pair_selector(source_lanes, first, out_lanes, offset, count):
    source = iota((source_lanes, out_lanes), 0) - first
    target = iota((source_lanes, out_lanes), 1) - offset
    return selector_of(
        (source >= 0) & (source < 2 * count) & ((source >> 1) == target)
    )


def spread_selector(first, offset, count):
    source = iota((128, 128), 0) - first
    target = iota((128, 128), 1) - offset
    return selector_of((source >= 0) & (source < count) & ((target >> 1) == source))


class Level:
    names = ("b", "g", "fx", "fy", "fz", "d", "ir", "ik", "r", "k")

    def __init__(self, refs, columns, walled):
        self.walled = walled
        self.columns = columns
        for index, name in enumerate(self.names):
            setattr(self, name, refs[index * columns : (index + 1) * columns])
        self.lane = iota((8, 128), 1)
        self.parity = (iota((8, 128), 0) + self.lane) & 1

    @staticmethod
    def scratch(columns, planes, rows):
        return [(planes, rows + 16, 128)] * (len(Level.names) * columns)

    def at(self, refs, plane, row):
        return [ref[plane, row : row + 8] for ref in refs]

    def put(self, refs, plane, row, values):
        for ref, value in zip(refs, values):
            ref[plane, row : row + 8] = value

    def turn(self, values, step):
        rolled = [pltpu.roll(value, 127 if step > 0 else 1, 1) for value in values]
        if self.columns == 1:
            return rolled
        edge = self.lane == (127 if step > 0 else 0)
        first, second = rolled
        return [jnp.where(edge, second, first), jnp.where(edge, first, second)]

    def clear(self, planes, rows, ends):
        zero = jnp.zeros((8, 128), F32)
        for refs in (self.b, self.fy, self.r, self.k):
            for ref in refs:

                @pl.loop(0, planes)
                def _(plane):
                    ref[plane, 0:8] = zero
                    ref[plane, rows + 8 : rows + 16] = zero

        for refs in (self.r, self.k):
            for ref in refs:
                for plane in ends:
                    ref[plane] = jnp.zeros((rows + 16, 128), F32)

    def before(self, plane, rows):
        for row in range(8, rows + 8, 8):
            near = zip(self.at(self.b, plane, row), self.at(self.b, plane + 1, row))
            self.put(self.fx, plane, row, [own + other for own, other in near])

    def setup(self, plane, rows, red):
        for row in range(8, rows + 8, 8):
            b = self.at(self.b, plane, row)
            x_low, x_high = self.at(self.b, plane - 1, row), self.at(self.b, plane + 1, row)
            y_low, y_high = self.at(self.b, plane, row - 1), self.at(self.b, plane, row + 1)
            z_low, z_high = self.turn(b, -1), self.turn(b, 1)
            g = self.at(self.g, plane, row)
            for column in range(self.columns):
                own, z_before, z_after = b[column], z_low[column], z_high[column]
                face = own + z_after
                if self.walled:
                    z_before = jnp.where(self.lane > 0, z_before, 0.0)
                    z_after = jnp.where(self.lane < 127, z_after, 0.0)
                    face = jnp.where(self.lane < 127, face, 0.0)
                total = (6.0 * own + (x_low[column] + x_high[column])) + (
                    (y_low[column] + y_high[column]) + (z_before + z_after)
                )
                inside = own > 0.0
                inverse = 1.0 / jnp.where(inside, total, 1.0)
                first = self.parity == red
                reds = jnp.where(inside & first, inverse, 0.0)
                here = (plane, slice(row, row + 8))
                self.fx[column][here] = own + x_high[column]
                self.fy[column][here] = own + y_high[column]
                self.fz[column][here] = face
                self.d[column][here] = total
                self.ir[column][here] = reds
                self.ik[column][here] = jnp.where(inside & ~first, inverse, 0.0)
                self.r[column][here] = g[column] * reds
                self.k[column][here] = jnp.zeros((8, 128), F32)

    def total(self, source, plane, row):
        v = self.at(source, plane, row)
        face_z = self.at(self.fz, plane, row)
        z_high = self.turn(v, 1)
        z_low = self.turn([face * value for face, value in zip(face_z, v)], -1)
        out = []
        for column in range(self.columns):
            ref, fx, fy = source[column], self.fx[column], self.fy[column]
            here = slice(row, row + 8)
            along_x = (
                fx[plane, here] * ref[plane + 1, here]
                + fx[plane - 1, here] * ref[plane - 1, here]
            )
            low, high = slice(row - 1, row + 7), slice(row + 1, row + 9)
            along_y = fy[plane, here] * ref[plane, high] + fy[plane, low] * ref[plane, low]
            along_z = face_z[column] * z_high[column] + z_low[column]
            out.append((self.g[column][plane, here] + along_x) + (along_y + along_z))
        return out

    def relax(self, step, plane, rows):
        source, inverse, target = (
            (self.r, self.ik, self.k),
            (self.k, self.ir, self.r),
            (self.r, self.ik, self.k),
        )[step]
        results = []
        for row in rows:
            values = self.total(source, plane, row)
            scale = self.at(inverse, plane, row)
            values = [value * factor for value, factor in zip(values, scale)]
            if step == 2:
                values = [a + b for a, b in zip(values, self.at(self.r, plane, row))]
            results.append(values)
        for row, values in zip(rows, results):
            self.put(target, plane, row, values)

    def rest(self, plane, row):
        values = self.total(self.k, plane, row)
        out = []
        for column, value in enumerate(values):
            here = (plane, slice(row, row + 8))
            value = value - self.d[column][here] * self.k[column][here]
            out.append(jnp.where(self.b[column][here] > 0.0, value, 0.0))
        return out


def halves(ref, rows):
    return ref[pl.ds(0, rows, stride=2), :] + ref[pl.ds(1, rows, stride=2), :]


def pack_kernel(f_ref, b_ref, low_ref, high_ref, main_ref, left_ref, right_ref):
    lane = iota((BLOCK, 128), 1)

    def source(index):
        if index < F_HALO:
            return low_ref[index]
        if index < F_HALO + BLOCK:
            return f_ref[index - F_HALO]
        if index < F_PLANES:
            return high_ref[index - F_HALO - BLOCK]
        index -= F_PLANES
        if index < B_HALO:
            return low_ref[F_HALO + index]
        if index < B_HALO + BLOCK:
            return b_ref[index - B_HALO]
        return high_ref[F_HALO + index - B_HALO - BLOCK]

    for group in range(GROUPS):
        left = jnp.zeros((BLOCK, 128), F32)
        right = jnp.zeros((BLOCK, 128), F32)
        for slot in range(8):
            index = group * 8 + slot
            if index >= PLANES:
                break
            plane = source(index)
            main_ref[index] = plane
            turned = pltpu.roll(plane, 16 * slot, 1) if slot else plane
            left = jnp.where((lane >> 4) == slot, turned, left)
            right = jnp.where((lane >> 4) == ((slot - 1) & 7), turned, right)
        left_ref[group] = left
        right_ref[group] = right


def fine_kernel(low_ref, own_ref, high_ref, u0_ref, u1_ref, coarse_ref, *scratch):
    count = len(Level.names)
    fine = Level(scratch[: 2 * count], 2, False)
    middle = Level(scratch[2 * count : 3 * count], 1, False)
    rest_main, rest_side, sum_main, sum_side, collect = scratch[3 * count :]

    lane = iota((BLOCK, 128), 1)
    even = ((lane >> 4) & 1) == 0
    edges = (lane < 16) | (lane >= 112)

    def place(target, first, group, slots, scale):
        for part, source in enumerate((low_ref, own_ref, high_ref)):
            after, before = source[PLANES + group], source[PLANES + GROUPS + group]
            merged = (jnp.where(even, after, before), jnp.where(even, before, after))
            rows = slice(8 + BLOCK * part, 8 + BLOCK * part + BLOCK)
            for slot in slots:
                side = merged[slot & 1]
                if slot:
                    side = pltpu.roll(side, 128 - 16 * slot, 1)
                side = jnp.where(edges, side, 0.0)
                plane = source[group * 8 + slot]
                if scale != 1.0:
                    side, plane = side * scale, plane * scale
                target[0][first + slot, rows] = plane
                target[1][first + slot, rows] = side

    @pl.loop(0, F_GROUPS)
    def _(group):
        place(fine.g, group * 8 + 1, group, range(8), 2.0)

    @pl.loop(F_GROUPS, GROUPS - 1)
    def _(group):
        place(fine.b, group * 8 - F_PLANES, group, range(8), 1.0)

    group = GROUPS - 1
    place(fine.b, group * 8 - F_PLANES, group, range(PLANES - 8 * group), 1.0)

    fine.clear(B_PLANES, ROWS, (0, B_PLANES - 1))
    fine.before(0, ROWS)

    @pl.loop(1, B_PLANES - 1, step=2)
    def _(plane):
        fine.setup(plane, ROWS, 0)
        fine.setup(plane + 1, ROWS, 1)

    every = range(8, ROWS + 8, 8)
    inner = range(16, ROWS, 8)
    for step in range(3):
        beside = 2 - step
        near = B_HALO - beside

        @pl.loop(near, near + BLOCK + 2 * beside, step=2)
        def _(plane):
            fine.relax(step, plane, every)
            fine.relax(step, plane + 1, every)

        @pl.loop(near - 9, near)
        def _(plane):
            fine.relax(step, plane, inner)
            fine.relax(step, plane + BLOCK + 2 * beside + 9, inner)

    for plane in range(BLOCK):
        u0_ref[plane] = fine.k[0][plane + B_HALO, 8 + BLOCK : 8 + 2 * BLOCK]

    @pl.loop(0, 16)
    def _(index):
        for row in inner:
            first = fine.rest(2 * index + 5, row)
            second = fine.rest(2 * index + 6, row)
            at = pl.ds(pl.multiple_of(32 * index + (row - 16), 8), 8)
            rest_main[at, :] = first[0] + second[0]
            rest_side[at, :] = first[1] + second[1]

    @pl.loop(0, 18)
    def _(index):
        for row in every:
            at = pl.ds(pl.multiple_of(48 * index + (row - 8), 8), 8)
            first, second = 2 * index + 3, 2 * index + 4
            here = slice(row, row + 8)
            sum_main[at, :] = fine.b[0][first, here] + fine.b[0][second, here]
            sum_side[at, :] = fine.b[1][first, here] + fine.b[1][second, here]

    to_main = pair_selector(128, 0, 128, 0, 64)
    to_side = pair_selector(128, 0, 128, 64, 64)
    g_next = split_matmul(halves(rest_main, 256), to_main)
    g_next = 0.5 * (g_next + split_matmul(halves(rest_side, 256), to_side))
    b_next = split_matmul(halves(sum_main, 432), to_main)
    b_next = 0.125 * (b_next + split_matmul(halves(sum_side, 432), to_side))

    middle.clear(20, 24, (1, 18))
    zero = jnp.zeros((8, 128), F32)
    for plane in range(2, 18):
        middle.g[0][plane, 8:16] = zero
        middle.g[0][plane, 24:32] = zero
        middle.g[0][plane, 12:28] = g_next[16 * (plane - 2) : 16 * (plane - 1)]
    for plane in range(1, 19):
        middle.b[0][plane, 8:32] = b_next[24 * (plane - 1) : 24 * plane]
    middle.before(1, 24)

    @pl.loop(2, 18, step=4)
    def _(plane):
        for index in range(4):
            middle.setup(plane + index, 24, index & 1)

    for step in range(3):

        @pl.loop(2, 18, step=4)
        def _(plane):
            for index in range(4):
                middle.relax(step, plane + index, range(8, 32, 8))

    for plane in range(8):
        u1_ref[plane] = middle.k[0][plane + 6, 16:24]
    for index in range(4):
        (first,) = middle.rest(2 * index + 6, 16)
        (second,) = middle.rest(2 * index + 7, 16)
        collect[8 * index : 8 * index + 8] = 0.5 * (first + second)
    for index in range(6):
        first, second = middle.b[0][2 * index + 4, 16:24], middle.b[0][2 * index + 5, 16:24]
        collect[8 * index + 32 : 8 * index + 40] = 0.125 * (first + second)
    collect[80:128] = jnp.zeros((48, 128), F32)
    out = jnp.zeros((16, 128), F32)
    for part in range(4):
        rows = collect[pl.ds(2 * part, 16, stride=8), :]
        rows = rows + collect[pl.ds(2 * part + 1, 16, stride=8), :]
        out = out + split_matmul(rows, pair_selector(128, 0, 128, 32 * part, 32))
    coarse_ref[...] = out


def spread_kernel(low_ref, own_ref, high_ref, out_ref, rows):
    rows[0:4] = low_ref[0:4]
    rows[4:8] = own_ref[0:4]
    rows[8:12] = high_ref[0:4]
    rows[12:17] = low_ref[4:9]
    rows[17:21] = own_ref[5:9]
    rows[21:26] = high_ref[5:10]
    rows[26:32] = jnp.zeros((6, 128), F32)
    value = rows[...]
    for index in range(32):
        out_ref[index] = value


def slab_kernel(gathered_ref, u2_ref, coarse_ref, *scratch):
    slab = Level(scratch[: len(Level.names)], 1, True)
    rest, sums = scratch[len(Level.names) :]
    row = iota((4, 8, 128), 1)
    lane = iota((4, 8, 128), 2)
    group = lane >> 5
    turn = (group - row) & 3

    def exchange(value):
        value = value.reshape(4, 8, 128)
        out = value
        for d in (1, 2, 3):
            moved = pltpu.roll(value, 32 * d, 2)
            near = pltpu.roll(moved, 8 - d, 1)
            far = pltpu.roll(moved, 4 - d, 1)
            out = jnp.where(turn == d, jnp.where(group >= d, near, far), out)
        return out.reshape(32, 128)

    for plane in range(12):
        slab.g[0][plane + 1, 8:40] = exchange(gathered_ref[pl.ds(plane, 32, stride=32), :])
    for plane in range(14):
        slab.b[0][plane, 8:40] = exchange(gathered_ref[pl.ds(plane + 12, 32, stride=32), :])

    slab.clear(14, 32, (0, 13))
    slab.before(0, 32)

    @pl.loop(1, 13, step=4)
    def _(plane):
        for index in range(4):
            slab.setup(plane + index, 32, index & 1)

    for step in range(3):

        @pl.loop(2 + step, 12 - step, step=2)
        def _(plane):
            for index in range(2):
                slab.relax(step, plane + index, range(8, 40, 8))

    for plane in range(4):
        u2_ref[plane] = slab.k[0][plane + 5, 8:40]
    for part in range(2):
        for row in range(8, 40, 8):
            (first,) = slab.rest(5 + 2 * part, row)
            (second,) = slab.rest(6 + 2 * part, row)
            at = slice(32 * part + row - 8, 32 * part + row)
            rest[at] = 0.5 * (first + second)
            here = slice(row, row + 8)
            sums[at] = 0.125 * (slab.b[0][5 + 2 * part, here] + slab.b[0][6 + 2 * part, here])
    g_rows, b_rows = halves(rest, 32), halves(sums, 32)
    value = jnp.zeros((32, 128), F32)
    for part in range(2):
        own = slice(16 * part, 16 * part + 16)
        rows = jnp.concatenate([g_rows[own], b_rows[own]], axis=0)
        value = value + split_matmul(rows, pair_selector(128, 0, 128, 64 * part, 64))
    for index in range(16):
        coarse_ref[index] = value


def coarse_kernel(
    gathered_ref, u0_ref, u1_ref, u2_ref, out_ref,
    r3, rs, k3, ks, inner_3, outer_3, fy3, fz3, d3, ir3, ik3, b3, bs,
    r4, k4, fx4, fy4, fz4, ir4, ik4, g4, b4,
    pair_3, pair_4, twice_3, twice_2, twice_1, twice_0, level_1,
):
    at_x = lax.axis_index("gx")
    at_y = lax.axis_index("gy")
    at_z = lax.axis_index("gz")
    lane = iota((8, 128), 1)
    row8 = iota((8, 128), 0)
    zero = jnp.zeros((8, 128), F32)

    cell = lane & 63
    parity = ((lane >> 6) + row8 + cell) & 1
    first_half = lane < 64
    for ref in (r3, rs, k3, ks, b3, bs):
        for plane in (0, 17):
            ref[plane] = jnp.zeros((32, 128), F32)
    for plane in range(1, 17):
        for ref in (r3, k3, b3, fy3):
            ref[plane, 0:8] = zero
            ref[plane, 24:32] = zero
        for row in (8, 16):
            value = gathered_ref[plane - 1, row + 8 : row + 16]
            b3[plane, row : row + 8] = value
            bs[plane, row : row + 8] = pltpu.roll(value, 64, 1)

    def outer(ref, plane, here):
        return jnp.where(first_half, ref[plane - 1, here], ref[plane + 1, here])

    for plane in range(1, 17):
        for row in (8, 16):
            here = slice(row, row + 8)
            b = b3[plane, here]
            partner, other = bs[plane, here], outer(bs, plane, here)
            y_high = b3[plane, row + 1 : row + 9]
            z_low = jnp.where(cell > 0, pltpu.roll(b, 1, 1), 0.0)
            z_high = jnp.where(cell < 63, pltpu.roll(b, 127, 1), 0.0)
            total = (6.0 * b + (partner + other)) + (
                (b3[plane, row - 1 : row + 7] + y_high) + (z_low + z_high)
            )
            inside = b > 0.0
            inverse = 1.0 / jnp.where(inside, total, 1.0)
            reds = jnp.where(inside & (parity == 0), inverse, 0.0)
            inner_3[plane, here] = b + partner
            outer_3[plane, here] = b + other
            fy3[plane, here] = b + y_high
            fz3[plane, here] = jnp.where(cell < 63, b + z_high, 0.0)
            d3[plane, here] = total
            ir3[plane, here] = reds
            ik3[plane, here] = jnp.where(inside & (parity == 1), inverse, 0.0)
            value = gathered_ref[plane - 1, row - 8 : row] * reds
            r3[plane, here] = value
            rs[plane, here] = pltpu.roll(value, 64, 1)

    def total_3(ref, swapped, plane, row):
        here, low, high = slice(row, row + 8), slice(row - 1, row + 7), slice(row + 1, row + 9)
        v, face = ref[plane, here], fz3[plane, here]
        along_x = inner_3[plane, here] * swapped[plane, here]
        along_x = along_x + outer_3[plane, here] * outer(swapped, plane, here)
        along_y = fy3[plane, here] * ref[plane, high] + fy3[plane, low] * ref[plane, low]
        along_z = face * pltpu.roll(v, 127, 1) + pltpu.roll(face * v, 1, 1)
        return (gathered_ref[plane - 1, row - 8 : row] + along_x) + (along_y + along_z)

    for step in range(3):
        source, inverse, target = (
            ((r3, rs), ik3, (k3, ks)),
            ((k3, ks), ir3, (r3, rs)),
            ((r3, rs), ik3, (k3, ks)),
        )[step]
        for plane in range(1, 17):
            for row in (8, 16):
                here = slice(row, row + 8)
                value = total_3(*source, plane, row) * inverse[plane, here]
                if step == 2:
                    value = value + r3[plane, here]
                target[0][plane, here] = value
                target[1][plane, here] = pltpu.roll(value, 64, 1)

    for plane in range(1, 17):
        for row in (8, 16):
            here = slice(row, row + 8)
            value = total_3(k3, ks, plane, row) - d3[plane, here] * k3[plane, here]
            at = slice(16 * (plane - 1) + row - 8, 16 * (plane - 1) + row)
            pair_3[at] = value + pltpu.roll(value, 64, 1)
            pair_4[at] = b3[plane, here] + bs[plane, here]
    halve = pair_selector(128, 0, 128, 0, 32)
    g4[...] = 0.5 * split_matmul(halves(pair_3, 128), halve).reshape(16, 8, 128)
    b4[0] = zero
    b4[17] = zero
    b4[1:17] = 0.125 * split_matmul(halves(pair_4, 128), halve).reshape(16, 8, 128)

    parity = (row8 + lane) & 1
    for ref in (r4, k4):
        ref[0] = zero
        ref[17] = zero
    fx4[0] = b4[1]
    for plane in range(1, 17):
        b = b4[plane]
        x_high = b4[plane + 1]
        y_low = jnp.where(row8 > 0, pltpu.roll(b, 1, 0), 0.0)
        y_high = jnp.where(row8 < 7, pltpu.roll(b, 7, 0), 0.0)
        z_high = pltpu.roll(b, 127, 1)
        total = (6.0 * b + (b4[plane - 1] + x_high)) + (
            (y_low + y_high) + (pltpu.roll(b, 1, 1) + z_high)
        )
        inside = b > 0.0
        inverse = 1.0 / jnp.where(inside, total, 1.0)
        reds = jnp.where(inside & (parity == (plane - 1) & 1), inverse, 0.0)
        fx4[plane] = b + x_high
        fy4[plane] = jnp.where(row8 < 7, b + y_high, 0.0)
        fz4[plane] = jnp.where(lane < 31, b + z_high, 0.0)
        ir4[plane] = reds
        ik4[plane] = jnp.where(inside & (parity != (plane - 1) & 1), inverse, 0.0)
        r4[plane] = g4[plane - 1] * reds

    def half_4(source, inverse, target):
        for plane in range(1, 17):
            v = source[plane]
            face_y, face_z = fy4[plane], fz4[plane]
            along_x = fx4[plane] * source[plane + 1] + fx4[plane - 1] * source[plane - 1]
            along_y = face_y * pltpu.roll(v, 7, 0) + pltpu.roll(face_y * v, 1, 0)
            along_z = face_z * pltpu.roll(v, 127, 1) + pltpu.roll(face_z * v, 1, 1)
            value = (g4[plane - 1] + along_x) + (along_y + along_z)
            target[plane] = value * inverse[plane]

    half_4(r4, ik4, k4)

    @pl.loop(1, COARSE_SWEEPS)
    def _(sweep):
        half_4(k4, ir4, r4)
        half_4(r4, ik4, k4)

    source = iota((128, 128), 0)
    target = iota((128, 128), 1)
    spread = selector_of((source < 32) & (((target & 63) >> 1) == source))
    value = split_matmul(r4[at_x + 1] + k4[at_x + 1], spread)
    twice_3[pl.ds(0, 8, stride=2), :] = value
    twice_3[pl.ds(1, 8, stride=2), :] = value
    value = k3[at_x + 1, 8:24] + twice_3[...]
    value = pltpu.roll(value, lax.rem(16 - 2 * at_y, 16), 0)
    value = pltpu.roll(value, lax.rem(128 - 16 * at_z, 128), 1)
    level_2 = []
    for part in range(2):
        fine = split_matmul(value, spread_selector(64 * part, 0, 16))[0:8]
        twice_2[pl.ds(0, 8, stride=2), :] = fine
        twice_2[pl.ds(1, 8, stride=2), :] = fine
        for index in range(2):
            own = u2_ref[2 * part + index]
            own = pltpu.roll(own, lax.rem(32 - 4 * at_y, 32), 0)
            own = pltpu.roll(own, lax.rem(128 - 32 * at_z, 128), 1)
            level_2.append(own[0:8] + twice_2[0:8])
    fine = split_matmul(jnp.concatenate(level_2, axis=0), spread_selector(0, 0, 32))
    twice_1[pl.ds(0, 32, stride=2), :] = fine
    twice_1[pl.ds(1, 32, stride=2), :] = fine
    for index in range(8):
        start = 16 * (index // 2)
        level_1[8 * index : 8 * index + 8] = u1_ref[index] + twice_1[start : start + 8]
    fine = split_matmul(level_1[...], spread_selector(0, 0, 64))
    twice_0[pl.ds(0, 64, stride=2), :] = fine
    twice_0[pl.ds(1, 64, stride=2), :] = fine
    for index in range(16):
        start = 16 * (index // 2)
        out_ref[index] = u0_ref[index] + twice_0[start : start + 16]


def call(kernel, outs, scratch, *operands):
    whole = pl.BlockSpec(memory_space=pltpu.VMEM)
    return pl.pallas_call(
        kernel,
        out_shape=[jax.ShapeDtypeStruct(shape, F32) for shape in outs],
        in_specs=[whole] * len(operands),
        out_specs=[whole] * len(outs),
        scratch_shapes=[pltpu.VMEM(shape, F32) for shape in scratch],
        compiler_params=pltpu.CompilerParams(vmem_limit_bytes=60000 * 1024),
    )(*operands)


def shift(value, axis, step):
    count = lax.axis_size(axis)
    pairs = [(i, i + step) for i in range(count) if 0 <= i + step < count]
    return lax.ppermute(value, axis, pairs)


def on_device(right_side, conductivity):
    f, b = right_side, conductivity
    upper = jnp.concatenate([f[BLOCK - F_HALO :], b[BLOCK - B_HALO :]], axis=0)
    lower = jnp.concatenate([f[:F_HALO], b[:B_HALO]], axis=0)
    low, high = shift(upper, "gx", 1), shift(lower, "gx", -1)

    strip = (GROUPS, BLOCK, 128)
    main, left, right = call(
        pack_kernel, [(PLANES, BLOCK, 128), strip, strip], [], f, b, low, high
    )
    beyond, before = shift(left, "gz", -1), shift(right, "gz", 1)
    own = jnp.concatenate([main, beyond, before], axis=0)
    low, high = shift(own, "gy", 1), shift(own, "gy", -1)

    u0, u1, coarse = call(
        fine_kernel,
        [(BLOCK, BLOCK, 128), (8, 8, 128), (16, 128)],
        Level.scratch(2, B_PLANES, ROWS)
        + Level.scratch(1, 20, 24)
        + [(512, 128)] * 2
        + [(864, 128)] * 2
        + [(128, 128)],
        low, own, high,
    )

    low, high = shift(coarse, "gx", 1), shift(coarse, "gx", -1)
    (slab,) = call(spread_kernel, [(32, 32, 128)], [(32, 128)], low, coarse, high)
    slab = lax.all_to_all(slab, ("gy", "gz"), 0, 0, tiled=True)
    u2, coarse = call(
        slab_kernel,
        [(4, 32, 128), (16, 32, 128)],
        Level.scratch(1, 14, 32) + [(64, 128)] * 2,
        slab.reshape(1024, 128),
    )

    whole = lax.all_to_all(coarse, "gx", 0, 0, tiled=True)
    (out,) = call(
        coarse_kernel,
        [(BLOCK, BLOCK, 128)],
        [(18, 32, 128)] * 13
        + [(18, 8, 128)] * 7
        + [(16, 8, 128), (18, 8, 128)]
        + [(256, 128)] * 2
        + [(16, 128), (16, 128), (64, 128), (128, 128), (64, 128)],
        whole, u0, u1, u2,
    )
    return out


def solution(mesh):
    spec = P("gx", "gy", "gz")
    return jax.shard_map(
        on_device, mesh=mesh, in_specs=(spec, spec), out_specs=spec, check_vma=False
    )
```

```python
import jax
import jax.numpy as jnp
from jax import lax
from jax.experimental import pallas as pl
from jax.experimental.pallas import tpu as pltpu
from jax.sharding import PartitionSpec as P

F_HALO = 12
B_HALO = 13
BLOCK = 16
F_PLANES = BLOCK + 2 * F_HALO
B_PLANES = BLOCK + 2 * B_HALO
PLANES = F_PLANES + B_PLANES
GROUPS = -(-PLANES // 8)
F_GROUPS = F_PLANES // 8
ROWS = 48
COARSE_SWEEPS = 8
F32 = jnp.float32


def iota(shape, dim):
    return lax.broadcasted_iota(jnp.int32, shape, dim)


def split_matmul(value, selector):
    high = value.astype(jnp.bfloat16)
    low = (value - high.astype(F32)).astype(jnp.bfloat16)
    return jnp.dot(high, selector, preferred_element_type=F32) + jnp.dot(
        low, selector, preferred_element_type=F32
    )


def selector_of(condition):
    return jnp.where(condition, 1.0, 0.0).astype(jnp.bfloat16)


def pair_selector(source_lanes, first, out_lanes, offset, count):
    source = iota((source_lanes, out_lanes), 0) - first
    target = iota((source_lanes, out_lanes), 1) - offset
    return selector_of(
        (source >= 0) & (source < 2 * count) & ((source >> 1) == target)
    )


def spread_selector(first, offset, count):
    source = iota((128, 128), 0) - first
    target = iota((128, 128), 1) - offset
    return selector_of((source >= 0) & (source < count) & ((target >> 1) == source))


class Level:
    names = ("b", "g", "fx", "fy", "fz", "d", "ir", "ik", "r", "k")

    def __init__(self, refs, columns, walled):
        self.walled = walled
        self.columns = columns
        for index, name in enumerate(self.names):
            setattr(self, name, refs[index * columns : (index + 1) * columns])
        self.lane = iota((8, 128), 1)
        self.parity = (iota((8, 128), 0) + self.lane) & 1

    @staticmethod
    def scratch(columns, planes, rows):
        return [(planes, rows + 16, 128)] * (len(Level.names) * columns)

    def at(self, refs, plane, row):
        return [ref[plane, row : row + 8] for ref in refs]

    def put(self, refs, plane, row, values):
        for ref, value in zip(refs, values):
            ref[plane, row : row + 8] = value

    def turn(self, values, step):
        rolled = [pltpu.roll(value, 127 if step > 0 else 1, 1) for value in values]
        if self.columns == 1:
            return rolled
        edge = self.lane == (127 if step > 0 else 0)
        first, second = rolled
        return [jnp.where(edge, second, first), jnp.where(edge, first, second)]

    def clear(self, planes, rows, ends):
        zero = jnp.zeros((8, 128), F32)
        for refs in (self.b, self.fy, self.r, self.k):
            for ref in refs:

                @pl.loop(0, planes)
                def _(plane):
                    ref[plane, 0:8] = zero
                    ref[plane, rows + 8 : rows + 16] = zero

        for refs in (self.r, self.k):
            for ref in refs:
                for plane in ends:
                    ref[plane] = jnp.zeros((rows + 16, 128), F32)

    def before(self, plane, rows):
        for row in range(8, rows + 8, 8):
            near = zip(self.at(self.b, plane, row), self.at(self.b, plane + 1, row))
            self.put(self.fx, plane, row, [own + other for own, other in near])

    def setup(self, plane, rows, red):
        for row in range(8, rows + 8, 8):
            b = self.at(self.b, plane, row)
            x_low, x_high = self.at(self.b, plane - 1, row), self.at(self.b, plane + 1, row)
            y_low, y_high = self.at(self.b, plane, row - 1), self.at(self.b, plane, row + 1)
            z_low, z_high = self.turn(b, -1), self.turn(b, 1)
            g = self.at(self.g, plane, row)
            for column in range(self.columns):
                own, z_before, z_after = b[column], z_low[column], z_high[column]
                face = own + z_after
                if self.walled:
                    z_before = jnp.where(self.lane > 0, z_before, 0.0)
                    z_after = jnp.where(self.lane < 127, z_after, 0.0)
                    face = jnp.where(self.lane < 127, face, 0.0)
                total = (6.0 * own + (x_low[column] + x_high[column])) + (
                    (y_low[column] + y_high[column]) + (z_before + z_after)
                )
                inside = own > 0.0
                inverse = 1.0 / jnp.where(inside, total, 1.0)
                first = self.parity == red
                reds = jnp.where(inside & first, inverse, 0.0)
                here = (plane, slice(row, row + 8))
                self.fx[column][here] = own + x_high[column]
                self.fy[column][here] = own + y_high[column]
                self.fz[column][here] = face
                self.d[column][here] = total
                self.ir[column][here] = reds
                self.ik[column][here] = jnp.where(inside & ~first, inverse, 0.0)
                self.r[column][here] = g[column] * reds
                self.k[column][here] = jnp.zeros((8, 128), F32)

    def total(self, source, plane, row):
        v = self.at(source, plane, row)
        face_z = self.at(self.fz, plane, row)
        z_high = self.turn(v, 1)
        z_low = self.turn([face * value for face, value in zip(face_z, v)], -1)
        out = []
        for column in range(self.columns):
            ref, fx, fy = source[column], self.fx[column], self.fy[column]
            here = slice(row, row + 8)
            along_x = (
                fx[plane, here] * ref[plane + 1, here]
                + fx[plane - 1, here] * ref[plane - 1, here]
            )
            low, high = slice(row - 1, row + 7), slice(row + 1, row + 9)
            along_y = fy[plane, here] * ref[plane, high] + fy[plane, low] * ref[plane, low]
            along_z = face_z[column] * z_high[column] + z_low[column]
            out.append((self.g[column][plane, here] + along_x) + (along_y + along_z))
        return out

    def relax(self, step, plane, rows):
        source, inverse, target = (
            (self.r, self.ik, self.k),
            (self.k, self.ir, self.r),
            (self.r, self.ik, self.k),
        )[step]
        results = []
        for row in rows:
            values = self.total(source, plane, row)
            scale = self.at(inverse, plane, row)
            values = [value * factor for value, factor in zip(values, scale)]
            if step == 2:
                values = [a + b for a, b in zip(values, self.at(self.r, plane, row))]
            results.append(values)
        for row, values in zip(rows, results):
            self.put(target, plane, row, values)

    def rest(self, plane, row):
        values = self.total(self.k, plane, row)
        out = []
        for column, value in enumerate(values):
            here = (plane, slice(row, row + 8))
            value = value - self.d[column][here] * self.k[column][here]
            out.append(jnp.where(self.b[column][here] > 0.0, value, 0.0))
        return out


def halves(ref, rows):
    return ref[pl.ds(0, rows, stride=2), :] + ref[pl.ds(1, rows, stride=2), :]


def pack_kernel(f_ref, b_ref, low_ref, high_ref, main_ref, left_ref, right_ref):
    lane = iota((BLOCK, 128), 1)

    def source(index):
        if index < F_HALO:
            return low_ref[index]
        if index < F_HALO + BLOCK:
            return f_ref[index - F_HALO]
        if index < F_PLANES:
            return high_ref[index - F_HALO - BLOCK]
        index -= F_PLANES
        if index < B_HALO:
            return low_ref[F_HALO + index]
        if index < B_HALO + BLOCK:
            return b_ref[index - B_HALO]
        return high_ref[F_HALO + index - B_HALO - BLOCK]

    for group in range(GROUPS):
        left = jnp.zeros((BLOCK, 128), F32)
        right = jnp.zeros((BLOCK, 128), F32)
        for slot in range(8):
            index = group * 8 + slot
            if index >= PLANES:
                break
            plane = source(index)
            main_ref[index] = plane
            turned = pltpu.roll(plane, 16 * slot, 1) if slot else plane
            left = jnp.where((lane >> 4) == slot, turned, left)
            right = jnp.where((lane >> 4) == ((slot - 1) & 7), turned, right)
        left_ref[group] = left
        right_ref[group] = right


def fine_kernel(low_ref, own_ref, high_ref, u0_ref, u1_ref, coarse_ref, *scratch):
    count = len(Level.names)
    fine = Level(scratch[: 2 * count], 2, False)
    middle = Level(scratch[2 * count : 3 * count], 1, False)
    rest_main, rest_side, sum_main, sum_side, collect = scratch[3 * count :]

    lane = iota((BLOCK, 128), 1)
    even = ((lane >> 4) & 1) == 0
    edges = (lane < 16) | (lane >= 112)

    def place(target, first, group, slots, scale):
        for part, source in enumerate((low_ref, own_ref, high_ref)):
            after, before = source[PLANES + group], source[PLANES + GROUPS + group]
            merged = (jnp.where(even, after, before), jnp.where(even, before, after))
            rows = slice(8 + BLOCK * part, 8 + BLOCK * part + BLOCK)
            for slot in slots:
                side = merged[slot & 1]
                if slot:
                    side = pltpu.roll(side, 128 - 16 * slot, 1)
                side = jnp.where(edges, side, 0.0)
                plane = source[group * 8 + slot]
                if scale != 1.0:
                    side, plane = side * scale, plane * scale
                target[0][first + slot, rows] = plane
                target[1][first + slot, rows] = side

    @pl.loop(0, F_GROUPS)
    def _(group):
        place(fine.g, group * 8 + 1, group, range(8), 2.0)

    @pl.loop(F_GROUPS, GROUPS - 1)
    def _(group):
        place(fine.b, group * 8 - F_PLANES, group, range(8), 1.0)

    group = GROUPS - 1
    place(fine.b, group * 8 - F_PLANES, group, range(PLANES - 8 * group), 1.0)

    fine.clear(B_PLANES, ROWS, (0, B_PLANES - 1))
    fine.before(0, ROWS)

    @pl.loop(1, B_PLANES - 1, step=2)
    def _(plane):
        fine.setup(plane, ROWS, 0)
        fine.setup(plane + 1, ROWS, 1)

    every = range(8, ROWS + 8, 8)
    inner = range(16, ROWS, 8)
    for step in range(3):
        beside = 2 - step
        near = B_HALO - beside

        @pl.loop(near, near + BLOCK + 2 * beside, step=2)
        def _(plane):
            fine.relax(step, plane, every)
            fine.relax(step, plane + 1, every)

        @pl.loop(near - 9, near)
        def _(plane):
            fine.relax(step, plane, inner)
            fine.relax(step, plane + BLOCK + 2 * beside + 9, inner)

    for plane in range(BLOCK):
        u0_ref[plane] = fine.k[0][plane + B_HALO, 8 + BLOCK : 8 + 2 * BLOCK]

    @pl.loop(0, 16)
    def _(index):
        for row in inner:
            first = fine.rest(2 * index + 5, row)
            second = fine.rest(2 * index + 6, row)
            at = pl.ds(pl.multiple_of(32 * index + (row - 16), 8), 8)
            rest_main[at, :] = first[0] + second[0]
            rest_side[at, :] = first[1] + second[1]

    @pl.loop(0, 18)
    def _(index):
        for row in every:
            at = pl.ds(pl.multiple_of(48 * index + (row - 8), 8), 8)
            first, second = 2 * index + 3, 2 * index + 4
            here = slice(row, row + 8)
            sum_main[at, :] = fine.b[0][first, here] + fine.b[0][second, here]
            sum_side[at, :] = fine.b[1][first, here] + fine.b[1][second, here]

    to_main = pair_selector(128, 0, 128, 0, 64)
    to_side = pair_selector(128, 0, 128, 64, 64)
    g_next = split_matmul(halves(rest_main, 256), to_main)
    g_next = 0.5 * (g_next + split_matmul(halves(rest_side, 256), to_side))
    b_next = split_matmul(halves(sum_main, 432), to_main)
    b_next = 0.125 * (b_next + split_matmul(halves(sum_side, 432), to_side))

    middle.clear(20, 24, (1, 18))
    zero = jnp.zeros((8, 128), F32)
    for plane in range(2, 18):
        middle.g[0][plane, 8:16] = zero
        middle.g[0][plane, 24:32] = zero
        middle.g[0][plane, 12:28] = g_next[16 * (plane - 2) : 16 * (plane - 1)]
    for plane in range(1, 19):
        middle.b[0][plane, 8:32] = b_next[24 * (plane - 1) : 24 * plane]
    middle.before(1, 24)

    @pl.loop(2, 18, step=4)
    def _(plane):
        for index in range(4):
            middle.setup(plane + index, 24, index & 1)

    for step in range(3):

        @pl.loop(2, 18, step=4)
        def _(plane):
            for index in range(4):
                middle.relax(step, plane + index, range(8, 32, 8))

    for plane in range(8):
        u1_ref[plane] = middle.k[0][plane + 6, 16:24]
    for index in range(4):
        (first,) = middle.rest(2 * index + 6, 16)
        (second,) = middle.rest(2 * index + 7, 16)
        collect[8 * index : 8 * index + 8] = 0.5 * (first + second)
    for index in range(6):
        first, second = middle.b[0][2 * index + 4, 16:24], middle.b[0][2 * index + 5, 16:24]
        collect[8 * index + 32 : 8 * index + 40] = 0.125 * (first + second)
    collect[80:128] = jnp.zeros((48, 128), F32)
    out = jnp.zeros((16, 128), F32)
    for part in range(4):
        rows = collect[pl.ds(2 * part, 16, stride=8), :]
        rows = rows + collect[pl.ds(2 * part + 1, 16, stride=8), :]
        out = out + split_matmul(rows, pair_selector(128, 0, 128, 32 * part, 32))
    coarse_ref[...] = out


def spread_kernel(low_ref, own_ref, high_ref, out_ref, rows):
    rows[0:4] = low_ref[0:4]
    rows[4:8] = own_ref[0:4]
    rows[8:12] = high_ref[0:4]
    rows[12:17] = low_ref[4:9]
    rows[17:21] = own_ref[5:9]
    rows[21:26] = high_ref[5:10]
    rows[26:32] = jnp.zeros((6, 128), F32)
    value = rows[...]
    for index in range(32):
        out_ref[index] = value


def slab_kernel(gathered_ref, u2_ref, coarse_ref, *scratch):
    slab = Level(scratch[: len(Level.names)], 1, True)
    rest, sums = scratch[len(Level.names) :]
    row = iota((4, 8, 128), 1)
    lane = iota((4, 8, 128), 2)
    group = lane >> 5
    turn = (group - row) & 3

    def exchange(value):
        value = value.reshape(4, 8, 128)
        out = value
        for d in (1, 2, 3):
            moved = pltpu.roll(value, 32 * d, 2)
            near = pltpu.roll(moved, 8 - d, 1)
            far = pltpu.roll(moved, 4 - d, 1)
            out = jnp.where(turn == d, jnp.where(group >= d, near, far), out)
        return out.reshape(32, 128)

    for plane in range(12):
        slab.g[0][plane + 1, 8:40] = exchange(gathered_ref[pl.ds(plane, 32, stride=32), :])
    for plane in range(14):
        slab.b[0][plane, 8:40] = exchange(gathered_ref[pl.ds(plane + 12, 32, stride=32), :])

    slab.clear(14, 32, (0, 13))
    slab.before(0, 32)

    @pl.loop(1, 13, step=4)
    def _(plane):
        for index in range(4):
            slab.setup(plane + index, 32, index & 1)

    for step in range(3):

        @pl.loop(2 + step, 12 - step, step=2)
        def _(plane):
            for index in range(2):
                slab.relax(step, plane + index, range(8, 40, 8))

    for plane in range(4):
        u2_ref[plane] = slab.k[0][plane + 5, 8:40]
    for part in range(2):
        for row in range(8, 40, 8):
            (first,) = slab.rest(5 + 2 * part, row)
            (second,) = slab.rest(6 + 2 * part, row)
            at = slice(32 * part + row - 8, 32 * part + row)
            rest[at] = 0.5 * (first + second)
            here = slice(row, row + 8)
            sums[at] = 0.125 * (slab.b[0][5 + 2 * part, here] + slab.b[0][6 + 2 * part, here])
    g_rows, b_rows = halves(rest, 32), halves(sums, 32)
    value = jnp.zeros((32, 128), F32)
    for part in range(2):
        own = slice(16 * part, 16 * part + 16)
        rows = jnp.concatenate([g_rows[own], b_rows[own]], axis=0)
        value = value + split_matmul(rows, pair_selector(128, 0, 128, 64 * part, 64))
    for index in range(16):
        coarse_ref[index] = value


def coarse_kernel(
    gathered_ref, u0_ref, u1_ref, u2_ref, out_ref,
    r3, rs, k3, ks, inner_3, outer_3, fy3, fz3, d3, ir3, ik3, b3, bs,
    r4, k4, fx4, fy4, fz4, ir4, ik4, g4, b4,
    pair_3, pair_4, twice_3, twice_2, twice_1, twice_0, level_1,
):
    at_x = lax.axis_index("gx")
    at_y = lax.axis_index("gy")
    at_z = lax.axis_index("gz")
    lane = iota((8, 128), 1)
    row8 = iota((8, 128), 0)
    zero = jnp.zeros((8, 128), F32)

    cell = lane & 63
    parity = ((lane >> 6) + row8 + cell) & 1
    first_half = lane < 64
    for ref in (r3, rs, k3, ks, b3, bs):
        for plane in (0, 17):
            ref[plane] = jnp.zeros((32, 128), F32)
    for plane in range(1, 17):
        for ref in (r3, k3, b3, fy3):
            ref[plane, 0:8] = zero
            ref[plane, 24:32] = zero
        for row in (8, 16):
            value = gathered_ref[plane - 1, row + 8 : row + 16]
            b3[plane, row : row + 8] = value
            bs[plane, row : row + 8] = pltpu.roll(value, 64, 1)

    def outer(ref, plane, here):
        return jnp.where(first_half, ref[plane - 1, here], ref[plane + 1, here])

    for plane in range(1, 17):
        for row in (8, 16):
            here = slice(row, row + 8)
            b = b3[plane, here]
            partner, other = bs[plane, here], outer(bs, plane, here)
            y_high = b3[plane, row + 1 : row + 9]
            z_low = jnp.where(cell > 0, pltpu.roll(b, 1, 1), 0.0)
            z_high = jnp.where(cell < 63, pltpu.roll(b, 127, 1), 0.0)
            total = (6.0 * b + (partner + other)) + (
                (b3[plane, row - 1 : row + 7] + y_high) + (z_low + z_high)
            )
            inside = b > 0.0
            inverse = 1.0 / jnp.where(inside, total, 1.0)
            reds = jnp.where(inside & (parity == 0), inverse, 0.0)
            inner_3[plane, here] = b + partner
            outer_3[plane, here] = b + other
            fy3[plane, here] = b + y_high
            fz3[plane, here] = jnp.where(cell < 63, b + z_high, 0.0)
            d3[plane, here] = total
            ir3[plane, here] = reds
            ik3[plane, here] = jnp.where(inside & (parity == 1), inverse, 0.0)
            value = gathered_ref[plane - 1, row - 8 : row] * reds
            r3[plane, here] = value
            rs[plane, here] = pltpu.roll(value, 64, 1)

    def total_3(ref, swapped, plane, row):
        here, low, high = slice(row, row + 8), slice(row - 1, row + 7), slice(row + 1, row + 9)
        v, face = ref[plane, here], fz3[plane, here]
        along_x = inner_3[plane, here] * swapped[plane, here]
        along_x = along_x + outer_3[plane, here] * outer(swapped, plane, here)
        along_y = fy3[plane, here] * ref[plane, high] + fy3[plane, low] * ref[plane, low]
        along_z = face * pltpu.roll(v, 127, 1) + pltpu.roll(face * v, 1, 1)
        return (gathered_ref[plane - 1, row - 8 : row] + along_x) + (along_y + along_z)

    for step in range(3):
        source, inverse, target = (
            ((r3, rs), ik3, (k3, ks)),
            ((k3, ks), ir3, (r3, rs)),
            ((r3, rs), ik3, (k3, ks)),
        )[step]
        for plane in range(1, 17):
            for row in (8, 16):
                here = slice(row, row + 8)
                value = total_3(*source, plane, row) * inverse[plane, here]
                if step == 2:
                    value = value + r3[plane, here]
                target[0][plane, here] = value
                target[1][plane, here] = pltpu.roll(value, 64, 1)

    for plane in range(1, 17):
        for row in (8, 16):
            here = slice(row, row + 8)
            value = total_3(k3, ks, plane, row) - d3[plane, here] * k3[plane, here]
            at = slice(16 * (plane - 1) + row - 8, 16 * (plane - 1) + row)
            pair_3[at] = value + pltpu.roll(value, 64, 1)
            pair_4[at] = b3[plane, here] + bs[plane, here]
    halve = pair_selector(128, 0, 128, 0, 32)
    g4[...] = 0.5 * split_matmul(halves(pair_3, 128), halve).reshape(16, 8, 128)
    b4[0] = zero
    b4[17] = zero
    b4[1:17] = 0.125 * split_matmul(halves(pair_4, 128), halve).reshape(16, 8, 128)

    parity = (row8 + lane) & 1
    for ref in (r4, k4):
        ref[0] = zero
        ref[17] = zero
    fx4[0] = b4[1]
    for plane in range(1, 17):
        b = b4[plane]
        x_high = b4[plane + 1]
        y_low = jnp.where(row8 > 0, pltpu.roll(b, 1, 0), 0.0)
        y_high = jnp.where(row8 < 7, pltpu.roll(b, 7, 0), 0.0)
        z_high = pltpu.roll(b, 127, 1)
        total = (6.0 * b + (b4[plane - 1] + x_high)) + (
            (y_low + y_high) + (pltpu.roll(b, 1, 1) + z_high)
        )
        inside = b > 0.0
        inverse = 1.0 / jnp.where(inside, total, 1.0)
        reds = jnp.where(inside & (parity == (plane - 1) & 1), inverse, 0.0)
        fx4[plane] = b + x_high
        fy4[plane] = jnp.where(row8 < 7, b + y_high, 0.0)
        fz4[plane] = jnp.where(lane < 31, b + z_high, 0.0)
        ir4[plane] = reds
        ik4[plane] = jnp.where(inside & (parity != (plane - 1) & 1), inverse, 0.0)
        r4[plane] = g4[plane - 1] * reds

    def half_4(source, inverse, target):
        for plane in range(1, 17):
            v = source[plane]
            face_y, face_z = fy4[plane], fz4[plane]
            along_x = fx4[plane] * source[plane + 1] + fx4[plane - 1] * source[plane - 1]
            along_y = face_y * pltpu.roll(v, 7, 0) + pltpu.roll(face_y * v, 1, 0)
            along_z = face_z * pltpu.roll(v, 127, 1) + pltpu.roll(face_z * v, 1, 1)
            value = (g4[plane - 1] + along_x) + (along_y + along_z)
            target[plane] = value * inverse[plane]

    half_4(r4, ik4, k4)

    @pl.loop(1, COARSE_SWEEPS)
    def _(sweep):
        half_4(k4, ir4, r4)
        half_4(r4, ik4, k4)

    source = iota((128, 128), 0)
    target = iota((128, 128), 1)
    spread = selector_of((source < 32) & (((target & 63) >> 1) == source))
    value = split_matmul(r4[at_x + 1] + k4[at_x + 1], spread)
    twice_3[pl.ds(0, 8, stride=2), :] = value
    twice_3[pl.ds(1, 8, stride=2), :] = value
    value = k3[at_x + 1, 8:24] + twice_3[...]
    value = pltpu.roll(value, lax.rem(16 - 2 * at_y, 16), 0)
    value = pltpu.roll(value, lax.rem(128 - 16 * at_z, 128), 1)
    level_2 = []
    for part in range(2):
        fine = split_matmul(value, spread_selector(64 * part, 0, 16))[0:8]
        twice_2[pl.ds(0, 8, stride=2), :] = fine
        twice_2[pl.ds(1, 8, stride=2), :] = fine
        for index in range(2):
            own = u2_ref[2 * part + index]
            own = pltpu.roll(own, lax.rem(32 - 4 * at_y, 32), 0)
            own = pltpu.roll(own, lax.rem(128 - 32 * at_z, 128), 1)
            level_2.append(own[0:8] + twice_2[0:8])
    fine = split_matmul(jnp.concatenate(level_2, axis=0), spread_selector(0, 0, 32))
    twice_1[pl.ds(0, 32, stride=2), :] = fine
    twice_1[pl.ds(1, 32, stride=2), :] = fine
    for index in range(8):
        start = 16 * (index // 2)
        level_1[8 * index : 8 * index + 8] = u1_ref[index] + twice_1[start : start + 8]
    fine = split_matmul(level_1[...], spread_selector(0, 0, 64))
    twice_0[pl.ds(0, 64, stride=2), :] = fine
    twice_0[pl.ds(1, 64, stride=2), :] = fine
    for index in range(16):
        start = 16 * (index // 2)
        out_ref[index] = u0_ref[index] + twice_0[start : start + 16]


def call(kernel, megabytes, outs, scratch, *operands):
    whole = pl.BlockSpec(memory_space=pltpu.VMEM)
    return pl.pallas_call(
        kernel,
        out_shape=[jax.ShapeDtypeStruct(shape, F32) for shape in outs],
        in_specs=[whole] * len(operands),
        out_specs=[whole] * len(outs),
        scratch_shapes=[pltpu.VMEM(shape, F32) for shape in scratch],
        compiler_params=pltpu.CompilerParams(vmem_limit_bytes=megabytes << 20),
    )(*operands)


def shift(value, axis, step):
    count = lax.axis_size(axis)
    pairs = [(i, i + step) for i in range(count) if 0 <= i + step < count]
    return lax.ppermute(value, axis, pairs)


def on_device(right_side, conductivity):
    f, b = right_side, conductivity
    upper = jnp.concatenate([f[BLOCK - F_HALO :], b[BLOCK - B_HALO :]], axis=0)
    lower = jnp.concatenate([f[:F_HALO], b[:B_HALO]], axis=0)
    low, high = shift(upper, "gx", 1), shift(lower, "gx", -1)

    strip = (GROUPS, BLOCK, 128)
    main, left, right = call(
        pack_kernel, 4, [(PLANES, BLOCK, 128), strip, strip], [], f, b, low, high
    )
    beyond, before = shift(left, "gz", -1), shift(right, "gz", 1)
    own = jnp.concatenate([main, beyond, before], axis=0)
    low, high = shift(own, "gy", 1), shift(own, "gy", -1)

    u0, u1, coarse = call(
        fine_kernel,
        40,
        [(BLOCK, BLOCK, 128), (8, 8, 128), (16, 128)],
        Level.scratch(2, B_PLANES, ROWS)
        + Level.scratch(1, 20, 24)
        + [(512, 128)] * 2
        + [(864, 128)] * 2
        + [(128, 128)],
        low, own, high,
    )

    low, high = shift(coarse, "gx", 1), shift(coarse, "gx", -1)
    (slab,) = call(spread_kernel, 2, [(32, 32, 128)], [(32, 128)], low, coarse, high)
    slab = lax.all_to_all(slab, ("gy", "gz"), 0, 0, tiled=True)
    u2, coarse = call(
        slab_kernel,
        8,
        [(4, 32, 128), (16, 32, 128)],
        Level.scratch(1, 14, 32) + [(64, 128)] * 2,
        slab.reshape(1024, 128),
    )

    whole = lax.all_to_all(coarse, "gx", 0, 0, tiled=True)
    (out,) = call(
        coarse_kernel,
        8,
        [(BLOCK, BLOCK, 128)],
        [(18, 32, 128)] * 13
        + [(18, 8, 128)] * 7
        + [(16, 8, 128), (18, 8, 128)]
        + [(256, 128)] * 2
        + [(16, 128), (16, 128), (64, 128), (128, 128), (64, 128)],
        whole, u0, u1, u2,
    )
    return out


def solution(mesh):
    spec = P("gx", "gy", "gz")
    return jax.shard_map(
        on_device, mesh=mesh, in_specs=(spec, spec), out_specs=spec, check_vma=False
    )
```

```python
import jax
import jax.numpy as jnp
from jax import lax
from jax.experimental import pallas as pl
from jax.experimental.pallas import tpu as pltpu
from jax.sharding import PartitionSpec as P

F_HALO = 12
B_HALO = 13
BLOCK = 16
F_PLANES = BLOCK + 2 * F_HALO
B_PLANES = BLOCK + 2 * B_HALO
PLANES = F_PLANES + B_PLANES
GROUPS = -(-PLANES // 8)
F_GROUPS = F_PLANES // 8
ROWS = 48


def rows_of(index):
    if index < F_PLANES:
        return F_HALO - max(F_HALO - index, index - F_HALO - BLOCK + 1, 0)
    index -= F_PLANES
    return B_HALO - max(B_HALO - index, index - B_HALO - BLOCK + 1, 0)


COUNTS = [rows_of(index) for index in range(PLANES)]
OFFSETS = [sum(COUNTS[:index]) for index in range(PLANES)]
PACKED = sum(COUNTS)
STRIP_ROWS = [
    8 * -(-max(0, max(COUNTS[8 * group : 8 * group + 8]) - 1) // 8) for group in range(GROUPS)
]
STRIP_OFFSETS = [PACKED + sum(STRIP_ROWS[:group]) for group in range(GROUPS)]
SIDE = sum(STRIP_ROWS)
PAYLOAD = PACKED + 2 * SIDE
COARSE_SWEEPS = 8
F32 = jnp.float32


def iota(shape, dim):
    return lax.broadcasted_iota(jnp.int32, shape, dim)


def split_matmul(value, selector):
    high = value.astype(jnp.bfloat16)
    low = (value - high.astype(F32)).astype(jnp.bfloat16)
    return jnp.dot(high, selector, preferred_element_type=F32) + jnp.dot(
        low, selector, preferred_element_type=F32
    )


def selector_of(condition):
    return jnp.where(condition, 1.0, 0.0).astype(jnp.bfloat16)


def pair_selector(source_lanes, first, out_lanes, offset, count):
    source = iota((source_lanes, out_lanes), 0) - first
    target = iota((source_lanes, out_lanes), 1) - offset
    return selector_of(
        (source >= 0) & (source < 2 * count) & ((source >> 1) == target)
    )


def spread_selector(first, offset, count):
    source = iota((128, 128), 0) - first
    target = iota((128, 128), 1) - offset
    return selector_of((source >= 0) & (source < count) & ((target >> 1) == source))


class Level:
    names = ("b", "g", "fx", "fy", "fz", "d", "ir", "ik", "r", "k")

    def __init__(self, refs, columns, walled):
        self.walled = walled
        self.columns = columns
        for index, name in enumerate(self.names):
            setattr(self, name, refs[index * columns : (index + 1) * columns])
        self.lane = iota((8, 128), 1)
        self.parity = (iota((8, 128), 0) + self.lane) & 1

    @staticmethod
    def scratch(columns, planes, rows):
        return [(planes, rows + 16, 128)] * (len(Level.names) * columns)

    def at(self, refs, plane, row):
        return [ref[plane, row : row + 8] for ref in refs]

    def put(self, refs, plane, row, values):
        for ref, value in zip(refs, values):
            ref[plane, row : row + 8] = value

    def turn(self, values, step):
        rolled = [pltpu.roll(value, 127 if step > 0 else 1, 1) for value in values]
        if self.columns == 1:
            return rolled
        edge = self.lane == (127 if step > 0 else 0)
        first, second = rolled
        return [jnp.where(edge, second, first), jnp.where(edge, first, second)]

    def clear(self, planes, rows, ends):
        zero = jnp.zeros((8, 128), F32)

        @pl.loop(0, planes)
        def _(plane):
            for refs in (self.b, self.r, self.k):
                for ref in refs:
                    ref[plane, 0:8] = zero
                    ref[plane, rows + 8 : rows + 16] = zero
            for ref in self.fy:
                ref[plane, 0:8] = zero

        for refs in (self.r, self.k):
            for ref in refs:
                for plane in ends:
                    ref[plane] = jnp.zeros((rows + 16, 128), F32)

    def before(self, plane, rows):
        for row in range(8, rows + 8, 8):
            near = zip(self.at(self.b, plane, row), self.at(self.b, plane + 1, row))
            self.put(self.fx, plane, row, [own + other for own, other in near])

    def setup(self, plane, rows, red):
        for row in range(8, rows + 8, 8):
            b = self.at(self.b, plane, row)
            x_low, x_high = self.at(self.b, plane - 1, row), self.at(self.b, plane + 1, row)
            y_low, y_high = self.at(self.b, plane, row - 1), self.at(self.b, plane, row + 1)
            z_low, z_high = self.turn(b, -1), self.turn(b, 1)
            g = self.at(self.g, plane, row)
            for column in range(self.columns):
                own, z_before, z_after = b[column], z_low[column], z_high[column]
                face = own + z_after
                if self.walled:
                    z_before = jnp.where(self.lane > 0, z_before, 0.0)
                    z_after = jnp.where(self.lane < 127, z_after, 0.0)
                    face = jnp.where(self.lane < 127, face, 0.0)
                total = (6.0 * own + (x_low[column] + x_high[column])) + (
                    (y_low[column] + y_high[column]) + (z_before + z_after)
                )
                inside = own > 0.0
                inverse = 1.0 / jnp.where(inside, total, 1.0)
                first = self.parity == red
                reds = jnp.where(inside & first, inverse, 0.0)
                here = (plane, slice(row, row + 8))
                self.fx[column][here] = own + x_high[column]
                self.fy[column][here] = own + y_high[column]
                self.fz[column][here] = face
                self.d[column][here] = total
                self.ir[column][here] = reds
                self.ik[column][here] = jnp.where(inside & ~first, inverse, 0.0)
                self.r[column][here] = g[column] * reds
                self.k[column][here] = jnp.zeros((8, 128), F32)

    def total(self, source, base, step, row, held=None):
        held = {} if held is None else held

        def load(ref, plane):
            key = (id(ref), plane)
            if key not in held:
                held[key] = ref[base + plane, row : row + 8]
            return held[key]

        v = [load(ref, step) for ref in source]
        face_z = [load(ref, step) for ref in self.fz]
        z_high = self.turn(v, 1)
        z_low = self.turn([face * value for face, value in zip(face_z, v)], -1)
        out = []
        for column in range(self.columns):
            ref, fx, fy = source[column], self.fx[column], self.fy[column]
            along_x = load(fx, step) * load(ref, step + 1) + load(fx, step - 1) * load(ref, step - 1)
            low, high = slice(row - 1, row + 7), slice(row + 1, row + 9)
            plane = base + step
            along_y = load(fy, step) * ref[plane, high] + fy[plane, low] * ref[plane, low]
            along_z = face_z[column] * z_high[column] + z_low[column]
            out.append((load(self.g[column], step) + along_x) + (along_y + along_z))
        return out

    def relax(self, step, base, count, rows):
        source, inverse, target = (
            (self.r, self.ik, self.k),
            (self.k, self.ir, self.r),
            (self.r, self.ik, self.k),
        )[step]
        for row in rows:
            held = {}
            for index in range(count):
                values = self.total(source, base, index, row, held)
                scale = self.at(inverse, base + index, row)
                values = [value * factor for value, factor in zip(values, scale)]
                if step == 2:
                    own = self.at(self.r, base + index, row)
                    values = [a + b for a, b in zip(values, own)]
                self.put(target, base + index, row, values)

    def rest(self, base, row, step=0, held=None):
        values = self.total(self.k, base, step, row, held)
        plane = base + step
        out = []
        for column, value in enumerate(values):
            here = (plane, slice(row, row + 8))
            value = value - self.d[column][here] * self.k[column][here]
            out.append(jnp.where(self.b[column][here] > 0.0, value, 0.0))
        return out


def halves(ref, rows):
    return ref[pl.ds(0, rows, stride=2), :] + ref[pl.ds(1, rows, stride=2), :]


def pack_kernel(
    f_ref, b_ref, low_ref, high_ref, main_ref, left_ref, right_ref, down_ref, up_ref
):
    lane = iota((BLOCK, 128), 1)

    def source(index):
        if index < F_HALO:
            return low_ref[index]
        if index < F_HALO + BLOCK:
            return f_ref[index - F_HALO]
        if index < F_PLANES:
            return high_ref[index - F_HALO - BLOCK]
        index -= F_PLANES
        if index < B_HALO:
            return low_ref[F_HALO + index]
        if index < B_HALO + BLOCK:
            return b_ref[index - B_HALO]
        return high_ref[F_HALO + index - B_HALO - BLOCK]

    for group in range(GROUPS):
        left = jnp.zeros((BLOCK, 128), F32)
        right = jnp.zeros((BLOCK, 128), F32)
        for slot in range(8):
            index = group * 8 + slot
            if index >= PLANES:
                break
            plane = source(index)
            main_ref[index] = plane
            count, start = COUNTS[index], OFFSETS[index]
            if count:
                down_ref[start : start + count] = plane[0:count]
                up_ref[start : start + count] = plane[BLOCK - count : BLOCK]
            turned = pltpu.roll(plane, 16 * slot, 1) if slot else plane
            left = jnp.where((lane >> 4) == slot, turned, left)
            right = jnp.where((lane >> 4) == ((slot - 1) & 7), turned, right)
        left_ref[group] = left
        right_ref[group] = right


def join_kernel(down_ref, up_ref, after_ref, before_ref, down_out, up_out):
    down_out[0:PACKED] = down_ref[...]
    up_out[0:PACKED] = up_ref[...]
    for side, strips in enumerate((after_ref, before_ref)):
        for group in range(GROUPS):
            count = STRIP_ROWS[group]
            start = STRIP_OFFSETS[group] + side * SIDE
            if count:
                down_out[start : start + count] = strips[group, 0:count]
                up_out[start : start + count] = strips[group, BLOCK - count : BLOCK]


def fine_kernel(
    low_ref, high_ref, main_ref, after_ref, before_ref, u0_ref, u1_ref, coarse_ref, *scratch
):
    count = len(Level.names)
    fine = Level(scratch[: 2 * count], 2, False)
    middle = Level(scratch[2 * count : 3 * count], 1, False)
    rest_main, rest_side, sum_main, sum_side, collect = scratch[3 * count :]

    blank = jnp.zeros((BLOCK, 128), F32)

    def unpack(after, before):
        even = ((iota(after.shape, 1) >> 4) & 1) == 0
        return jnp.where(even, after, before), jnp.where(even, before, after)

    def place(target, plane, index, scale):
        group, slot = index // 8, index % 8
        count, start = COUNTS[index], OFFSETS[index]
        main, side = target
        first, own, last = 8, 8 + BLOCK, 8 + 2 * BLOCK
        main[plane, first:own] = blank
        main[plane, last : last + BLOCK] = blank
        main[plane, own:last] = main_ref[index] * scale
        if count:
            main[plane, own - count : own] = low_ref[start : start + count] * scale
            main[plane, last : last + count] = high_ref[start : start + count] * scale

        def turned(pair):
            value = pair[slot & 1]
            if slot:
                value = pltpu.roll(value, 128 - 16 * slot, 1)
            lane = iota(value.shape, 1)
            return jnp.where((lane < 16) | (lane >= 112), value, 0.0) * scale

        side[plane, own:last] = turned(unpack(after_ref[group], before_ref[group]))
        rows = STRIP_ROWS[group]
        if rows < BLOCK:
            side[plane, first:own] = blank
            side[plane, last : last + BLOCK] = blank
        if rows:
            start = STRIP_OFFSETS[group]
            beyond = slice(start, start + rows), slice(start + SIDE, start + SIDE + rows)
            side[plane, own - rows : own] = turned(unpack(low_ref[beyond[0]], low_ref[beyond[1]]))
            side[plane, last : last + rows] = turned(
                unpack(high_ref[beyond[0]], high_ref[beyond[1]])
            )

    for index in range(F_PLANES):
        place(fine.g, index + 1, index, 2.0)
    for index in range(F_PLANES, PLANES):
        place(fine.b, index - F_PLANES, index, 1.0)

    fine.clear(B_PLANES, ROWS, (0, B_PLANES - 1))
    fine.before(0, ROWS)

    @pl.loop(1, B_PLANES - 1, step=4)
    def _(plane):
        for index in range(4):
            fine.setup(plane + index, ROWS, index & 1)

    every = range(8, ROWS + 8, 8)
    inner = range(16, ROWS, 8)
    for step in range(3):
        beside = 2 - step
        near = B_HALO - beside

        count = (4, 3, 4)[step]

        @pl.loop(near, near + BLOCK + 2 * beside, step=count)
        def _(plane):
            fine.relax(step, plane, count, every)

        @pl.loop(near - 9, near, step=3)
        def _(plane):
            fine.relax(step, plane, 3, inner)
            fine.relax(step, plane + BLOCK + 2 * beside + 9, 3, inner)

    for plane in range(BLOCK):
        u0_ref[plane] = fine.k[0][plane + B_HALO, 8 + BLOCK : 8 + 2 * BLOCK]

    @pl.loop(0, 16)
    def _(index):
        for row in inner:
            held = {}
            first = fine.rest(2 * index + 5, row, 0, held)
            second = fine.rest(2 * index + 5, row, 1, held)
            at = pl.ds(pl.multiple_of(32 * index + (row - 16), 8), 8)
            rest_main[at, :] = first[0] + second[0]
            rest_side[at, :] = first[1] + second[1]

    @pl.loop(0, 18)
    def _(index):
        for row in every:
            at = pl.ds(pl.multiple_of(48 * index + (row - 8), 8), 8)
            first, second = 2 * index + 3, 2 * index + 4
            here = slice(row, row + 8)
            sum_main[at, :] = fine.b[0][first, here] + fine.b[0][second, here]
            sum_side[at, :] = fine.b[1][first, here] + fine.b[1][second, here]

    to_main = pair_selector(128, 0, 128, 0, 64)
    to_side = pair_selector(128, 0, 128, 64, 64)
    g_next = split_matmul(halves(rest_main, 256), to_main)
    g_next = 0.5 * (g_next + split_matmul(halves(rest_side, 256), to_side))
    b_next = split_matmul(halves(sum_main, 432), to_main)
    b_next = 0.125 * (b_next + split_matmul(halves(sum_side, 432), to_side))

    middle.clear(20, 24, (1, 18))
    zero = jnp.zeros((8, 128), F32)
    for plane in range(2, 18):
        middle.g[0][plane, 8:16] = zero
        middle.g[0][plane, 24:32] = zero
        middle.g[0][plane, 12:28] = g_next[16 * (plane - 2) : 16 * (plane - 1)]
    for plane in range(1, 19):
        middle.b[0][plane, 8:32] = b_next[24 * (plane - 1) : 24 * plane]
    middle.before(1, 24)

    @pl.loop(2, 18, step=4)
    def _(plane):
        for index in range(4):
            middle.setup(plane + index, 24, index & 1)

    for step in range(3):

        @pl.loop(2, 18, step=4)
        def _(plane):
            middle.relax(step, plane, 4, range(8, 32, 8))

    for plane in range(8):
        u1_ref[plane] = middle.k[0][plane + 6, 16:24]
    for index in range(4):
        (first,) = middle.rest(2 * index + 6, 16)
        (second,) = middle.rest(2 * index + 7, 16)
        collect[8 * index : 8 * index + 8] = 0.5 * (first + second)
    for index in range(6):
        first, second = middle.b[0][2 * index + 4, 16:24], middle.b[0][2 * index + 5, 16:24]
        collect[8 * index + 32 : 8 * index + 40] = 0.125 * (first + second)
    collect[80:128] = jnp.zeros((48, 128), F32)
    out = jnp.zeros((16, 128), F32)
    for part in range(4):
        rows = collect[pl.ds(2 * part, 16, stride=8), :]
        rows = rows + collect[pl.ds(2 * part + 1, 16, stride=8), :]
        out = out + split_matmul(rows, pair_selector(128, 0, 128, 32 * part, 32))
    coarse_ref[...] = out


def spread_kernel(low_ref, own_ref, high_ref, out_ref, rows):
    rows[0:4] = low_ref[0:4]
    rows[4:8] = own_ref[0:4]
    rows[8:12] = high_ref[0:4]
    rows[12:17] = low_ref[4:9]
    rows[17:21] = own_ref[5:9]
    rows[21:26] = high_ref[5:10]
    rows[26:32] = jnp.zeros((6, 128), F32)
    value = rows[...]
    for index in range(32):
        out_ref[index] = value


def slab_kernel(gathered_ref, u2_ref, coarse_ref, *scratch):
    slab = Level(scratch[: len(Level.names)], 1, True)
    rest, sums = scratch[len(Level.names) :]
    row = iota((4, 8, 128), 1)
    lane = iota((4, 8, 128), 2)
    group = lane >> 5
    turn = (group - row) & 3

    def exchange(value):
        value = value.reshape(4, 8, 128)
        out = value
        for d in (1, 2, 3):
            moved = pltpu.roll(value, 32 * d, 2)
            near = pltpu.roll(moved, 8 - d, 1)
            far = pltpu.roll(moved, 4 - d, 1)
            out = jnp.where(turn == d, jnp.where(group >= d, near, far), out)
        return out.reshape(32, 128)

    for plane in range(12):
        slab.g[0][plane + 1, 8:40] = exchange(gathered_ref[pl.ds(plane, 32, stride=32), :])
    for plane in range(14):
        slab.b[0][plane, 8:40] = exchange(gathered_ref[pl.ds(plane + 12, 32, stride=32), :])

    slab.clear(14, 32, (0, 13))
    slab.before(0, 32)

    @pl.loop(1, 13, step=4)
    def _(plane):
        for index in range(4):
            slab.setup(plane + index, 32, index & 1)

    for step in range(3):

        @pl.loop(2 + step, 12 - step, step=2)
        def _(plane):
            slab.relax(step, plane, 2, range(8, 40, 8))

    for plane in range(4):
        u2_ref[plane] = slab.k[0][plane + 5, 8:40]
    for part in range(2):
        for row in range(8, 40, 8):
            (first,) = slab.rest(5 + 2 * part, row)
            (second,) = slab.rest(6 + 2 * part, row)
            at = slice(32 * part + row - 8, 32 * part + row)
            rest[at] = 0.5 * (first + second)
            here = slice(row, row + 8)
            sums[at] = 0.125 * (slab.b[0][5 + 2 * part, here] + slab.b[0][6 + 2 * part, here])
    g_rows, b_rows = halves(rest, 32), halves(sums, 32)
    value = jnp.zeros((32, 128), F32)
    for part in range(2):
        own = slice(16 * part, 16 * part + 16)
        rows = jnp.concatenate([g_rows[own], b_rows[own]], axis=0)
        value = value + split_matmul(rows, pair_selector(128, 0, 128, 64 * part, 64))
    for index in range(16):
        coarse_ref[index] = value


def coarse_kernel(
    gathered_ref, u0_ref, u1_ref, u2_ref, out_ref,
    r3, rs, k3, ks, inner_3, outer_3, fy3, fz3, d3, ir3, ik3, b3, bs,
    r4, k4, fx4, fy4, fz4, ir4, ik4, g4, b4,
    pair_3, pair_4, twice_3, twice_2, twice_1, twice_0, level_1,
):
    at_x = lax.axis_index("gx")
    at_y = lax.axis_index("gy")
    at_z = lax.axis_index("gz")
    lane = iota((8, 128), 1)
    row8 = iota((8, 128), 0)
    zero = jnp.zeros((8, 128), F32)

    cell = lane & 63
    parity = ((lane >> 6) + row8 + cell) & 1
    first_half = lane < 64
    for ref in (r3, rs, k3, ks, b3, bs):
        for plane in (0, 17):
            ref[plane] = jnp.zeros((32, 128), F32)
    for plane in range(1, 17):
        for ref in (r3, k3, b3, fy3):
            ref[plane, 0:8] = zero
            ref[plane, 24:32] = zero
        for row in (8, 16):
            value = gathered_ref[plane - 1, row + 8 : row + 16]
            b3[plane, row : row + 8] = value
            bs[plane, row : row + 8] = pltpu.roll(value, 64, 1)

    def outer(ref, plane, here):
        return jnp.where(first_half, ref[plane - 1, here], ref[plane + 1, here])

    for plane in range(1, 17):
        for row in (8, 16):
            here = slice(row, row + 8)
            b = b3[plane, here]
            partner, other = bs[plane, here], outer(bs, plane, here)
            y_high = b3[plane, row + 1 : row + 9]
            z_low = jnp.where(cell > 0, pltpu.roll(b, 1, 1), 0.0)
            z_high = jnp.where(cell < 63, pltpu.roll(b, 127, 1), 0.0)
            total = (6.0 * b + (partner + other)) + (
                (b3[plane, row - 1 : row + 7] + y_high) + (z_low + z_high)
            )
            inside = b > 0.0
            inverse = 1.0 / jnp.where(inside, total, 1.0)
            reds = jnp.where(inside & (parity == 0), inverse, 0.0)
            inner_3[plane, here] = b + partner
            outer_3[plane, here] = b + other
            fy3[plane, here] = b + y_high
            fz3[plane, here] = jnp.where(cell < 63, b + z_high, 0.0)
            d3[plane, here] = total
            ir3[plane, here] = reds
            ik3[plane, here] = jnp.where(inside & (parity == 1), inverse, 0.0)
            value = gathered_ref[plane - 1, row - 8 : row] * reds
            r3[plane, here] = value
            rs[plane, here] = pltpu.roll(value, 64, 1)

    def total_3(ref, swapped, plane, row):
        here, low, high = slice(row, row + 8), slice(row - 1, row + 7), slice(row + 1, row + 9)
        v, face = ref[plane, here], fz3[plane, here]
        along_x = inner_3[plane, here] * swapped[plane, here]
        along_x = along_x + outer_3[plane, here] * outer(swapped, plane, here)
        along_y = fy3[plane, here] * ref[plane, high] + fy3[plane, low] * ref[plane, low]
        along_z = face * pltpu.roll(v, 127, 1) + pltpu.roll(face * v, 1, 1)
        return (gathered_ref[plane - 1, row - 8 : row] + along_x) + (along_y + along_z)

    for step in range(3):
        source, inverse, target = (
            ((r3, rs), ik3, (k3, ks)),
            ((k3, ks), ir3, (r3, rs)),
            ((r3, rs), ik3, (k3, ks)),
        )[step]
        for plane in range(1, 17):
            for row in (8, 16):
                here = slice(row, row + 8)
                value = total_3(*source, plane, row) * inverse[plane, here]
                if step == 2:
                    value = value + r3[plane, here]
                target[0][plane, here] = value
                target[1][plane, here] = pltpu.roll(value, 64, 1)

    for plane in range(1, 17):
        for row in (8, 16):
            here = slice(row, row + 8)
            value = total_3(k3, ks, plane, row) - d3[plane, here] * k3[plane, here]
            at = slice(16 * (plane - 1) + row - 8, 16 * (plane - 1) + row)
            pair_3[at] = value + pltpu.roll(value, 64, 1)
            pair_4[at] = b3[plane, here] + bs[plane, here]
    halve = pair_selector(128, 0, 128, 0, 32)
    g4[...] = 0.5 * split_matmul(halves(pair_3, 128), halve).reshape(16, 8, 128)
    b4[0] = zero
    b4[17] = zero
    b4[1:17] = 0.125 * split_matmul(halves(pair_4, 128), halve).reshape(16, 8, 128)

    parity = (row8 + lane) & 1
    for ref in (r4, k4):
        ref[0] = zero
        ref[17] = zero
    fx4[0] = b4[1]
    for plane in range(1, 17):
        b = b4[plane]
        x_high = b4[plane + 1]
        y_low = jnp.where(row8 > 0, pltpu.roll(b, 1, 0), 0.0)
        y_high = jnp.where(row8 < 7, pltpu.roll(b, 7, 0), 0.0)
        z_high = pltpu.roll(b, 127, 1)
        total = (6.0 * b + (b4[plane - 1] + x_high)) + (
            (y_low + y_high) + (pltpu.roll(b, 1, 1) + z_high)
        )
        inside = b > 0.0
        inverse = 1.0 / jnp.where(inside, total, 1.0)
        reds = jnp.where(inside & (parity == (plane - 1) & 1), inverse, 0.0)
        fx4[plane] = b + x_high
        fy4[plane] = jnp.where(row8 < 7, b + y_high, 0.0)
        fz4[plane] = jnp.where(lane < 31, b + z_high, 0.0)
        ir4[plane] = reds
        ik4[plane] = jnp.where(inside & (parity != (plane - 1) & 1), inverse, 0.0)
        r4[plane] = g4[plane - 1] * reds

    def half_4(source, inverse, target):
        for plane in range(1, 17):
            v = source[plane]
            face_y, face_z = fy4[plane], fz4[plane]
            along_x = fx4[plane] * source[plane + 1] + fx4[plane - 1] * source[plane - 1]
            along_y = face_y * pltpu.roll(v, 7, 0) + pltpu.roll(face_y * v, 1, 0)
            along_z = face_z * pltpu.roll(v, 127, 1) + pltpu.roll(face_z * v, 1, 1)
            value = (g4[plane - 1] + along_x) + (along_y + along_z)
            target[plane] = value * inverse[plane]

    half_4(r4, ik4, k4)

    @pl.loop(1, COARSE_SWEEPS)
    def _(sweep):
        half_4(k4, ir4, r4)
        half_4(r4, ik4, k4)

    source = iota((128, 128), 0)
    target = iota((128, 128), 1)
    spread = selector_of((source < 32) & (((target & 63) >> 1) == source))
    value = split_matmul(r4[at_x + 1] + k4[at_x + 1], spread)
    twice_3[pl.ds(0, 8, stride=2), :] = value
    twice_3[pl.ds(1, 8, stride=2), :] = value
    value = k3[at_x + 1, 8:24] + twice_3[...]
    value = pltpu.roll(value, lax.rem(16 - 2 * at_y, 16), 0)
    value = pltpu.roll(value, lax.rem(128 - 16 * at_z, 128), 1)
    level_2 = []
    for part in range(2):
        fine = split_matmul(value, spread_selector(64 * part, 0, 16))[0:8]
        twice_2[pl.ds(0, 8, stride=2), :] = fine
        twice_2[pl.ds(1, 8, stride=2), :] = fine
        for index in range(2):
            own = u2_ref[2 * part + index]
            own = pltpu.roll(own, lax.rem(32 - 4 * at_y, 32), 0)
            own = pltpu.roll(own, lax.rem(128 - 32 * at_z, 128), 1)
            level_2.append(own[0:8] + twice_2[0:8])
    fine = split_matmul(jnp.concatenate(level_2, axis=0), spread_selector(0, 0, 32))
    twice_1[pl.ds(0, 32, stride=2), :] = fine
    twice_1[pl.ds(1, 32, stride=2), :] = fine
    for index in range(8):
        start = 16 * (index // 2)
        level_1[8 * index : 8 * index + 8] = u1_ref[index] + twice_1[start : start + 8]
    fine = split_matmul(level_1[...], spread_selector(0, 0, 64))
    twice_0[pl.ds(0, 64, stride=2), :] = fine
    twice_0[pl.ds(1, 64, stride=2), :] = fine
    for index in range(16):
        start = 16 * (index // 2)
        out_ref[index] = u0_ref[index] + twice_0[start : start + 16]


def call(kernel, megabytes, outs, scratch, *operands):
    whole = pl.BlockSpec(memory_space=pltpu.VMEM)
    return pl.pallas_call(
        kernel,
        out_shape=[jax.ShapeDtypeStruct(shape, F32) for shape in outs],
        in_specs=[whole] * len(operands),
        out_specs=[whole] * len(outs),
        scratch_shapes=[pltpu.VMEM(shape, F32) for shape in scratch],
        compiler_params=pltpu.CompilerParams(vmem_limit_bytes=megabytes << 20),
    )(*operands)


def shift(value, axis, step):
    count = lax.axis_size(axis)
    pairs = [(i, i + step) for i in range(count) if 0 <= i + step < count]
    return lax.ppermute(value, axis, pairs)


def on_device(right_side, conductivity):
    f, b = right_side, conductivity
    upper = jnp.concatenate([f[BLOCK - F_HALO :], b[BLOCK - B_HALO :]], axis=0)
    lower = jnp.concatenate([f[:F_HALO], b[:B_HALO]], axis=0)
    low, high = shift(upper, "gx", 1), shift(lower, "gx", -1)

    strip = (GROUPS, BLOCK, 128)
    packed = (PACKED, 128)
    main, left, right, down, up = call(
        pack_kernel, 4, [(PLANES, BLOCK, 128), strip, strip, packed, packed], [], f, b, low, high
    )
    after, before = shift(left, "gz", -1), shift(right, "gz", 1)
    down, up = call(join_kernel, 4, [(PAYLOAD, 128)] * 2, [], down, up, after, before)
    low, high = shift(up, "gy", 1), shift(down, "gy", -1)

    u0, u1, coarse = call(
        fine_kernel,
        40,
        [(BLOCK, BLOCK, 128), (8, 8, 128), (16, 128)],
        Level.scratch(2, B_PLANES, ROWS)
        + Level.scratch(1, 20, 24)
        + [(512, 128)] * 2
        + [(864, 128)] * 2
        + [(128, 128)],
        low, high, main, after, before,
    )

    low, high = shift(coarse, "gx", 1), shift(coarse, "gx", -1)
    (slab,) = call(spread_kernel, 2, [(32, 32, 128)], [(32, 128)], low, coarse, high)
    slab = lax.all_to_all(slab, ("gy", "gz"), 0, 0, tiled=True)
    u2, coarse = call(
        slab_kernel,
        8,
        [(4, 32, 128), (16, 32, 128)],
        Level.scratch(1, 14, 32) + [(64, 128)] * 2,
        slab.reshape(1024, 128),
    )

    whole = lax.all_to_all(coarse, "gx", 0, 0, tiled=True)
    (out,) = call(
        coarse_kernel,
        8,
        [(BLOCK, BLOCK, 128)],
        [(18, 32, 128)] * 13
        + [(18, 8, 128)] * 7
        + [(16, 8, 128), (18, 8, 128)]
        + [(256, 128)] * 2
        + [(16, 128), (16, 128), (64, 128), (128, 128), (64, 128)],
        whole, u0, u1, u2,
    )
    return out


def solution(mesh):
    spec = P("gx", "gy", "gz")
    return jax.shard_map(
        on_device, mesh=mesh, in_specs=(spec, spec), out_specs=spec, check_vma=False
    )
```

```python
import jax
import jax.numpy as jnp
from jax import lax
from jax.experimental import pallas as pl
from jax.experimental.pallas import tpu as pltpu
from jax.sharding import PartitionSpec as P

F_HALO = 12
B_HALO = 13
BLOCK = 16
F_PLANES = BLOCK + 2 * F_HALO
B_PLANES = BLOCK + 2 * B_HALO
PLANES = F_PLANES + B_PLANES
GROUPS = -(-PLANES // 8)
F_GROUPS = F_PLANES // 8
ROWS = 48


def rows_of(index):
    if index < F_PLANES:
        return F_HALO - max(F_HALO - index, index - F_HALO - BLOCK + 1, 0)
    index -= F_PLANES
    return B_HALO - max(B_HALO - index, index - B_HALO - BLOCK + 1, 0)


COUNTS = [rows_of(index) for index in range(PLANES)]
OFFSETS = [sum(COUNTS[:index]) for index in range(PLANES)]
PACKED = sum(COUNTS)
STRIP_ROWS = [
    8 * -(-max(0, max(COUNTS[8 * group : 8 * group + 8]) - 1) // 8) for group in range(GROUPS)
]
STRIP_OFFSETS = [PACKED + sum(STRIP_ROWS[:group]) for group in range(GROUPS)]
SIDE = sum(STRIP_ROWS)
PAYLOAD = PACKED + 2 * SIDE
COARSE_SWEEPS = 8
F32 = jnp.float32


def iota(shape, dim):
    return lax.broadcasted_iota(jnp.int32, shape, dim)


def split_matmul(value, selector):
    high = value.astype(jnp.bfloat16)
    low = (value - high.astype(F32)).astype(jnp.bfloat16)
    return jnp.dot(high, selector, preferred_element_type=F32) + jnp.dot(
        low, selector, preferred_element_type=F32
    )


def selector_of(condition):
    return jnp.where(condition, 1.0, 0.0).astype(jnp.bfloat16)


def pair_selector(source_lanes, first, out_lanes, offset, count):
    source = iota((source_lanes, out_lanes), 0) - first
    target = iota((source_lanes, out_lanes), 1) - offset
    return selector_of(
        (source >= 0) & (source < 2 * count) & ((source >> 1) == target)
    )


def spread_selector(first, offset, count):
    source = iota((128, 128), 0) - first
    target = iota((128, 128), 1) - offset
    return selector_of((source >= 0) & (source < count) & ((target >> 1) == source))


class Level:
    names = ("b", "g", "fx", "fy", "fz", "d", "ir", "ik", "r", "k")

    def __init__(self, refs, columns, walled):
        self.walled = walled
        self.columns = columns
        for index, name in enumerate(self.names):
            setattr(self, name, refs[index * columns : (index + 1) * columns])
        self.lane = iota((8, 128), 1)
        self.parity = (iota((8, 128), 0) + self.lane) & 1

    @staticmethod
    def scratch(columns, planes, rows):
        return [(planes, rows + 16, 128)] * (len(Level.names) * columns)

    def at(self, refs, plane, row):
        return [ref[plane, row : row + 8] for ref in refs]

    def put(self, refs, plane, row, values):
        for ref, value in zip(refs, values):
            ref[plane, row : row + 8] = value

    def turn(self, values, step):
        rolled = [pltpu.roll(value, 127 if step > 0 else 1, 1) for value in values]
        if self.columns == 1:
            return rolled
        edge = self.lane == (127 if step > 0 else 0)
        first, second = rolled
        return [jnp.where(edge, second, first), jnp.where(edge, first, second)]

    def clear(self, planes, rows, ends):
        zero = jnp.zeros((8, 128), F32)

        @pl.loop(0, planes)
        def _(plane):
            for refs in (self.b, self.r, self.k):
                for ref in refs:
                    ref[plane, 0:8] = zero
                    ref[plane, rows + 8 : rows + 16] = zero
            for ref in self.fy:
                ref[plane, 0:8] = zero

        for refs in (self.r, self.k):
            for ref in refs:
                for plane in ends:
                    ref[plane] = jnp.zeros((rows + 16, 128), F32)

    def before(self, plane, rows):
        for row in range(8, rows + 8, 8):
            near = zip(self.at(self.b, plane, row), self.at(self.b, plane + 1, row))
            self.put(self.fx, plane, row, [own + other for own, other in near])

    def setup(self, plane, rows, red):
        for row in range(8, rows + 8, 8):
            b = self.at(self.b, plane, row)
            x_low, x_high = self.at(self.b, plane - 1, row), self.at(self.b, plane + 1, row)
            y_low, y_high = self.at(self.b, plane, row - 1), self.at(self.b, plane, row + 1)
            z_low, z_high = self.turn(b, -1), self.turn(b, 1)
            g = self.at(self.g, plane, row)
            for column in range(self.columns):
                own, z_before, z_after = b[column], z_low[column], z_high[column]
                face = own + z_after
                if self.walled:
                    z_before = jnp.where(self.lane > 0, z_before, 0.0)
                    z_after = jnp.where(self.lane < 127, z_after, 0.0)
                    face = jnp.where(self.lane < 127, face, 0.0)
                total = (6.0 * own + (x_low[column] + x_high[column])) + (
                    (y_low[column] + y_high[column]) + (z_before + z_after)
                )
                inside = own > 0.0
                inverse = 1.0 / jnp.where(inside, total, 1.0)
                first = self.parity == red
                reds = jnp.where(inside & first, inverse, 0.0)
                here = (plane, slice(row, row + 8))
                self.fx[column][here] = own + x_high[column]
                self.fy[column][here] = own + y_high[column]
                self.fz[column][here] = face
                self.d[column][here] = total
                self.ir[column][here] = reds
                self.ik[column][here] = jnp.where(inside & ~first, inverse, 0.0)
                self.r[column][here] = g[column] * reds
                self.k[column][here] = jnp.zeros((8, 128), F32)

    def total(self, source, base, step, row, held=None):
        held = {} if held is None else held

        def load(ref, plane):
            key = (id(ref), plane)
            if key not in held:
                held[key] = ref[base + plane, row : row + 8]
            return held[key]

        v = [load(ref, step) for ref in source]
        face_z = [load(ref, step) for ref in self.fz]
        z_high = self.turn(v, 1)
        z_low = self.turn([face * value for face, value in zip(face_z, v)], -1)
        out = []
        for column in range(self.columns):
            ref, fx, fy = source[column], self.fx[column], self.fy[column]
            along_x = load(fx, step) * load(ref, step + 1) + load(fx, step - 1) * load(ref, step - 1)
            low, high = slice(row - 1, row + 7), slice(row + 1, row + 9)
            plane = base + step
            along_y = load(fy, step) * ref[plane, high] + fy[plane, low] * ref[plane, low]
            along_z = face_z[column] * z_high[column] + z_low[column]
            out.append((load(self.g[column], step) + along_x) + (along_y + along_z))
        return out

    def relax(self, step, base, count, rows):
        source, inverse, target = (
            (self.r, self.ik, self.k),
            (self.k, self.ir, self.r),
            (self.r, self.ik, self.k),
        )[step]
        for row in rows:
            held = {}
            for index in range(count):
                values = self.total(source, base, index, row, held)
                scale = self.at(inverse, base + index, row)
                values = [value * factor for value, factor in zip(values, scale)]
                if step == 2:
                    own = self.at(self.r, base + index, row)
                    values = [a + b for a, b in zip(values, own)]
                self.put(target, base + index, row, values)

    def rest(self, base, row, step=0, held=None):
        values = self.total(self.k, base, step, row, held)
        plane = base + step
        out = []
        for column, value in enumerate(values):
            here = (plane, slice(row, row + 8))
            value = value - self.d[column][here] * self.k[column][here]
            out.append(jnp.where(self.b[column][here] > 0.0, value, 0.0))
        return out


def halves(ref, rows):
    return ref[pl.ds(0, rows, stride=2), :] + ref[pl.ds(1, rows, stride=2), :]


def pack_kernel(
    f_ref, b_ref, low_ref, high_ref, main_ref, left_ref, right_ref, down_ref, up_ref
):
    lane = iota((BLOCK, 128), 1)
    even = lax.rem(lax.axis_index("gz"), 2) == 0

    def source(index):
        if index < F_HALO:
            return low_ref[index]
        if index < F_HALO + BLOCK:
            return f_ref[index - F_HALO]
        if index < F_PLANES:
            return high_ref[index - F_HALO - BLOCK]
        index -= F_PLANES
        if index < B_HALO:
            return low_ref[F_HALO + index]
        if index < B_HALO + BLOCK:
            return b_ref[index - B_HALO]
        return high_ref[F_HALO + index - B_HALO - BLOCK]

    for group in range(GROUPS):
        left = jnp.zeros((BLOCK, 128), F32)
        right = jnp.zeros((BLOCK, 128), F32)
        for slot in range(8):
            index = group * 8 + slot
            if index >= PLANES:
                break
            plane = source(index)
            main_ref[index] = plane
            count, start = COUNTS[index], OFFSETS[index]
            if count:
                down_ref[start : start + count] = plane[0:count]
                up_ref[start : start + count] = plane[BLOCK - count : BLOCK]
            turned = pltpu.roll(plane, 16 * slot, 1) if slot else plane
            left = jnp.where((lane >> 4) == slot, turned, left)
            right = jnp.where((lane >> 4) == ((slot - 1) & 7), turned, right)
        left_ref[group] = jnp.where(even, right, left)
        right_ref[group] = jnp.where(even, left, right)


def join_kernel(
    down_ref, up_ref, first_ref, second_ref, down_out, up_out, after_ref, before_ref
):
    even = lax.rem(lax.axis_index("gz"), 2) == 0
    for group in range(GROUPS):
        first, second = first_ref[group], second_ref[group]
        after_ref[group] = jnp.where(even, first, second)
        before_ref[group] = jnp.where(even, second, first)
    down_out[0:PACKED] = down_ref[...]
    up_out[0:PACKED] = up_ref[...]
    for side, strips in enumerate((after_ref, before_ref)):
        for group in range(GROUPS):
            count = STRIP_ROWS[group]
            start = STRIP_OFFSETS[group] + side * SIDE
            if count:
                down_out[start : start + count] = strips[group, 0:count]
                up_out[start : start + count] = strips[group, BLOCK - count : BLOCK]


def fine_kernel(
    low_ref, high_ref, main_ref, after_ref, before_ref, u0_ref, u1_ref, coarse_ref, *scratch
):
    count = len(Level.names)
    fine = Level(scratch[: 2 * count], 2, False)
    middle = Level(scratch[2 * count : 3 * count], 1, False)
    rest_main, rest_side, sum_main, sum_side, collect = scratch[3 * count :]

    blank = jnp.zeros((BLOCK, 128), F32)

    def unpack(after, before):
        even = ((iota(after.shape, 1) >> 4) & 1) == 0
        return jnp.where(even, after, before), jnp.where(even, before, after)

    at_y = lax.axis_index("gy")
    low_there = jnp.where(at_y > 0, 1.0, 0.0)
    high_there = jnp.where(at_y < lax.axis_size("gy") - 1, 1.0, 0.0)

    def place(target, plane, index, scale):
        low_scale, high_scale = low_there * scale, high_there * scale
        group, slot = index // 8, index % 8
        count, start = COUNTS[index], OFFSETS[index]
        main, side = target
        first, own, last = 8, 8 + BLOCK, 8 + 2 * BLOCK
        main[plane, first:own] = blank
        main[plane, last : last + BLOCK] = blank
        main[plane, own:last] = main_ref[index] * scale
        if count:
            main[plane, own - count : own] = low_ref[start : start + count] * low_scale
            main[plane, last : last + count] = high_ref[start : start + count] * high_scale

        def turned(pair, scale):
            value = pair[slot & 1]
            if slot:
                value = pltpu.roll(value, 128 - 16 * slot, 1)
            lane = iota(value.shape, 1)
            return jnp.where((lane < 16) | (lane >= 112), value, 0.0) * scale

        side[plane, own:last] = turned(unpack(after_ref[group], before_ref[group]), scale)
        rows = STRIP_ROWS[group]
        if rows < BLOCK:
            side[plane, first:own] = blank
            side[plane, last : last + BLOCK] = blank
        if rows:
            start = STRIP_OFFSETS[group]
            beyond = slice(start, start + rows), slice(start + SIDE, start + SIDE + rows)
            side[plane, own - rows : own] = turned(
                unpack(low_ref[beyond[0]], low_ref[beyond[1]]), low_scale
            )
            side[plane, last : last + rows] = turned(
                unpack(high_ref[beyond[0]], high_ref[beyond[1]]), high_scale
            )

    for index in range(F_PLANES):
        place(fine.g, index + 1, index, 2.0)
    for index in range(F_PLANES, PLANES):
        place(fine.b, index - F_PLANES, index, 1.0)

    fine.clear(B_PLANES, ROWS, (0, B_PLANES - 1))
    fine.before(0, ROWS)

    @pl.loop(1, B_PLANES - 1, step=4)
    def _(plane):
        for index in range(4):
            fine.setup(plane + index, ROWS, index & 1)

    every = range(8, ROWS + 8, 8)
    inner = range(16, ROWS, 8)
    for step in range(3):
        beside = 2 - step
        near = B_HALO - beside

        count = (4, 3, 4)[step]

        @pl.loop(near, near + BLOCK + 2 * beside, step=count)
        def _(plane):
            fine.relax(step, plane, count, every)

        @pl.loop(near - 9, near, step=3)
        def _(plane):
            fine.relax(step, plane, 3, inner)
            fine.relax(step, plane + BLOCK + 2 * beside + 9, 3, inner)

    for plane in range(BLOCK):
        u0_ref[plane] = fine.k[0][plane + B_HALO, 8 + BLOCK : 8 + 2 * BLOCK]

    @pl.loop(0, 16)
    def _(index):
        for row in inner:
            held = {}
            first = fine.rest(2 * index + 5, row, 0, held)
            second = fine.rest(2 * index + 5, row, 1, held)
            at = pl.ds(pl.multiple_of(32 * index + (row - 16), 8), 8)
            rest_main[at, :] = first[0] + second[0]
            rest_side[at, :] = first[1] + second[1]

    @pl.loop(0, 18)
    def _(index):
        for row in every:
            at = pl.ds(pl.multiple_of(48 * index + (row - 8), 8), 8)
            first, second = 2 * index + 3, 2 * index + 4
            here = slice(row, row + 8)
            sum_main[at, :] = fine.b[0][first, here] + fine.b[0][second, here]
            sum_side[at, :] = fine.b[1][first, here] + fine.b[1][second, here]

    to_main = pair_selector(128, 0, 128, 0, 64)
    to_side = pair_selector(128, 0, 128, 64, 64)
    g_next = split_matmul(halves(rest_main, 256), to_main)
    g_next = 0.5 * (g_next + split_matmul(halves(rest_side, 256), to_side))
    b_next = split_matmul(halves(sum_main, 432), to_main)
    b_next = 0.125 * (b_next + split_matmul(halves(sum_side, 432), to_side))

    middle.clear(20, 24, (1, 18))
    zero = jnp.zeros((8, 128), F32)
    for plane in range(2, 18):
        middle.g[0][plane, 8:16] = zero
        middle.g[0][plane, 24:32] = zero
        middle.g[0][plane, 12:28] = g_next[16 * (plane - 2) : 16 * (plane - 1)]
    for plane in range(1, 19):
        middle.b[0][plane, 8:32] = b_next[24 * (plane - 1) : 24 * plane]
    middle.before(1, 24)

    @pl.loop(2, 18, step=4)
    def _(plane):
        for index in range(4):
            middle.setup(plane + index, 24, index & 1)

    for step in range(3):

        @pl.loop(2, 18, step=4)
        def _(plane):
            middle.relax(step, plane, 4, range(8, 32, 8))

    for plane in range(8):
        u1_ref[plane] = middle.k[0][plane + 6, 16:24]
    for index in range(4):
        (first,) = middle.rest(2 * index + 6, 16)
        (second,) = middle.rest(2 * index + 7, 16)
        collect[8 * index : 8 * index + 8] = 0.5 * (first + second)
    for index in range(6):
        first, second = middle.b[0][2 * index + 4, 16:24], middle.b[0][2 * index + 5, 16:24]
        collect[8 * index + 32 : 8 * index + 40] = 0.125 * (first + second)
    collect[80:128] = jnp.zeros((48, 128), F32)
    out = jnp.zeros((16, 128), F32)
    for part in range(4):
        rows = collect[pl.ds(2 * part, 16, stride=8), :]
        rows = rows + collect[pl.ds(2 * part + 1, 16, stride=8), :]
        out = out + split_matmul(rows, pair_selector(128, 0, 128, 32 * part, 32))
    coarse_ref[...] = out


def spread_kernel(low_ref, own_ref, high_ref, out_ref, rows):
    rows[0:4] = low_ref[0:4]
    rows[4:8] = own_ref[0:4]
    rows[8:12] = high_ref[0:4]
    rows[12:17] = low_ref[4:9]
    rows[17:21] = own_ref[5:9]
    rows[21:26] = high_ref[5:10]
    rows[26:32] = jnp.zeros((6, 128), F32)
    value = rows[...]
    for index in range(32):
        out_ref[index] = value


def slab_kernel(gathered_ref, u2_ref, coarse_ref, *scratch):
    slab = Level(scratch[: len(Level.names)], 1, True)
    rest, sums = scratch[len(Level.names) :]
    row = iota((4, 8, 128), 1)
    lane = iota((4, 8, 128), 2)
    group = lane >> 5
    turn = (group - row) & 3

    def exchange(value):
        value = value.reshape(4, 8, 128)
        out = value
        for d in (1, 2, 3):
            moved = pltpu.roll(value, 32 * d, 2)
            near = pltpu.roll(moved, 8 - d, 1)
            far = pltpu.roll(moved, 4 - d, 1)
            out = jnp.where(turn == d, jnp.where(group >= d, near, far), out)
        return out.reshape(32, 128)

    for plane in range(12):
        slab.g[0][plane + 1, 8:40] = exchange(gathered_ref[pl.ds(plane, 32, stride=32), :])
    for plane in range(14):
        slab.b[0][plane, 8:40] = exchange(gathered_ref[pl.ds(plane + 12, 32, stride=32), :])

    slab.clear(14, 32, (0, 13))
    slab.before(0, 32)

    @pl.loop(1, 13, step=4)
    def _(plane):
        for index in range(4):
            slab.setup(plane + index, 32, index & 1)

    for step in range(3):

        @pl.loop(2 + step, 12 - step, step=2)
        def _(plane):
            slab.relax(step, plane, 2, range(8, 40, 8))

    for plane in range(4):
        u2_ref[plane] = slab.k[0][plane + 5, 8:40]
    for part in range(2):
        for row in range(8, 40, 8):
            (first,) = slab.rest(5 + 2 * part, row)
            (second,) = slab.rest(6 + 2 * part, row)
            at = slice(32 * part + row - 8, 32 * part + row)
            rest[at] = 0.5 * (first + second)
            here = slice(row, row + 8)
            sums[at] = 0.125 * (slab.b[0][5 + 2 * part, here] + slab.b[0][6 + 2 * part, here])
    g_rows, b_rows = halves(rest, 32), halves(sums, 32)
    value = jnp.zeros((32, 128), F32)
    for part in range(2):
        own = slice(16 * part, 16 * part + 16)
        rows = jnp.concatenate([g_rows[own], b_rows[own]], axis=0)
        value = value + split_matmul(rows, pair_selector(128, 0, 128, 64 * part, 64))
    for index in range(16):
        coarse_ref[index] = value


def coarse_kernel(
    gathered_ref, u0_ref, u1_ref, u2_ref, out_ref,
    r3, rs, k3, ks, inner_3, outer_3, fy3, fz3, d3, ir3, ik3, b3, bs,
    r4, k4, fx4, fy4, fz4, ir4, ik4, g4, b4,
    pair_3, pair_4, twice_3, twice_2, twice_1, twice_0, level_1,
):
    at_x = lax.axis_index("gx")
    at_y = lax.axis_index("gy")
    at_z = lax.axis_index("gz")
    lane = iota((8, 128), 1)
    row8 = iota((8, 128), 0)
    zero = jnp.zeros((8, 128), F32)

    cell = lane & 63
    parity = ((lane >> 6) + row8 + cell) & 1
    first_half = lane < 64
    for ref in (r3, rs, k3, ks, b3, bs):
        for plane in (0, 17):
            ref[plane] = jnp.zeros((32, 128), F32)
    for plane in range(1, 17):
        for ref in (r3, k3, b3, fy3):
            ref[plane, 0:8] = zero
            ref[plane, 24:32] = zero
        for row in (8, 16):
            value = gathered_ref[plane - 1, row + 8 : row + 16]
            b3[plane, row : row + 8] = value
            bs[plane, row : row + 8] = pltpu.roll(value, 64, 1)

    def outer(ref, plane, here):
        return jnp.where(first_half, ref[plane - 1, here], ref[plane + 1, here])

    for plane in range(1, 17):
        for row in (8, 16):
            here = slice(row, row + 8)
            b = b3[plane, here]
            partner, other = bs[plane, here], outer(bs, plane, here)
            y_high = b3[plane, row + 1 : row + 9]
            z_low = jnp.where(cell > 0, pltpu.roll(b, 1, 1), 0.0)
            z_high = jnp.where(cell < 63, pltpu.roll(b, 127, 1), 0.0)
            total = (6.0 * b + (partner + other)) + (
                (b3[plane, row - 1 : row + 7] + y_high) + (z_low + z_high)
            )
            inside = b > 0.0
            inverse = 1.0 / jnp.where(inside, total, 1.0)
            reds = jnp.where(inside & (parity == 0), inverse, 0.0)
            inner_3[plane, here] = b + partner
            outer_3[plane, here] = b + other
            fy3[plane, here] = b + y_high
            fz3[plane, here] = jnp.where(cell < 63, b + z_high, 0.0)
            d3[plane, here] = total
            ir3[plane, here] = reds
            ik3[plane, here] = jnp.where(inside & (parity == 1), inverse, 0.0)
            value = gathered_ref[plane - 1, row - 8 : row] * reds
            r3[plane, here] = value
            rs[plane, here] = pltpu.roll(value, 64, 1)

    def total_3(ref, swapped, plane, row):
        here, low, high = slice(row, row + 8), slice(row - 1, row + 7), slice(row + 1, row + 9)
        v, face = ref[plane, here], fz3[plane, here]
        along_x = inner_3[plane, here] * swapped[plane, here]
        along_x = along_x + outer_3[plane, here] * outer(swapped, plane, here)
        along_y = fy3[plane, here] * ref[plane, high] + fy3[plane, low] * ref[plane, low]
        along_z = face * pltpu.roll(v, 127, 1) + pltpu.roll(face * v, 1, 1)
        return (gathered_ref[plane - 1, row - 8 : row] + along_x) + (along_y + along_z)

    for step in range(3):
        source, inverse, target = (
            ((r3, rs), ik3, (k3, ks)),
            ((k3, ks), ir3, (r3, rs)),
            ((r3, rs), ik3, (k3, ks)),
        )[step]
        for plane in range(1, 17):
            for row in (8, 16):
                here = slice(row, row + 8)
                value = total_3(*source, plane, row) * inverse[plane, here]
                if step == 2:
                    value = value + r3[plane, here]
                target[0][plane, here] = value
                target[1][plane, here] = pltpu.roll(value, 64, 1)

    for plane in range(1, 17):
        for row in (8, 16):
            here = slice(row, row + 8)
            value = total_3(k3, ks, plane, row) - d3[plane, here] * k3[plane, here]
            at = slice(16 * (plane - 1) + row - 8, 16 * (plane - 1) + row)
            pair_3[at] = value + pltpu.roll(value, 64, 1)
            pair_4[at] = b3[plane, here] + bs[plane, here]
    halve = pair_selector(128, 0, 128, 0, 32)
    g4[...] = 0.5 * split_matmul(halves(pair_3, 128), halve).reshape(16, 8, 128)
    b4[0] = zero
    b4[17] = zero
    b4[1:17] = 0.125 * split_matmul(halves(pair_4, 128), halve).reshape(16, 8, 128)

    parity = (row8 + lane) & 1
    for ref in (r4, k4):
        ref[0] = zero
        ref[17] = zero
    fx4[0] = b4[1]
    for plane in range(1, 17):
        b = b4[plane]
        x_high = b4[plane + 1]
        y_low = jnp.where(row8 > 0, pltpu.roll(b, 1, 0), 0.0)
        y_high = jnp.where(row8 < 7, pltpu.roll(b, 7, 0), 0.0)
        z_high = pltpu.roll(b, 127, 1)
        total = (6.0 * b + (b4[plane - 1] + x_high)) + (
            (y_low + y_high) + (pltpu.roll(b, 1, 1) + z_high)
        )
        inside = b > 0.0
        inverse = 1.0 / jnp.where(inside, total, 1.0)
        reds = jnp.where(inside & (parity == (plane - 1) & 1), inverse, 0.0)
        fx4[plane] = b + x_high
        fy4[plane] = jnp.where(row8 < 7, b + y_high, 0.0)
        fz4[plane] = jnp.where(lane < 31, b + z_high, 0.0)
        ir4[plane] = reds
        ik4[plane] = jnp.where(inside & (parity != (plane - 1) & 1), inverse, 0.0)
        r4[plane] = g4[plane - 1] * reds

    def half_4(source, inverse, target):
        for plane in range(1, 17):
            v = source[plane]
            face_y, face_z = fy4[plane], fz4[plane]
            along_x = fx4[plane] * source[plane + 1] + fx4[plane - 1] * source[plane - 1]
            along_y = face_y * pltpu.roll(v, 7, 0) + pltpu.roll(face_y * v, 1, 0)
            along_z = face_z * pltpu.roll(v, 127, 1) + pltpu.roll(face_z * v, 1, 1)
            value = (g4[plane - 1] + along_x) + (along_y + along_z)
            target[plane] = value * inverse[plane]

    half_4(r4, ik4, k4)

    @pl.loop(1, COARSE_SWEEPS)
    def _(sweep):
        half_4(k4, ir4, r4)
        half_4(r4, ik4, k4)

    source = iota((128, 128), 0)
    target = iota((128, 128), 1)
    spread = selector_of((source < 32) & (((target & 63) >> 1) == source))
    value = split_matmul(r4[at_x + 1] + k4[at_x + 1], spread)
    twice_3[pl.ds(0, 8, stride=2), :] = value
    twice_3[pl.ds(1, 8, stride=2), :] = value
    value = k3[at_x + 1, 8:24] + twice_3[...]
    value = pltpu.roll(value, lax.rem(16 - 2 * at_y, 16), 0)
    value = pltpu.roll(value, lax.rem(128 - 16 * at_z, 128), 1)
    level_2 = []
    for part in range(2):
        fine = split_matmul(value, spread_selector(64 * part, 0, 16))[0:8]
        twice_2[pl.ds(0, 8, stride=2), :] = fine
        twice_2[pl.ds(1, 8, stride=2), :] = fine
        for index in range(2):
            own = u2_ref[2 * part + index]
            own = pltpu.roll(own, lax.rem(32 - 4 * at_y, 32), 0)
            own = pltpu.roll(own, lax.rem(128 - 32 * at_z, 128), 1)
            level_2.append(own[0:8] + twice_2[0:8])
    fine = split_matmul(jnp.concatenate(level_2, axis=0), spread_selector(0, 0, 32))
    twice_1[pl.ds(0, 32, stride=2), :] = fine
    twice_1[pl.ds(1, 32, stride=2), :] = fine
    for index in range(8):
        start = 16 * (index // 2)
        level_1[8 * index : 8 * index + 8] = u1_ref[index] + twice_1[start : start + 8]
    fine = split_matmul(level_1[...], spread_selector(0, 0, 64))
    twice_0[pl.ds(0, 64, stride=2), :] = fine
    twice_0[pl.ds(1, 64, stride=2), :] = fine
    for index in range(16):
        start = 16 * (index // 2)
        out_ref[index] = u0_ref[index] + twice_0[start : start + 16]


def call(kernel, megabytes, outs, scratch, *operands):
    whole = pl.BlockSpec(memory_space=pltpu.VMEM)
    return pl.pallas_call(
        kernel,
        out_shape=[jax.ShapeDtypeStruct(shape, F32) for shape in outs],
        in_specs=[whole] * len(operands),
        out_specs=[whole] * len(outs),
        scratch_shapes=[pltpu.VMEM(shape, F32) for shape in scratch],
        compiler_params=pltpu.CompilerParams(vmem_limit_bytes=megabytes << 20),
    )(*operands)


def shift(value, axis, step):
    count = lax.axis_size(axis)
    pairs = [(i, i + step) for i in range(count) if 0 <= i + step < count]
    return lax.ppermute(value, axis, pairs)


def around(value, axis, step):
    count = lax.axis_size(axis)
    return lax.ppermute(value, axis, [(i, (i + step) % count) for i in range(count)])


def swap(value, axis, first):
    count = lax.axis_size(axis)
    lower = range(first, count - 1, 2)
    pairs = [(i, i + 1) for i in lower] + [(i + 1, i) for i in lower]
    return lax.ppermute(value, axis, pairs)


def on_device(right_side, conductivity):
    f, b = right_side, conductivity
    upper = jnp.concatenate([f[BLOCK - F_HALO :], b[BLOCK - B_HALO :]], axis=0)
    lower = jnp.concatenate([f[:F_HALO], b[:B_HALO]], axis=0)
    low, high = shift(upper, "gx", 1), shift(lower, "gx", -1)

    strip = (GROUPS, BLOCK, 128)
    packed = (PACKED, 128)
    main, left, right, down, up = call(
        pack_kernel, 4, [(PLANES, BLOCK, 128), strip, strip, packed, packed], [], f, b, low, high
    )
    first, second = swap(left, "gz", 0), swap(right, "gz", 1)
    down, up, after, before = call(
        join_kernel, 4, [(PAYLOAD, 128)] * 2 + [strip] * 2, [], down, up, first, second
    )
    low, high = around(up, "gy", 1), around(down, "gy", -1)

    u0, u1, coarse = call(
        fine_kernel,
        40,
        [(BLOCK, BLOCK, 128), (8, 8, 128), (16, 128)],
        Level.scratch(2, B_PLANES, ROWS)
        + Level.scratch(1, 20, 24)
        + [(512, 128)] * 2
        + [(864, 128)] * 2
        + [(128, 128)],
        low, high, main, after, before,
    )

    low, high = shift(coarse, "gx", 1), shift(coarse, "gx", -1)
    (slab,) = call(spread_kernel, 2, [(32, 32, 128)], [(32, 128)], low, coarse, high)
    slab = lax.all_to_all(slab, ("gy", "gz"), 0, 0, tiled=True)
    u2, coarse = call(
        slab_kernel,
        8,
        [(4, 32, 128), (16, 32, 128)],
        Level.scratch(1, 14, 32) + [(64, 128)] * 2,
        slab.reshape(1024, 128),
    )

    whole = lax.all_to_all(coarse, "gx", 0, 0, tiled=True)
    (out,) = call(
        coarse_kernel,
        8,
        [(BLOCK, BLOCK, 128)],
        [(18, 32, 128)] * 13
        + [(18, 8, 128)] * 7
        + [(16, 8, 128), (18, 8, 128)]
        + [(256, 128)] * 2
        + [(16, 128), (16, 128), (64, 128), (128, 128), (64, 128)],
        whole, u0, u1, u2,
    )
    return out


def solution(mesh):
    spec = P("gx", "gy", "gz")
    return jax.shard_map(
        on_device, mesh=mesh, in_specs=(spec, spec), out_specs=spec, check_vma=False
    )
```

```python
import jax
import jax.numpy as jnp
from jax import lax
from jax.experimental import pallas as pl
from jax.experimental.pallas import tpu as pltpu
from jax.sharding import PartitionSpec as P

F_HALO = 12
B_HALO = 13
BLOCK = 16
F_PLANES = BLOCK + 2 * F_HALO
B_PLANES = BLOCK + 2 * B_HALO
PLANES = F_PLANES + B_PLANES
GROUPS = -(-PLANES // 8)
F_GROUPS = F_PLANES // 8
ROWS = 48


def rows_of(index):
    if index < F_PLANES:
        return F_HALO - max(F_HALO - index, index - F_HALO - BLOCK + 1, 0)
    index -= F_PLANES
    return B_HALO - max(B_HALO - index, index - B_HALO - BLOCK + 1, 0)


COUNTS = [rows_of(index) for index in range(PLANES)]
OFFSETS = [sum(COUNTS[:index]) for index in range(PLANES)]
PACKED = sum(COUNTS)
STRIP_ROWS = [
    8 * -(-max(0, max(COUNTS[8 * group : 8 * group + 8]) - 1) // 8) for group in range(GROUPS)
]
STRIP_OFFSETS = [PACKED + sum(STRIP_ROWS[:group]) for group in range(GROUPS)]
SIDE = sum(STRIP_ROWS)
PAYLOAD = PACKED + 2 * SIDE
COARSE_SWEEPS = 8
F32 = jnp.float32


def iota(shape, dim):
    return lax.broadcasted_iota(jnp.int32, shape, dim)


def split_matmul(value, selector):
    high = value.astype(jnp.bfloat16)
    low = (value - high.astype(F32)).astype(jnp.bfloat16)
    return jnp.dot(high, selector, preferred_element_type=F32) + jnp.dot(
        low, selector, preferred_element_type=F32
    )


def selector_of(condition):
    return jnp.where(condition, 1.0, 0.0).astype(jnp.bfloat16)


def pair_selector(source_lanes, first, out_lanes, offset, count):
    source = iota((source_lanes, out_lanes), 0) - first
    target = iota((source_lanes, out_lanes), 1) - offset
    return selector_of(
        (source >= 0) & (source < 2 * count) & ((source >> 1) == target)
    )


def spread_selector(first, offset, count):
    source = iota((128, 128), 0) - first
    target = iota((128, 128), 1) - offset
    return selector_of((source >= 0) & (source < count) & ((target >> 1) == source))


class Level:
    names = ("b", "g", "fx", "fy", "fz", "d", "ir", "ik", "r", "k")

    def __init__(self, refs, columns, walled):
        self.walled = walled
        self.columns = columns
        for index, name in enumerate(self.names):
            setattr(self, name, refs[index * columns : (index + 1) * columns])
        self.lane = iota((8, 128), 1)
        self.parity = (iota((8, 128), 0) + self.lane) & 1

    @staticmethod
    def scratch(columns, planes, rows):
        return [(planes, rows + 16, 128)] * (len(Level.names) * columns)

    def low(self, row):
        return row - 1

    def high(self, row):
        return row + 1

    def at(self, refs, plane, row):
        return [ref[plane, row : row + 8] for ref in refs]

    def put(self, refs, plane, row, values):
        for ref, value in zip(refs, values):
            ref[plane, row : row + 8] = value

    def turn(self, values, step):
        rolled = [pltpu.roll(value, 127 if step > 0 else 1, 1) for value in values]
        if self.columns == 1:
            return rolled
        edge = self.lane == (127 if step > 0 else 0)
        first, second = rolled
        return [jnp.where(edge, second, first), jnp.where(edge, first, second)]

    def clear(self, planes, rows, ends):
        zero = jnp.zeros((8, 128), F32)

        @pl.loop(0, planes)
        def _(plane):
            for refs in (self.b, self.r, self.k):
                for ref in refs:
                    ref[plane, 0:8] = zero
                    ref[plane, rows + 8 : rows + 16] = zero
            for ref in self.fy:
                ref[plane, 0:8] = zero

        for refs in (self.r, self.k):
            for ref in refs:
                for plane in ends:
                    ref[plane] = jnp.zeros((rows + 16, 128), F32)

    def before(self, plane, rows):
        for row in rows:
            near = zip(self.at(self.b, plane, row), self.at(self.b, plane + 1, row))
            self.put(self.fx, plane, row, [own + other for own, other in near])

    def setup(self, plane, rows, red):
        for row in rows:
            b = self.at(self.b, plane, row)
            x_low, x_high = self.at(self.b, plane - 1, row), self.at(self.b, plane + 1, row)
            y_low, y_high = self.at(self.b, plane, self.low(row)), self.at(self.b, plane, self.high(row))
            z_low, z_high = self.turn(b, -1), self.turn(b, 1)
            g = self.at(self.g, plane, row)
            for column in range(self.columns):
                own, z_before, z_after = b[column], z_low[column], z_high[column]
                face = own + z_after
                if self.walled:
                    z_before = jnp.where(self.lane > 0, z_before, 0.0)
                    z_after = jnp.where(self.lane < 127, z_after, 0.0)
                    face = jnp.where(self.lane < 127, face, 0.0)
                total = (6.0 * own + (x_low[column] + x_high[column])) + (
                    (y_low[column] + y_high[column]) + (z_before + z_after)
                )
                inside = own > 0.0
                inverse = 1.0 / jnp.where(inside, total, 1.0)
                first = self.parity == red
                reds = jnp.where(inside & first, inverse, 0.0)
                here = (plane, slice(row, row + 8))
                self.fx[column][here] = own + x_high[column]
                self.fy[column][here] = own + y_high[column]
                self.fz[column][here] = face
                self.d[column][here] = total
                self.ir[column][here] = reds
                self.ik[column][here] = jnp.where(inside & ~first, inverse, 0.0)
                self.r[column][here] = g[column] * reds
                self.k[column][here] = jnp.zeros((8, 128), F32)

    def total(self, source, base, step, row, held=None):
        held = {} if held is None else held

        def load(ref, plane):
            key = (id(ref), plane)
            if key not in held:
                held[key] = ref[base + plane, row : row + 8]
            return held[key]

        v = [load(ref, step) for ref in source]
        face_z = [load(ref, step) for ref in self.fz]
        z_high = self.turn(v, 1)
        z_low = self.turn([face * value for face, value in zip(face_z, v)], -1)
        out = []
        for column in range(self.columns):
            ref, fx, fy = source[column], self.fx[column], self.fy[column]
            along_x = load(fx, step) * load(ref, step + 1) + load(fx, step - 1) * load(ref, step - 1)
            low = slice(self.low(row), self.low(row) + 8)
            high = slice(self.high(row), self.high(row) + 8)
            plane = base + step
            along_y = load(fy, step) * ref[plane, high] + fy[plane, low] * ref[plane, low]
            along_z = face_z[column] * z_high[column] + z_low[column]
            out.append((load(self.g[column], step) + along_x) + (along_y + along_z))
        return out

    def relax(self, step, base, count, rows):
        source, inverse, target = (
            (self.r, self.ik, self.k),
            (self.k, self.ir, self.r),
            (self.r, self.ik, self.k),
        )[step]
        for row in rows:
            held = {}
            for index in range(count):
                values = self.total(source, base, index, row, held)
                scale = self.at(inverse, base + index, row)
                values = [value * factor for value, factor in zip(values, scale)]
                if step == 2:
                    own = self.at(self.r, base + index, row)
                    values = [a + b for a, b in zip(values, own)]
                self.put(target, base + index, row, values)

    def rest(self, base, row, step=0, held=None):
        values = self.total(self.k, base, step, row, held)
        plane = base + step
        out = []
        for column, value in enumerate(values):
            here = (plane, slice(row, row + 8))
            value = value - self.d[column][here] * self.k[column][here]
            out.append(jnp.where(self.b[column][here] > 0.0, value, 0.0))
        return out


def halves(ref, rows):
    return ref[pl.ds(0, rows, stride=2), :] + ref[pl.ds(1, rows, stride=2), :]


def pack_kernel(
    f_ref, b_ref, low_ref, high_ref, main_ref, left_ref, right_ref, down_ref, up_ref
):
    lane = iota((BLOCK, 128), 1)
    even = lax.rem(lax.axis_index("gz"), 2) == 0

    def source(index):
        if index < F_HALO:
            return low_ref[index]
        if index < F_HALO + BLOCK:
            return f_ref[index - F_HALO]
        if index < F_PLANES:
            return high_ref[index - F_HALO - BLOCK]
        index -= F_PLANES
        if index < B_HALO:
            return low_ref[F_HALO + index]
        if index < B_HALO + BLOCK:
            return b_ref[index - B_HALO]
        return high_ref[F_HALO + index - B_HALO - BLOCK]

    for group in range(GROUPS):
        left = jnp.zeros((BLOCK, 128), F32)
        right = jnp.zeros((BLOCK, 128), F32)
        for slot in range(8):
            index = group * 8 + slot
            if index >= PLANES:
                break
            plane = source(index)
            main_ref[index] = plane
            count, start = COUNTS[index], OFFSETS[index]
            if count:
                down_ref[start : start + count] = plane[0:count]
                up_ref[start : start + count] = plane[BLOCK - count : BLOCK]
            turned = pltpu.roll(plane, 16 * slot, 1) if slot else plane
            left = jnp.where((lane >> 4) == slot, turned, left)
            right = jnp.where((lane >> 4) == ((slot - 1) & 7), turned, right)
        left_ref[group] = jnp.where(even, right, left)
        right_ref[group] = jnp.where(even, left, right)


def join_kernel(
    down_ref, up_ref, first_ref, second_ref, down_out, up_out, after_ref, before_ref
):
    even = lax.rem(lax.axis_index("gz"), 2) == 0
    for group in range(GROUPS):
        first, second = first_ref[group], second_ref[group]
        after_ref[group] = jnp.where(even, first, second)
        before_ref[group] = jnp.where(even, second, first)
    down_out[0:PACKED] = down_ref[...]
    up_out[0:PACKED] = up_ref[...]
    for side, strips in enumerate((after_ref, before_ref)):
        for group in range(GROUPS):
            count = STRIP_ROWS[group]
            start = STRIP_OFFSETS[group] + side * SIDE
            if count:
                down_out[start : start + count] = strips[group, 0:count]
                up_out[start : start + count] = strips[group, BLOCK - count : BLOCK]


def fine_kernel(
    low_ref, high_ref, main_ref, after_ref, before_ref, u0_ref, u1_ref, coarse_ref, *scratch
):
    count = len(Level.names)
    fine = Level(scratch[: 2 * count], 2, False)
    middle = Level(scratch[2 * count : 3 * count], 1, False)
    rest_main, rest_side, sum_main, sum_side, collect = scratch[3 * count :]

    blank = jnp.zeros((BLOCK, 128), F32)

    def unpack(after, before):
        even = ((iota(after.shape, 1) >> 4) & 1) == 0
        return jnp.where(even, after, before), jnp.where(even, before, after)

    at_y = lax.axis_index("gy")
    low_there = jnp.where(at_y > 0, 1.0, 0.0)
    high_there = jnp.where(at_y < lax.axis_size("gy") - 1, 1.0, 0.0)

    def place(target, plane, index, scale):
        low_scale, high_scale = low_there * scale, high_there * scale
        group, slot = index // 8, index % 8
        count, start = COUNTS[index], OFFSETS[index]
        main, side = target
        first, own, last = 8, 8 + BLOCK, 8 + 2 * BLOCK
        main[plane, first:own] = blank
        main[plane, last : last + BLOCK] = blank
        main[plane, own:last] = main_ref[index] * scale
        if count:
            main[plane, own - count : own] = low_ref[start : start + count] * low_scale
            main[plane, last : last + count] = high_ref[start : start + count] * high_scale

        def turned(pair, scale):
            value = pair[slot & 1]
            if slot:
                value = pltpu.roll(value, 128 - 16 * slot, 1)
            lane = iota(value.shape, 1)
            return jnp.where((lane < 16) | (lane >= 112), value, 0.0) * scale

        side[plane, own:last] = turned(unpack(after_ref[group], before_ref[group]), scale)
        rows = STRIP_ROWS[group]
        if rows < BLOCK:
            side[plane, first:own] = blank
            side[plane, last : last + BLOCK] = blank
        if rows:
            start = STRIP_OFFSETS[group]
            beyond = slice(start, start + rows), slice(start + SIDE, start + SIDE + rows)
            side[plane, own - rows : own] = turned(
                unpack(low_ref[beyond[0]], low_ref[beyond[1]]), low_scale
            )
            side[plane, last : last + rows] = turned(
                unpack(high_ref[beyond[0]], high_ref[beyond[1]]), high_scale
            )

    for index in range(F_PLANES):
        place(fine.g, index + 1, index, 2.0)
    for index in range(F_PLANES, PLANES):
        place(fine.b, index - F_PLANES, index, 1.0)

    fine.clear(B_PLANES, ROWS, (0, B_PLANES - 1))
    every = range(8, ROWS + 8, 8)
    fine.before(0, every)

    @pl.loop(1, B_PLANES - 1, step=4)
    def _(plane):
        for index in range(4):
            fine.setup(plane + index, every, index & 1)

    inner = range(16, ROWS, 8)
    for step in range(3):
        beside = 2 - step
        near = B_HALO - beside

        count = (4, 3, 4)[step]

        @pl.loop(near, near + BLOCK + 2 * beside, step=count)
        def _(plane):
            fine.relax(step, plane, count, every)

        @pl.loop(near - 9, near, step=3)
        def _(plane):
            fine.relax(step, plane, 3, inner)
            fine.relax(step, plane + BLOCK + 2 * beside + 9, 3, inner)

    for plane in range(BLOCK):
        u0_ref[plane] = fine.k[0][plane + B_HALO, 8 + BLOCK : 8 + 2 * BLOCK]

    @pl.loop(0, 16)
    def _(index):
        for row in inner:
            held = {}
            first = fine.rest(2 * index + 5, row, 0, held)
            second = fine.rest(2 * index + 5, row, 1, held)
            at = pl.ds(pl.multiple_of(32 * index + (row - 16), 8), 8)
            rest_main[at, :] = first[0] + second[0]
            rest_side[at, :] = first[1] + second[1]

    @pl.loop(0, 18)
    def _(index):
        for row in every:
            at = pl.ds(pl.multiple_of(48 * index + (row - 8), 8), 8)
            first, second = 2 * index + 3, 2 * index + 4
            here = slice(row, row + 8)
            sum_main[at, :] = fine.b[0][first, here] + fine.b[0][second, here]
            sum_side[at, :] = fine.b[1][first, here] + fine.b[1][second, here]

    to_main = pair_selector(128, 0, 128, 0, 64)
    to_side = pair_selector(128, 0, 128, 64, 64)
    g_next = split_matmul(halves(rest_main, 256), to_main)
    g_next = 0.5 * (g_next + split_matmul(halves(rest_side, 256), to_side))
    b_next = split_matmul(halves(sum_main, 432), to_main)
    b_next = 0.125 * (b_next + split_matmul(halves(sum_side, 432), to_side))

    middle.clear(20, 24, (1, 18))
    zero = jnp.zeros((8, 128), F32)
    for plane in range(2, 18):
        middle.g[0][plane, 8:16] = zero
        middle.g[0][plane, 24:32] = zero
        middle.g[0][plane, 12:28] = g_next[16 * (plane - 2) : 16 * (plane - 1)]
    for plane in range(1, 19):
        middle.b[0][plane, 8:32] = b_next[24 * (plane - 1) : 24 * plane]
    middle.before(1, range(8, 32, 8))

    @pl.loop(2, 18, step=4)
    def _(plane):
        for index in range(4):
            middle.setup(plane + index, range(8, 32, 8), index & 1)

    for step in range(3):

        @pl.loop(2, 18, step=4)
        def _(plane):
            middle.relax(step, plane, 4, range(8, 32, 8))

    for plane in range(8):
        u1_ref[plane] = middle.k[0][plane + 6, 16:24]
    for index in range(4):
        at = 32 * index
        (first,) = middle.rest(2 * index + 6, 16)
        (second,) = middle.rest(2 * index + 7, 16)
        collect[at : at + 8] = 0.5 * (first + second)
        first, second = middle.b[0][2 * index + 6, 14:26], middle.b[0][2 * index + 7, 14:26]
        collect[at + 8 : at + 20] = 0.125 * (first + second)
        collect[at + 20 : at + 32] = jnp.zeros((12, 128), F32)
    out = jnp.zeros((16, 128), F32)
    for index in range(4):
        rows = collect[pl.ds(32 * index, 16, stride=2), :]
        rows = rows + collect[pl.ds(32 * index + 1, 16, stride=2), :]
        out = out + split_matmul(rows, pair_selector(128, 0, 128, 32 * index, 32))
    for index in range(16):
        coarse_ref[index] = out


def squeeze_kernel(gathered_ref, out_ref):
    for row in range(10):
        value = gathered_ref[pl.ds(row, 16, stride=16), :]
        for index in range(4):
            out_ref[index, 16 * row : 16 * row + 16] = value


def line_kernel(gathered_ref, out_ref):
    group = iota((16, 128), 1) >> 5
    for row in range(10):
        here = slice(16 * row, 16 * row + 16)
        pieces = [gathered_ref[position, here] for position in range(4)]
        for part in range(4):
            value = pieces[part]
            for position in range(4):
                if position != part:
                    moved = pltpu.roll(pieces[position], (32 * (position - part)) % 128, 1)
                    value = jnp.where(group == position, moved, value)
            start = 64 * row + 16 * part
            out_ref[start : start + 16] = value


class Blocks(Level):
    starts = tuple(32 * block + 8 for block in range(4))

    def __init__(self, refs):
        super().__init__(refs, 1, True)
        self.parity = self.lane & 1

    def low(self, row):
        return row - 32 if row >= self.starts[1] else row + 95

    def high(self, row):
        return row + 32 if row < self.starts[3] else row - 95


def column_kernel(low_ref, own_ref, high_ref, u2_ref, coarse_ref, *scratch):
    column = Blocks(scratch)
    at_y = lax.axis_index("gy")
    low_there = jnp.where(at_y > 0, 1.0, 0.0)
    high_there = jnp.where(at_y < lax.axis_size("gy") - 1, 1.0, 0.0)
    (b,), (g,) = column.b, column.g

    def put(target, plane, source, index, scale=None):
        for block, start in enumerate(column.starts):
            at = 64 * index + 16 * block
            value = source[at : at + 16]
            if scale is not None:
                value = value * scale
            target[plane, start : start + 16] = value

    for index in range(4):
        put(g, 1 + index, low_ref, index, low_there)
        put(g, 5 + index, own_ref, index)
        put(g, 9 + index, high_ref, index, high_there)
        put(b, 5 + index, own_ref, 5 + index)
    for index in range(5):
        put(b, index, low_ref, 4 + index, low_there)
        put(b, 9 + index, high_ref, 5 + index, high_there)

    zero = jnp.zeros((8, 128), F32)
    for refs in (column.b, column.fy, column.r, column.k):
        for plane in range(14):
            refs[0][plane, 24:32] = zero
            refs[0][plane, 96:104] = zero
    halves_of = [range(start, start + 16, 8) for start in column.starts]
    rows = [row for half in halves_of for row in half]
    for refs in (column.r, column.k):
        for plane in (0, 13):
            for row in rows:
                refs[0][plane, row : row + 8] = zero
    column.before(0, rows)

    @pl.loop(1, 13, step=2)
    def _(plane):
        for index in range(2):
            for block, half in enumerate(halves_of):
                column.setup(plane + index, half, (index + block) & 1)

    for step in range(3):

        @pl.loop(2 + step, 12 - step, step=2)
        def _(plane):
            column.relax(step, plane, 2, rows)

    at_x = lax.axis_index("gx")
    for index, start in enumerate(column.starts):
        for plane in range(4):
            u2_ref[index, plane : plane + 1] = column.k[0][plane + 5, pl.ds(start + at_x, 1), :]
        u2_ref[index, 4:8] = jnp.zeros((4, 128), F32)

    halve = [pair_selector(128, 0, 128, 64 * part, 64) for part in range(2)]
    g_out, b_out = [], []
    for plane in (5, 7):
        g_value = jnp.zeros((16, 128), F32)
        b_value = jnp.zeros((16, 128), F32)
        for part in range(2):
            g_parts, b_parts = [], []
            for offset in (0, 8):
                g_sum = b_sum = None
                for block in (2 * part, 2 * part + 1):
                    row = column.starts[block] + offset
                    for step in range(2):
                        (value,) = column.rest(plane, row, step)
                        weight = b[plane + step, row : row + 8]
                        g_sum = value if g_sum is None else g_sum + value
                        b_sum = weight if b_sum is None else b_sum + weight
                g_parts.append(0.5 * g_sum)
                b_parts.append(0.125 * b_sum)
            g_value = g_value + split_matmul(jnp.concatenate(g_parts, axis=0), halve[part])
            b_value = b_value + split_matmul(jnp.concatenate(b_parts, axis=0), halve[part])
        g_out.append(g_value)
        b_out.append(b_value)
    for index in range(8):
        for part, value in enumerate(g_out + b_out):
            coarse_ref[index, 16 * part : 16 * part + 16] = value


def coarse_kernel(
    gathered_ref, u0_ref, u1_ref, u2_ref, out_ref,
    r3, rs, k3, ks, inner_3, outer_3, fy3, fz3, d3, ir3, ik3, b3, bs,
    r4, k4, fx4, fy4, fz4, ir4, ik4, g4, b4,
    g_rows, b_rows, pair_3, pair_4, twice_3, twice_2, twice_1, twice_0, level_1,
):
    at_x = lax.axis_index("gx")
    at_y = lax.axis_index("gy")
    at_z = lax.axis_index("gz")
    lane = iota((8, 128), 1)
    row8 = iota((8, 128), 0)
    zero = jnp.zeros((8, 128), F32)

    cell = lane & 63
    parity = ((lane >> 6) + row8 + cell) & 1
    first_half = lane < 64
    for index in range(8):
        for part in range(2):
            rows = pl.ds(2 * index + part, 16, stride=16)
            g_rows[rows, :] = gathered_ref[index, 16 * part : 16 * part + 16]
            b_rows[rows, :] = gathered_ref[index, 16 * part + 32 : 16 * part + 48]
    for ref in (r3, rs, k3, ks, b3, bs):
        for plane in (0, 17):
            ref[plane] = jnp.zeros((32, 128), F32)
    for plane in range(1, 17):
        for ref in (r3, k3, b3, fy3):
            ref[plane, 0:8] = zero
            ref[plane, 24:32] = zero
        for row in (8, 16):
            value = b_rows[16 * plane + row - 24 : 16 * plane + row - 16]
            b3[plane, row : row + 8] = value
            bs[plane, row : row + 8] = pltpu.roll(value, 64, 1)

    def outer(ref, plane, here):
        return jnp.where(first_half, ref[plane - 1, here], ref[plane + 1, here])

    for plane in range(1, 17):
        for row in (8, 16):
            here = slice(row, row + 8)
            b = b3[plane, here]
            partner, other = bs[plane, here], outer(bs, plane, here)
            y_high = b3[plane, row + 1 : row + 9]
            z_low = jnp.where(cell > 0, pltpu.roll(b, 1, 1), 0.0)
            z_high = jnp.where(cell < 63, pltpu.roll(b, 127, 1), 0.0)
            total = (6.0 * b + (partner + other)) + (
                (b3[plane, row - 1 : row + 7] + y_high) + (z_low + z_high)
            )
            inside = b > 0.0
            inverse = 1.0 / jnp.where(inside, total, 1.0)
            reds = jnp.where(inside & (parity == 0), inverse, 0.0)
            inner_3[plane, here] = b + partner
            outer_3[plane, here] = b + other
            fy3[plane, here] = b + y_high
            fz3[plane, here] = jnp.where(cell < 63, b + z_high, 0.0)
            d3[plane, here] = total
            ir3[plane, here] = reds
            ik3[plane, here] = jnp.where(inside & (parity == 1), inverse, 0.0)
            value = g_rows[16 * plane + row - 24 : 16 * plane + row - 16] * reds
            r3[plane, here] = value
            rs[plane, here] = pltpu.roll(value, 64, 1)

    def total_3(ref, swapped, plane, row):
        here, low, high = slice(row, row + 8), slice(row - 1, row + 7), slice(row + 1, row + 9)
        v, face = ref[plane, here], fz3[plane, here]
        along_x = inner_3[plane, here] * swapped[plane, here]
        along_x = along_x + outer_3[plane, here] * outer(swapped, plane, here)
        along_y = fy3[plane, here] * ref[plane, high] + fy3[plane, low] * ref[plane, low]
        along_z = face * pltpu.roll(v, 127, 1) + pltpu.roll(face * v, 1, 1)
        g = g_rows[16 * plane + row - 24 : 16 * plane + row - 16]
        return (g + along_x) + (along_y + along_z)

    for step in range(3):
        source, inverse, target = (
            ((r3, rs), ik3, (k3, ks)),
            ((k3, ks), ir3, (r3, rs)),
            ((r3, rs), ik3, (k3, ks)),
        )[step]
        for plane in range(1, 17):
            for row in (8, 16):
                here = slice(row, row + 8)
                value = total_3(*source, plane, row) * inverse[plane, here]
                if step == 2:
                    value = value + r3[plane, here]
                target[0][plane, here] = value
                target[1][plane, here] = pltpu.roll(value, 64, 1)

    for plane in range(1, 17):
        for row in (8, 16):
            here = slice(row, row + 8)
            value = total_3(k3, ks, plane, row) - d3[plane, here] * k3[plane, here]
            at = slice(16 * (plane - 1) + row - 8, 16 * (plane - 1) + row)
            pair_3[at] = value + pltpu.roll(value, 64, 1)
            pair_4[at] = b3[plane, here] + bs[plane, here]
    halve = pair_selector(128, 0, 128, 0, 32)
    g4[...] = 0.5 * split_matmul(halves(pair_3, 128), halve).reshape(16, 8, 128)
    b4[0] = zero
    b4[17] = zero
    b4[1:17] = 0.125 * split_matmul(halves(pair_4, 128), halve).reshape(16, 8, 128)

    parity = (row8 + lane) & 1
    for ref in (r4, k4):
        ref[0] = zero
        ref[17] = zero
    fx4[0] = b4[1]
    for plane in range(1, 17):
        b = b4[plane]
        x_high = b4[plane + 1]
        y_low = jnp.where(row8 > 0, pltpu.roll(b, 1, 0), 0.0)
        y_high = jnp.where(row8 < 7, pltpu.roll(b, 7, 0), 0.0)
        z_high = pltpu.roll(b, 127, 1)
        total = (6.0 * b + (b4[plane - 1] + x_high)) + (
            (y_low + y_high) + (pltpu.roll(b, 1, 1) + z_high)
        )
        inside = b > 0.0
        inverse = 1.0 / jnp.where(inside, total, 1.0)
        reds = jnp.where(inside & (parity == (plane - 1) & 1), inverse, 0.0)
        fx4[plane] = b + x_high
        fy4[plane] = jnp.where(row8 < 7, b + y_high, 0.0)
        fz4[plane] = jnp.where(lane < 31, b + z_high, 0.0)
        ir4[plane] = reds
        ik4[plane] = jnp.where(inside & (parity != (plane - 1) & 1), inverse, 0.0)
        r4[plane] = g4[plane - 1] * reds

    def half_4(source, inverse, target):
        for plane in range(1, 17):
            v = source[plane]
            face_y, face_z = fy4[plane], fz4[plane]
            along_x = fx4[plane] * source[plane + 1] + fx4[plane - 1] * source[plane - 1]
            along_y = face_y * pltpu.roll(v, 7, 0) + pltpu.roll(face_y * v, 1, 0)
            along_z = face_z * pltpu.roll(v, 127, 1) + pltpu.roll(face_z * v, 1, 1)
            value = (g4[plane - 1] + along_x) + (along_y + along_z)
            target[plane] = value * inverse[plane]

    half_4(r4, ik4, k4)

    @pl.loop(1, COARSE_SWEEPS)
    def _(sweep):
        half_4(k4, ir4, r4)
        half_4(r4, ik4, k4)

    source = iota((128, 128), 0)
    target = iota((128, 128), 1)
    spread = selector_of((source < 32) & (((target & 63) >> 1) == source))
    value = split_matmul(r4[at_x + 1] + k4[at_x + 1], spread)
    twice_3[pl.ds(0, 8, stride=2), :] = value
    twice_3[pl.ds(1, 8, stride=2), :] = value
    value = k3[at_x + 1, 8:24] + twice_3[...]
    value = pltpu.roll(value, lax.rem(16 - 2 * at_y, 16), 0)
    value = pltpu.roll(value, lax.rem(128 - 16 * at_z, 128), 1)
    level_2 = []
    for part in range(2):
        fine = split_matmul(value, spread_selector(64 * part, 0, 16))[0:8]
        twice_2[pl.ds(0, 8, stride=2), :] = fine
        twice_2[pl.ds(1, 8, stride=2), :] = fine
        for index in range(2):
            own = u2_ref[2 * part + index]
            own = pltpu.roll(own, lax.rem(128 - 32 * at_z, 128), 1)
            level_2.append(own + twice_2[0:8])
    fine = split_matmul(jnp.concatenate(level_2, axis=0), spread_selector(0, 0, 32))
    twice_1[pl.ds(0, 32, stride=2), :] = fine
    twice_1[pl.ds(1, 32, stride=2), :] = fine
    for index in range(8):
        start = 16 * (index // 2)
        level_1[8 * index : 8 * index + 8] = u1_ref[index] + twice_1[start : start + 8]
    fine = split_matmul(level_1[...], spread_selector(0, 0, 64))
    twice_0[pl.ds(0, 64, stride=2), :] = fine
    twice_0[pl.ds(1, 64, stride=2), :] = fine
    for index in range(16):
        start = 16 * (index // 2)
        out_ref[index] = u0_ref[index] + twice_0[start : start + 16]


def call(kernel, megabytes, outs, scratch, *operands):
    whole = pl.BlockSpec(memory_space=pltpu.VMEM)
    return pl.pallas_call(
        kernel,
        out_shape=[jax.ShapeDtypeStruct(shape, F32) for shape in outs],
        in_specs=[whole] * len(operands),
        out_specs=[whole] * len(outs),
        scratch_shapes=[pltpu.VMEM(shape, F32) for shape in scratch],
        compiler_params=pltpu.CompilerParams(vmem_limit_bytes=megabytes << 20),
    )(*operands)


def shift(value, axis, step):
    count = lax.axis_size(axis)
    pairs = [(i, i + step) for i in range(count) if 0 <= i + step < count]
    return lax.ppermute(value, axis, pairs)


def around(value, axis, step):
    count = lax.axis_size(axis)
    return lax.ppermute(value, axis, [(i, (i + step) % count) for i in range(count)])


def swap(value, axis, first):
    count = lax.axis_size(axis)
    lower = range(first, count - 1, 2)
    pairs = [(i, i + 1) for i in lower] + [(i + 1, i) for i in lower]
    return lax.ppermute(value, axis, pairs)


def on_device(right_side, conductivity):
    f, b = right_side, conductivity
    upper = jnp.concatenate([f[BLOCK - F_HALO :], b[BLOCK - B_HALO :]], axis=0)
    lower = jnp.concatenate([f[:F_HALO], b[:B_HALO]], axis=0)
    low, high = shift(upper, "gx", 1), shift(lower, "gx", -1)

    strip = (GROUPS, BLOCK, 128)
    packed = (PACKED, 128)
    main, left, right, down, up = call(
        pack_kernel, 4, [(PLANES, BLOCK, 128), strip, strip, packed, packed], [], f, b, low, high
    )
    first, second = swap(left, "gz", 0), swap(right, "gz", 1)
    down, up, after, before = call(
        join_kernel, 4, [(PAYLOAD, 128)] * 2 + [strip] * 2, [], down, up, first, second
    )
    low, high = around(up, "gy", 1), around(down, "gy", -1)

    u0, u1, coarse = call(
        fine_kernel,
        40,
        [(BLOCK, BLOCK, 128), (8, 8, 128), (16, 16, 128)],
        Level.scratch(2, B_PLANES, ROWS)
        + Level.scratch(1, 20, 24)
        + [(512, 128)] * 2
        + [(864, 128)] * 2
        + [(128, 128)],
        low, high, main, after, before,
    )

    column = lax.all_to_all(coarse, "gx", 0, 0, tiled=True)
    (column,) = call(squeeze_kernel, 2, [(4, 160, 128)], [], column.reshape(256, 128))
    column = lax.all_to_all(column, "gz", 0, 0, tiled=True)
    (column,) = call(line_kernel, 2, [(640, 128)], [], column)
    low, high = around(column, "gy", 1), around(column, "gy", -1)
    u2, coarse = call(
        column_kernel,
        13,
        [(4, 8, 128), (8, 64, 128)],
        Level.scratch(1, 14, 112),
        low, column, high,
    )

    whole = lax.all_to_all(coarse, "gy", 0, 0, tiled=True)
    (out,) = call(
        coarse_kernel,
        8,
        [(BLOCK, BLOCK, 128)],
        [(18, 32, 128)] * 13
        + [(18, 8, 128)] * 7
        + [(16, 8, 128), (18, 8, 128)]
        + [(256, 128)] * 4
        + [(16, 128), (16, 128), (64, 128), (128, 128), (64, 128)],
        whole, u0, u1, u2,
    )
    return out


def solution(mesh):
    spec = P("gx", "gy", "gz")
    return jax.shard_map(
        on_device, mesh=mesh, in_specs=(spec, spec), out_specs=spec, check_vma=False
    )
```

```python
import jax
import jax.numpy as jnp
from jax import lax
from jax.experimental import pallas as pl
from jax.experimental.pallas import tpu as pltpu
from jax.sharding import PartitionSpec as P

F_HALO = 12
B_HALO = 13
BLOCK = 16
F_PLANES = BLOCK + 2 * F_HALO
B_PLANES = BLOCK + 2 * B_HALO
PLANES = F_PLANES + B_PLANES
GROUPS = -(-PLANES // 8)
F_GROUPS = F_PLANES // 8
ROWS = 48


def rows_of(index):
    if index < F_PLANES:
        return F_HALO - max(F_HALO - index, index - F_HALO - BLOCK + 1, 0)
    index -= F_PLANES
    return B_HALO - max(B_HALO - index, index - B_HALO - BLOCK + 1, 0)


COUNTS = [rows_of(index) for index in range(PLANES)]
OFFSETS = [sum(COUNTS[:index]) for index in range(PLANES)]
PACKED = sum(COUNTS)
STRIP_ROWS = [
    8 * -(-max(0, max(COUNTS[8 * group : 8 * group + 8]) - 1) // 8) for group in range(GROUPS)
]
STRIP_OFFSETS = [PACKED + sum(STRIP_ROWS[:group]) for group in range(GROUPS)]
SIDE = sum(STRIP_ROWS)
PAYLOAD = PACKED + 2 * SIDE
COARSE_SWEEPS = 8
F32 = jnp.float32


def iota(shape, dim):
    return lax.broadcasted_iota(jnp.int32, shape, dim)


def split_matmul(value, selector):
    high = value.astype(jnp.bfloat16)
    low = (value - high.astype(F32)).astype(jnp.bfloat16)
    return jnp.dot(high, selector, preferred_element_type=F32) + jnp.dot(
        low, selector, preferred_element_type=F32
    )


def selector_of(condition):
    return jnp.where(condition, 1.0, 0.0).astype(jnp.bfloat16)


def pair_selector(source_lanes, first, out_lanes, offset, count):
    source = iota((source_lanes, out_lanes), 0) - first
    target = iota((source_lanes, out_lanes), 1) - offset
    return selector_of(
        (source >= 0) & (source < 2 * count) & ((source >> 1) == target)
    )


def spread_selector(first, offset, count):
    source = iota((128, 128), 0) - first
    target = iota((128, 128), 1) - offset
    return selector_of((source >= 0) & (source < count) & ((target >> 1) == source))


class Level:
    names = ("b", "g", "fx", "fy", "fz", "d", "ir", "ik", "r", "k")

    def __init__(self, refs, columns, walled):
        self.walled = walled
        self.columns = columns
        for index, name in enumerate(self.names):
            setattr(self, name, refs[index * columns : (index + 1) * columns])
        self.lane = iota((8, 128), 1)
        self.parity = (iota((8, 128), 0) + self.lane) & 1

    @staticmethod
    def scratch(columns, planes, rows):
        return [(planes, rows + 16, 128)] * (len(Level.names) * columns)

    def low(self, row):
        return row - 1

    def high(self, row):
        return row + 1

    def at(self, refs, plane, row):
        return [ref[plane, row : row + 8] for ref in refs]

    def put(self, refs, plane, row, values):
        for ref, value in zip(refs, values):
            ref[plane, row : row + 8] = value

    def turn(self, values, step):
        rolled = [pltpu.roll(value, 127 if step > 0 else 1, 1) for value in values]
        if self.columns == 1:
            return rolled
        edge = self.lane == (127 if step > 0 else 0)
        first, second = rolled
        return [jnp.where(edge, second, first), jnp.where(edge, first, second)]

    def clear(self, planes, rows, ends):
        zero = jnp.zeros((8, 128), F32)

        @pl.loop(0, planes)
        def _(plane):
            for refs in (self.b, self.r, self.k):
                for ref in refs:
                    ref[plane, 0:8] = zero
                    ref[plane, rows + 8 : rows + 16] = zero
            for ref in self.fy:
                ref[plane, 0:8] = zero

        for refs in (self.r, self.k):
            for ref in refs:
                for plane in ends:
                    ref[plane] = jnp.zeros((rows + 16, 128), F32)

    def before(self, plane, rows):
        for row in rows:
            near = zip(self.at(self.b, plane, row), self.at(self.b, plane + 1, row))
            self.put(self.fx, plane, row, [own + other for own, other in near])

    def setup(self, plane, rows, red):
        for row in rows:
            b = self.at(self.b, plane, row)
            x_low, x_high = self.at(self.b, plane - 1, row), self.at(self.b, plane + 1, row)
            y_low, y_high = self.at(self.b, plane, self.low(row)), self.at(self.b, plane, self.high(row))
            z_low, z_high = self.turn(b, -1), self.turn(b, 1)
            g = self.at(self.g, plane, row)
            for column in range(self.columns):
                own, z_before, z_after = b[column], z_low[column], z_high[column]
                face = own + z_after
                if self.walled:
                    z_before = jnp.where(self.lane > 0, z_before, 0.0)
                    z_after = jnp.where(self.lane < 127, z_after, 0.0)
                    face = jnp.where(self.lane < 127, face, 0.0)
                total = (6.0 * own + (x_low[column] + x_high[column])) + (
                    (y_low[column] + y_high[column]) + (z_before + z_after)
                )
                inside = own > 0.0
                inverse = 1.0 / jnp.where(inside, total, 1.0)
                first = self.parity == red
                reds = jnp.where(inside & first, inverse, 0.0)
                here = (plane, slice(row, row + 8))
                self.fx[column][here] = own + x_high[column]
                self.fy[column][here] = own + y_high[column]
                self.fz[column][here] = face
                self.d[column][here] = total
                self.ir[column][here] = reds
                self.ik[column][here] = jnp.where(inside & ~first, inverse, 0.0)
                self.r[column][here] = g[column] * reds
                self.k[column][here] = jnp.zeros((8, 128), F32)

    def load(self, ref, base, step, row, held):
        key = (id(ref), id(base), step)
        if key not in held:
            held[key] = ref[base + step, row : row + 8]
        return held[key]

    def along_z(self, source, places, row, held):
        fields, scaled = [], []
        for base, step in places:
            v = [self.load(ref, base, step, row, held) for ref in source]
            face = [self.load(ref, base, step, row, held) for ref in self.fz]
            fields.append((v, face))
            scaled.append([a * b for a, b in zip(face, v)])
        v_sum, w_sum = fields[0][0], scaled[0]
        for (v, _), w in zip(fields[1:], scaled[1:]):
            v_sum = [a + b for a, b in zip(v_sum, v)]
            w_sum = [a + b for a, b in zip(w_sum, w)]
        high, low = self.turn(v_sum, 1), self.turn(w_sum, -1)
        return [[f * h + l for f, h, l in zip(face, high, low)] for _, face in fields]

    def total(self, source, base, step, row, held, along_z):
        out = []
        for column in range(self.columns):
            ref, fx, fy = source[column], self.fx[column], self.fy[column]
            along_x = self.load(fx, base, step, row, held) * self.load(
                ref, base, step + 1, row, held
            ) + self.load(fx, base, step - 1, row, held) * self.load(
                ref, base, step - 1, row, held
            )
            low = slice(self.low(row), self.low(row) + 8)
            high = slice(self.high(row), self.high(row) + 8)
            plane = base + step
            along_y = (
                self.load(fy, base, step, row, held) * ref[plane, high]
                + fy[plane, low] * ref[plane, low]
            )
            g = self.load(self.g[column], base, step, row, held)
            out.append((g + along_x) + (along_y + along_z[column]))
        return out

    def relax(self, step, pairs, rows):
        source, inverse, target = (
            (self.r, self.ik, self.k),
            (self.k, self.ir, self.r),
            (self.r, self.ik, self.k),
        )[step]
        for row in rows:
            held = {}
            for places in pairs:
                sums = self.along_z(source, places, row, held)
                for (base, index), along_z in zip(places, sums):
                    values = self.total(source, base, index, row, held, along_z)
                    scale = self.at(inverse, base + index, row)
                    values = [value * factor for value, factor in zip(values, scale)]
                    if step == 2:
                        own = self.at(self.r, base + index, row)
                        values = [a + b for a, b in zip(values, own)]
                    self.put(target, base + index, row, values)

    @staticmethod
    def adjacent(base, count):
        return [((base, index), (base, index + 1)) for index in range(0, count, 2)]

    def rest(self, base, row, step=0, held=None):
        held = {} if held is None else held
        (along_z,) = self.along_z(self.k, ((base, step),), row, held)
        values = self.total(self.k, base, step, row, held, along_z)
        plane = base + step
        out = []
        for column, value in enumerate(values):
            here = (plane, slice(row, row + 8))
            value = value - self.d[column][here] * self.k[column][here]
            out.append(jnp.where(self.b[column][here] > 0.0, value, 0.0))
        return out


def halves(ref, rows):
    return ref[pl.ds(0, rows, stride=2), :] + ref[pl.ds(1, rows, stride=2), :]


def edge_kernel(f_ref, b_ref, upper_ref, lower_ref):
    upper_ref[0:F_HALO] = f_ref[BLOCK - F_HALO : BLOCK]
    upper_ref[F_HALO:] = b_ref[BLOCK - B_HALO : BLOCK]
    lower_ref[0:F_HALO] = f_ref[0:F_HALO]
    lower_ref[F_HALO:] = b_ref[0:B_HALO]


def pack_kernel(
    f_ref, b_ref, low_ref, high_ref, main_ref, left_ref, right_ref, down_ref, up_ref
):
    lane = iota((BLOCK, 128), 1)
    even = lax.rem(lax.axis_index("gz"), 2) == 0

    def source(index):
        if index < F_HALO:
            return low_ref[index]
        if index < F_HALO + BLOCK:
            return f_ref[index - F_HALO]
        if index < F_PLANES:
            return high_ref[index - F_HALO - BLOCK]
        index -= F_PLANES
        if index < B_HALO:
            return low_ref[F_HALO + index]
        if index < B_HALO + BLOCK:
            return b_ref[index - B_HALO]
        return high_ref[F_HALO + index - B_HALO - BLOCK]

    for group in range(GROUPS):
        left = jnp.zeros((BLOCK, 128), F32)
        right = jnp.zeros((BLOCK, 128), F32)
        for slot in range(8):
            index = group * 8 + slot
            if index >= PLANES:
                break
            plane = source(index)
            main_ref[index] = plane
            count, start = COUNTS[index], OFFSETS[index]
            if count:
                down_ref[start : start + count] = plane[0:count]
                up_ref[start : start + count] = plane[BLOCK - count : BLOCK]
            turned = pltpu.roll(plane, 16 * slot, 1) if slot else plane
            left = jnp.where((lane >> 4) == slot, turned, left)
            right = jnp.where((lane >> 4) == ((slot - 1) & 7), turned, right)
        left_ref[group] = jnp.where(even, right, left)
        right_ref[group] = jnp.where(even, left, right)


def join_kernel(
    down_ref, up_ref, first_ref, second_ref, down_out, up_out, after_ref, before_ref
):
    even = lax.rem(lax.axis_index("gz"), 2) == 0
    for group in range(GROUPS):
        first, second = first_ref[group], second_ref[group]
        after_ref[group] = jnp.where(even, first, second)
        before_ref[group] = jnp.where(even, second, first)
    down_out[0:PACKED] = down_ref[...]
    up_out[0:PACKED] = up_ref[...]
    for side, strips in enumerate((after_ref, before_ref)):
        for group in range(GROUPS):
            count = STRIP_ROWS[group]
            start = STRIP_OFFSETS[group] + side * SIDE
            if count:
                down_out[start : start + count] = strips[group, 0:count]
                up_out[start : start + count] = strips[group, BLOCK - count : BLOCK]


def fine_kernel(
    low_ref, high_ref, main_ref, after_ref, before_ref, u0_ref, u1_ref, coarse_ref, *scratch
):
    count = len(Level.names)
    fine = Level(scratch[: 2 * count], 2, False)
    middle = Level(scratch[2 * count : 3 * count], 1, False)
    rest_main, rest_side, sum_main, sum_side, collect = scratch[3 * count :]

    blank = jnp.zeros((BLOCK, 128), F32)

    def unpack(after, before):
        even = ((iota(after.shape, 1) >> 4) & 1) == 0
        return jnp.where(even, after, before), jnp.where(even, before, after)

    at_y = lax.axis_index("gy")
    low_there = jnp.where(at_y > 0, 1.0, 0.0)
    high_there = jnp.where(at_y < lax.axis_size("gy") - 1, 1.0, 0.0)

    def place(target, plane, index, scale):
        low_scale, high_scale = low_there * scale, high_there * scale
        group, slot = index // 8, index % 8
        count, start = COUNTS[index], OFFSETS[index]
        main, side = target
        first, own, last = 8, 8 + BLOCK, 8 + 2 * BLOCK
        main[plane, first:own] = blank
        main[plane, last : last + BLOCK] = blank
        main[plane, own:last] = main_ref[index] * scale
        if count:
            main[plane, own - count : own] = low_ref[start : start + count] * low_scale
            main[plane, last : last + count] = high_ref[start : start + count] * high_scale

        def turned(pair, scale):
            value = pair[slot & 1]
            if slot:
                value = pltpu.roll(value, 128 - 16 * slot, 1)
            lane = iota(value.shape, 1)
            return jnp.where((lane < 16) | (lane >= 112), value, 0.0) * scale

        side[plane, own:last] = turned(unpack(after_ref[group], before_ref[group]), scale)
        rows = STRIP_ROWS[group]
        if rows < BLOCK:
            side[plane, first:own] = blank
            side[plane, last : last + BLOCK] = blank
        if rows:
            start = STRIP_OFFSETS[group]
            beyond = slice(start, start + rows), slice(start + SIDE, start + SIDE + rows)
            side[plane, own - rows : own] = turned(
                unpack(low_ref[beyond[0]], low_ref[beyond[1]]), low_scale
            )
            side[plane, last : last + rows] = turned(
                unpack(high_ref[beyond[0]], high_ref[beyond[1]]), high_scale
            )

    for index in range(F_PLANES):
        place(fine.g, index + 1, index, 2.0)
    for index in range(F_PLANES, PLANES):
        place(fine.b, index - F_PLANES, index, 1.0)

    fine.clear(B_PLANES, ROWS, (0, B_PLANES - 1))
    every = range(8, ROWS + 8, 8)
    fine.before(0, every)

    @pl.loop(1, B_PLANES - 1, step=4)
    def _(plane):
        for index in range(4):
            fine.setup(plane + index, every, index & 1)

    inner = range(16, ROWS, 8)
    for step in range(3):
        beside = 2 - step
        near = B_HALO - beside


        @pl.loop(near, near + BLOCK + 2 * beside, step=2)
        def _(plane):
            fine.relax(step, fine.adjacent(plane, 2), every)

        @pl.loop(near - 9, near, step=3)
        def _(plane):
            other = plane + BLOCK + 2 * beside + 9
            for base in (plane, other):
                fine.relax(step, [((base, index),) for index in range(3)], inner)

    for plane in range(BLOCK):
        u0_ref[plane] = fine.k[0][plane + B_HALO, 8 + BLOCK : 8 + 2 * BLOCK]

    @pl.loop(0, 16)
    def _(index):
        for row in inner:
            held = {}
            first = fine.rest(2 * index + 5, row, 0, held)
            second = fine.rest(2 * index + 5, row, 1, held)
            at = pl.ds(pl.multiple_of(32 * index + (row - 16), 8), 8)
            rest_main[at, :] = first[0] + second[0]
            rest_side[at, :] = first[1] + second[1]

    @pl.loop(0, 18)
    def _(index):
        for row in every:
            at = pl.ds(pl.multiple_of(48 * index + (row - 8), 8), 8)
            first, second = 2 * index + 3, 2 * index + 4
            here = slice(row, row + 8)
            sum_main[at, :] = fine.b[0][first, here] + fine.b[0][second, here]
            sum_side[at, :] = fine.b[1][first, here] + fine.b[1][second, here]

    to_main = pair_selector(128, 0, 128, 0, 64)
    to_side = pair_selector(128, 0, 128, 64, 64)
    g_next = split_matmul(halves(rest_main, 256), to_main)
    g_next = 0.5 * (g_next + split_matmul(halves(rest_side, 256), to_side))
    b_next = split_matmul(halves(sum_main, 432), to_main)
    b_next = 0.125 * (b_next + split_matmul(halves(sum_side, 432), to_side))

    middle.clear(20, 24, (1, 18))
    zero = jnp.zeros((8, 128), F32)
    for plane in range(2, 18):
        middle.g[0][plane, 8:16] = zero
        middle.g[0][plane, 24:32] = zero
        middle.g[0][plane, 12:28] = g_next[16 * (plane - 2) : 16 * (plane - 1)]
    for plane in range(1, 19):
        middle.b[0][plane, 8:32] = b_next[24 * (plane - 1) : 24 * plane]
    middle.before(1, range(8, 32, 8))

    @pl.loop(2, 18, step=4)
    def _(plane):
        for index in range(4):
            middle.setup(plane + index, range(8, 32, 8), index & 1)

    for step in range(3):

        @pl.loop(2, 18, step=4)
        def _(plane):
            middle.relax(step, middle.adjacent(plane, 4), range(8, 32, 8))

    for plane in range(8):
        u1_ref[plane] = middle.k[0][plane + 6, 16:24]
    for index in range(4):
        at = 32 * index
        (first,) = middle.rest(2 * index + 6, 16)
        (second,) = middle.rest(2 * index + 7, 16)
        collect[at : at + 8] = 0.5 * (first + second)
        first, second = middle.b[0][2 * index + 6, 14:26], middle.b[0][2 * index + 7, 14:26]
        collect[at + 8 : at + 20] = 0.125 * (first + second)
        collect[at + 20 : at + 32] = jnp.zeros((12, 128), F32)
    out = jnp.zeros((16, 128), F32)
    for index in range(4):
        rows = collect[pl.ds(32 * index, 16, stride=2), :]
        rows = rows + collect[pl.ds(32 * index + 1, 16, stride=2), :]
        out = out + split_matmul(rows, pair_selector(128, 0, 128, 32 * index, 32))
    for index in range(16):
        coarse_ref[index] = out


def squeeze_kernel(gathered_ref, out_ref):
    for row in range(10):
        value = gathered_ref[pl.ds(row, 16, stride=16), :]
        for index in range(4):
            out_ref[index, 16 * row : 16 * row + 16] = value


def line_kernel(gathered_ref, out_ref):
    group = iota((16, 128), 1) >> 5
    for row in range(10):
        here = slice(16 * row, 16 * row + 16)
        pieces = [gathered_ref[position, here] for position in range(4)]
        for part in range(4):
            value = pieces[part]
            for position in range(4):
                if position != part:
                    moved = pltpu.roll(pieces[position], (32 * (position - part)) % 128, 1)
                    value = jnp.where(group == position, moved, value)
            start = 64 * row + 16 * part
            out_ref[start : start + 16] = value


class Blocks(Level):
    starts = tuple(32 * block + 8 for block in range(4))

    def __init__(self, refs):
        super().__init__(refs, 1, True)
        self.parity = self.lane & 1

    def low(self, row):
        return row - 32 if row >= self.starts[1] else row + 95

    def high(self, row):
        return row + 32 if row < self.starts[3] else row - 95


def column_kernel(low_ref, own_ref, high_ref, u2_ref, coarse_ref, *scratch):
    column = Blocks(scratch)
    at_y = lax.axis_index("gy")
    low_there = jnp.where(at_y > 0, 1.0, 0.0)
    high_there = jnp.where(at_y < lax.axis_size("gy") - 1, 1.0, 0.0)
    (b,), (g,) = column.b, column.g

    def put(target, plane, source, index, scale=None):
        for block, start in enumerate(column.starts):
            at = 64 * index + 16 * block
            value = source[at : at + 16]
            if scale is not None:
                value = value * scale
            target[plane, start : start + 16] = value

    for index in range(4):
        put(g, 1 + index, low_ref, index, low_there)
        put(g, 5 + index, own_ref, index)
        put(g, 9 + index, high_ref, index, high_there)
        put(b, 5 + index, own_ref, 5 + index)
    for index in range(5):
        put(b, index, low_ref, 4 + index, low_there)
        put(b, 9 + index, high_ref, 5 + index, high_there)

    zero = jnp.zeros((8, 128), F32)
    for refs in (column.b, column.fy, column.r, column.k):
        for plane in range(14):
            refs[0][plane, 24:32] = zero
            refs[0][plane, 96:104] = zero
    halves_of = [range(start, start + 16, 8) for start in column.starts]
    rows = [row for half in halves_of for row in half]
    for refs in (column.r, column.k):
        for plane in (0, 13):
            for row in rows:
                refs[0][plane, row : row + 8] = zero
    column.before(0, rows)

    @pl.loop(1, 13, step=2)
    def _(plane):
        for index in range(2):
            for block, half in enumerate(halves_of):
                column.setup(plane + index, half, (index + block) & 1)

    for step in range(3):

        @pl.loop(2 + step, 12 - step, step=2)
        def _(plane):
            column.relax(step, column.adjacent(plane, 2), rows)

    at_x = lax.axis_index("gx")
    for index, start in enumerate(column.starts):
        for plane in range(4):
            u2_ref[index, plane : plane + 1] = column.k[0][plane + 5, pl.ds(start + at_x, 1), :]
        u2_ref[index, 4:8] = jnp.zeros((4, 128), F32)

    halve = [pair_selector(128, 0, 128, 64 * part, 64) for part in range(2)]
    g_out, b_out = [], []
    for plane in (5, 7):
        g_value = jnp.zeros((16, 128), F32)
        b_value = jnp.zeros((16, 128), F32)
        for part in range(2):
            g_parts, b_parts = [], []
            for offset in (0, 8):
                g_sum = b_sum = None
                for block in (2 * part, 2 * part + 1):
                    row = column.starts[block] + offset
                    for step in range(2):
                        (value,) = column.rest(plane, row, step)
                        weight = b[plane + step, row : row + 8]
                        g_sum = value if g_sum is None else g_sum + value
                        b_sum = weight if b_sum is None else b_sum + weight
                g_parts.append(0.5 * g_sum)
                b_parts.append(0.125 * b_sum)
            g_value = g_value + split_matmul(jnp.concatenate(g_parts, axis=0), halve[part])
            b_value = b_value + split_matmul(jnp.concatenate(b_parts, axis=0), halve[part])
        g_out.append(g_value)
        b_out.append(b_value)
    for index in range(8):
        for part, value in enumerate(g_out + b_out):
            coarse_ref[index, 16 * part : 16 * part + 16] = value


def coarse_kernel(
    gathered_ref, u0_ref, u1_ref, u2_ref, out_ref,
    r3, rs, k3, ks, inner_3, outer_3, fy3, fz3, d3, ir3, ik3, b3, bs,
    r4, k4, fx4, fy4, fz4, ir4, ik4, g4, b4,
    g_rows, b_rows, pair_3, pair_4, twice_3, twice_2, twice_1, twice_0, level_1,
):
    at_x = lax.axis_index("gx")
    at_y = lax.axis_index("gy")
    at_z = lax.axis_index("gz")
    lane = iota((8, 128), 1)
    row8 = iota((8, 128), 0)
    zero = jnp.zeros((8, 128), F32)

    cell = lane & 63
    parity = ((lane >> 6) + row8 + cell) & 1
    first_half = lane < 64
    for index in range(8):
        for part in range(2):
            rows = pl.ds(2 * index + part, 16, stride=16)
            g_rows[rows, :] = gathered_ref[index, 16 * part : 16 * part + 16]
            b_rows[rows, :] = gathered_ref[index, 16 * part + 32 : 16 * part + 48]
    for ref in (r3, rs, k3, ks, b3, bs):
        for plane in (0, 17):
            ref[plane] = jnp.zeros((32, 128), F32)
    for plane in range(1, 17):
        for ref in (r3, k3, b3, fy3):
            ref[plane, 0:8] = zero
            ref[plane, 24:32] = zero
        for row in (8, 16):
            value = b_rows[16 * plane + row - 24 : 16 * plane + row - 16]
            b3[plane, row : row + 8] = value
            bs[plane, row : row + 8] = pltpu.roll(value, 64, 1)

    def outer(ref, plane, here):
        return jnp.where(first_half, ref[plane - 1, here], ref[plane + 1, here])

    for plane in range(1, 17):
        for row in (8, 16):
            here = slice(row, row + 8)
            b = b3[plane, here]
            partner, other = bs[plane, here], outer(bs, plane, here)
            y_high = b3[plane, row + 1 : row + 9]
            z_low = jnp.where(cell > 0, pltpu.roll(b, 1, 1), 0.0)
            z_high = jnp.where(cell < 63, pltpu.roll(b, 127, 1), 0.0)
            total = (6.0 * b + (partner + other)) + (
                (b3[plane, row - 1 : row + 7] + y_high) + (z_low + z_high)
            )
            inside = b > 0.0
            inverse = 1.0 / jnp.where(inside, total, 1.0)
            reds = jnp.where(inside & (parity == 0), inverse, 0.0)
            inner_3[plane, here] = b + partner
            outer_3[plane, here] = b + other
            fy3[plane, here] = b + y_high
            fz3[plane, here] = jnp.where(cell < 63, b + z_high, 0.0)
            d3[plane, here] = total
            ir3[plane, here] = reds
            ik3[plane, here] = jnp.where(inside & (parity == 1), inverse, 0.0)
            value = g_rows[16 * plane + row - 24 : 16 * plane + row - 16] * reds
            r3[plane, here] = value
            rs[plane, here] = pltpu.roll(value, 64, 1)

    def total_3(ref, swapped, plane, row):
        here, low, high = slice(row, row + 8), slice(row - 1, row + 7), slice(row + 1, row + 9)
        v, face = ref[plane, here], fz3[plane, here]
        along_x = inner_3[plane, here] * swapped[plane, here]
        along_x = along_x + outer_3[plane, here] * outer(swapped, plane, here)
        along_y = fy3[plane, here] * ref[plane, high] + fy3[plane, low] * ref[plane, low]
        along_z = face * pltpu.roll(v, 127, 1) + pltpu.roll(face * v, 1, 1)
        g = g_rows[16 * plane + row - 24 : 16 * plane + row - 16]
        return (g + along_x) + (along_y + along_z)

    for step in range(3):
        source, inverse, target = (
            ((r3, rs), ik3, (k3, ks)),
            ((k3, ks), ir3, (r3, rs)),
            ((r3, rs), ik3, (k3, ks)),
        )[step]
        for plane in range(1, 17):
            for row in (8, 16):
                here = slice(row, row + 8)
                value = total_3(*source, plane, row) * inverse[plane, here]
                if step == 2:
                    value = value + r3[plane, here]
                target[0][plane, here] = value
                target[1][plane, here] = pltpu.roll(value, 64, 1)

    for plane in range(1, 17):
        for row in (8, 16):
            here = slice(row, row + 8)
            value = total_3(k3, ks, plane, row) - d3[plane, here] * k3[plane, here]
            at = slice(16 * (plane - 1) + row - 8, 16 * (plane - 1) + row)
            pair_3[at] = value + pltpu.roll(value, 64, 1)
            pair_4[at] = b3[plane, here] + bs[plane, here]
    halve = pair_selector(128, 0, 128, 0, 32)
    g4[...] = 0.5 * split_matmul(halves(pair_3, 128), halve).reshape(16, 8, 128)
    b4[0] = zero
    b4[17] = zero
    b4[1:17] = 0.125 * split_matmul(halves(pair_4, 128), halve).reshape(16, 8, 128)

    parity = (row8 + lane) & 1
    for ref in (r4, k4):
        ref[0] = zero
        ref[17] = zero
    fx4[0] = b4[1]
    for plane in range(1, 17):
        b = b4[plane]
        x_high = b4[plane + 1]
        y_low = jnp.where(row8 > 0, pltpu.roll(b, 1, 0), 0.0)
        y_high = jnp.where(row8 < 7, pltpu.roll(b, 7, 0), 0.0)
        z_high = pltpu.roll(b, 127, 1)
        total = (6.0 * b + (b4[plane - 1] + x_high)) + (
            (y_low + y_high) + (pltpu.roll(b, 1, 1) + z_high)
        )
        inside = b > 0.0
        inverse = 1.0 / jnp.where(inside, total, 1.0)
        reds = jnp.where(inside & (parity == (plane - 1) & 1), inverse, 0.0)
        fx4[plane] = b + x_high
        fy4[plane] = jnp.where(row8 < 7, b + y_high, 0.0)
        fz4[plane] = jnp.where(lane < 31, b + z_high, 0.0)
        ir4[plane] = reds
        ik4[plane] = jnp.where(inside & (parity != (plane - 1) & 1), inverse, 0.0)
        r4[plane] = g4[plane - 1] * reds

    def half_4(source, inverse, target):
        for first in range(1, 17, 2):
            pair = (first, first + 1)
            v = source[first] + source[first + 1]
            y_face = fy4[first] * source[first] + fy4[first + 1] * source[first + 1]
            z_face = fz4[first] * source[first] + fz4[first + 1] * source[first + 1]
            y_high, y_low = pltpu.roll(v, 7, 0), pltpu.roll(y_face, 1, 0)
            z_high, z_low = pltpu.roll(v, 127, 1), pltpu.roll(z_face, 1, 1)
            for plane in pair:
                along_x = fx4[plane] * source[plane + 1] + fx4[plane - 1] * source[plane - 1]
                along_y = fy4[plane] * y_high + y_low
                along_z = fz4[plane] * z_high + z_low
                value = (g4[plane - 1] + along_x) + (along_y + along_z)
                target[plane] = value * inverse[plane]

    half_4(r4, ik4, k4)

    @pl.loop(1, COARSE_SWEEPS)
    def _(sweep):
        half_4(k4, ir4, r4)
        half_4(r4, ik4, k4)

    source = iota((128, 128), 0)
    target = iota((128, 128), 1)
    spread = selector_of((source < 32) & (((target & 63) >> 1) == source))
    value = split_matmul(r4[at_x + 1] + k4[at_x + 1], spread)
    twice_3[pl.ds(0, 8, stride=2), :] = value
    twice_3[pl.ds(1, 8, stride=2), :] = value
    value = k3[at_x + 1, 8:24] + twice_3[...]
    value = pltpu.roll(value, lax.rem(16 - 2 * at_y, 16), 0)
    value = pltpu.roll(value, lax.rem(128 - 16 * at_z, 128), 1)
    level_2 = []
    for part in range(2):
        fine = split_matmul(value, spread_selector(64 * part, 0, 16))[0:8]
        twice_2[pl.ds(0, 8, stride=2), :] = fine
        twice_2[pl.ds(1, 8, stride=2), :] = fine
        for index in range(2):
            own = u2_ref[2 * part + index]
            own = pltpu.roll(own, lax.rem(128 - 32 * at_z, 128), 1)
            level_2.append(own + twice_2[0:8])
    fine = split_matmul(jnp.concatenate(level_2, axis=0), spread_selector(0, 0, 32))
    twice_1[pl.ds(0, 32, stride=2), :] = fine
    twice_1[pl.ds(1, 32, stride=2), :] = fine
    for index in range(8):
        start = 16 * (index // 2)
        level_1[8 * index : 8 * index + 8] = u1_ref[index] + twice_1[start : start + 8]
    fine = split_matmul(level_1[...], spread_selector(0, 0, 64))
    twice_0[pl.ds(0, 64, stride=2), :] = fine
    twice_0[pl.ds(1, 64, stride=2), :] = fine
    for index in range(16):
        start = 16 * (index // 2)
        out_ref[index] = u0_ref[index] + twice_0[start : start + 16]


def call(kernel, megabytes, outs, scratch, *operands):
    whole = pl.BlockSpec(memory_space=pltpu.VMEM)
    return pl.pallas_call(
        kernel,
        out_shape=[jax.ShapeDtypeStruct(shape, F32) for shape in outs],
        in_specs=[whole] * len(operands),
        out_specs=[whole] * len(outs),
        scratch_shapes=[pltpu.VMEM(shape, F32) for shape in scratch],
        compiler_params=pltpu.CompilerParams(vmem_limit_bytes=megabytes << 20),
    )(*operands)


def shift(value, axis, step):
    count = lax.axis_size(axis)
    pairs = [(i, i + step) for i in range(count) if 0 <= i + step < count]
    return lax.ppermute(value, axis, pairs)


def around(value, axis, step):
    count = lax.axis_size(axis)
    return lax.ppermute(value, axis, [(i, (i + step) % count) for i in range(count)])


def swap(value, axis, first):
    count = lax.axis_size(axis)
    lower = range(first, count - 1, 2)
    pairs = [(i, i + 1) for i in lower] + [(i + 1, i) for i in lower]
    return lax.ppermute(value, axis, pairs)


def on_device(right_side, conductivity):
    f, b = right_side, conductivity
    edge = (F_HALO + B_HALO, BLOCK, 128)
    upper, lower = call(edge_kernel, 2, [edge, edge], [], f, b)
    low, high = shift(upper, "gx", 1), shift(lower, "gx", -1)

    strip = (GROUPS, BLOCK, 128)
    packed = (PACKED, 128)
    main, left, right, down, up = call(
        pack_kernel, 4, [(PLANES, BLOCK, 128), strip, strip, packed, packed], [], f, b, low, high
    )
    first, second = swap(left, "gz", 0), swap(right, "gz", 1)
    down, up, after, before = call(
        join_kernel, 4, [(PAYLOAD, 128)] * 2 + [strip] * 2, [], down, up, first, second
    )
    low, high = around(up, "gy", 1), around(down, "gy", -1)

    u0, u1, coarse = call(
        fine_kernel,
        40,
        [(BLOCK, BLOCK, 128), (8, 8, 128), (16, 16, 128)],
        Level.scratch(2, B_PLANES, ROWS)
        + Level.scratch(1, 20, 24)
        + [(512, 128)] * 2
        + [(864, 128)] * 2
        + [(128, 128)],
        low, high, main, after, before,
    )

    column = lax.all_to_all(coarse, "gx", 0, 0, tiled=True)
    (column,) = call(squeeze_kernel, 2, [(4, 160, 128)], [], column.reshape(256, 128))
    column = lax.all_to_all(column, "gz", 0, 0, tiled=True)
    (column,) = call(line_kernel, 2, [(640, 128)], [], column)
    low, high = around(column, "gy", 1), around(column, "gy", -1)
    u2, coarse = call(
        column_kernel,
        13,
        [(4, 8, 128), (8, 64, 128)],
        Level.scratch(1, 14, 112),
        low, column, high,
    )

    whole = lax.all_to_all(coarse, "gy", 0, 0, tiled=True)
    (out,) = call(
        coarse_kernel,
        8,
        [(BLOCK, BLOCK, 128)],
        [(18, 32, 128)] * 13
        + [(18, 8, 128)] * 7
        + [(16, 8, 128), (18, 8, 128)]
        + [(256, 128)] * 4
        + [(16, 128), (16, 128), (64, 128), (128, 128), (64, 128)],
        whole, u0, u1, u2,
    )
    return out


def solution(mesh):
    spec = P("gx", "gy", "gz")
    return jax.shard_map(
        on_device, mesh=mesh, in_specs=(spec, spec), out_specs=spec, check_vma=False
    )
```

```python
import jax
import jax.numpy as jnp
from jax import lax
from jax.experimental import pallas as pl
from jax.experimental.pallas import tpu as pltpu
from jax.sharding import PartitionSpec as P

F_HALO = 12
B_HALO = 13
BLOCK = 16
F_PLANES = BLOCK + 2 * F_HALO
B_PLANES = BLOCK + 2 * B_HALO
PLANES = F_PLANES + B_PLANES
GROUPS = -(-PLANES // 8)
F_GROUPS = F_PLANES // 8
ROWS = 48


def rows_of(index):
    if index < F_PLANES:
        return F_HALO - max(F_HALO - index, index - F_HALO - BLOCK + 1, 0)
    index -= F_PLANES
    return B_HALO - max(B_HALO - index, index - B_HALO - BLOCK + 1, 0)


COUNTS = [rows_of(index) for index in range(PLANES)]
OFFSETS = [sum(COUNTS[:index]) for index in range(PLANES)]
PACKED = sum(COUNTS)
STRIP_ROWS = [
    max(0, max(COUNTS[8 * group : 8 * group + 8]) - 1) for group in range(GROUPS)
]
STRIP_OFFSETS = [PACKED + sum(STRIP_ROWS[:group]) for group in range(GROUPS)]
SIDE = sum(STRIP_ROWS)
PAYLOAD = PACKED + 2 * SIDE
COARSE_SWEEPS = 8
F32 = jnp.float32


def iota(shape, dim):
    return lax.broadcasted_iota(jnp.int32, shape, dim)


def split_matmul(value, selector):
    high = value.astype(jnp.bfloat16)
    low = (value - high.astype(F32)).astype(jnp.bfloat16)
    return jnp.dot(high, selector, preferred_element_type=F32) + jnp.dot(
        low, selector, preferred_element_type=F32
    )


def selector_of(condition):
    return jnp.where(condition, 1.0, 0.0).astype(jnp.bfloat16)


def pair_selector(source_lanes, first, out_lanes, offset, count):
    source = iota((source_lanes, out_lanes), 0) - first
    target = iota((source_lanes, out_lanes), 1) - offset
    return selector_of(
        (source >= 0) & (source < 2 * count) & ((source >> 1) == target)
    )


def spread_selector(first, offset, count):
    source = iota((128, 128), 0) - first
    target = iota((128, 128), 1) - offset
    return selector_of((source >= 0) & (source < count) & ((target >> 1) == source))


class Level:
    names = ("b", "g", "fx", "fy", "fz", "d", "ir", "ik", "r", "k")

    def __init__(self, refs, columns, walled):
        self.walled = walled
        self.columns = columns
        for index, name in enumerate(self.names):
            setattr(self, name, refs[index * columns : (index + 1) * columns])
        self.lane = iota((8, 128), 1)
        self.parity = (iota((8, 128), 0) + self.lane) & 1

    @staticmethod
    def scratch(columns, planes, rows):
        return [(planes, rows + 16, 128)] * (len(Level.names) * columns)

    def low(self, row):
        return row - 1

    def high(self, row):
        return row + 1

    def at(self, refs, plane, row):
        return [ref[plane, row : row + 8] for ref in refs]

    def put(self, refs, plane, row, values):
        for ref, value in zip(refs, values):
            ref[plane, row : row + 8] = value

    def turn(self, values, step):
        rolled = [pltpu.roll(value, 127 if step > 0 else 1, 1) for value in values]
        if self.columns == 1:
            return rolled
        edge = self.lane == (127 if step > 0 else 0)
        first, second = rolled
        return [jnp.where(edge, second, first), jnp.where(edge, first, second)]

    def clear(self, planes, rows, ends):
        zero = jnp.zeros((8, 128), F32)

        @pl.loop(0, planes)
        def _(plane):
            for refs in (self.b, self.r, self.k):
                for ref in refs:
                    ref[plane, 0:8] = zero
                    ref[plane, rows + 8 : rows + 16] = zero
            for ref in self.fy:
                ref[plane, 0:8] = zero

        for refs in (self.r, self.k):
            for ref in refs:
                for plane in ends:
                    ref[plane] = jnp.zeros((rows + 16, 128), F32)

    def before(self, plane, rows):
        for row in rows:
            near = zip(self.at(self.b, plane, row), self.at(self.b, plane + 1, row))
            self.put(self.fx, plane, row, [own + other for own, other in near])

    def setup(self, plane, rows, red):
        for row in rows:
            b = self.at(self.b, plane, row)
            x_low, x_high = self.at(self.b, plane - 1, row), self.at(self.b, plane + 1, row)
            y_low, y_high = self.at(self.b, plane, self.low(row)), self.at(self.b, plane, self.high(row))
            z_low, z_high = self.turn(b, -1), self.turn(b, 1)
            g = self.at(self.g, plane, row)
            for column in range(self.columns):
                own, z_before, z_after = b[column], z_low[column], z_high[column]
                face = own + z_after
                if self.walled:
                    z_before = jnp.where(self.lane > 0, z_before, 0.0)
                    z_after = jnp.where(self.lane < 127, z_after, 0.0)
                    face = jnp.where(self.lane < 127, face, 0.0)
                total = (6.0 * own + (x_low[column] + x_high[column])) + (
                    (y_low[column] + y_high[column]) + (z_before + z_after)
                )
                inside = own > 0.0
                inverse = 1.0 / jnp.where(inside, total, 1.0)
                first = self.parity == red
                reds = jnp.where(inside & first, inverse, 0.0)
                here = (plane, slice(row, row + 8))
                self.fx[column][here] = own + x_high[column]
                self.fy[column][here] = own + y_high[column]
                self.fz[column][here] = face
                self.d[column][here] = total
                self.ir[column][here] = reds
                self.ik[column][here] = jnp.where(inside & ~first, inverse, 0.0)
                self.r[column][here] = g[column] * reds
                self.k[column][here] = jnp.zeros((8, 128), F32)

    def load(self, ref, base, step, row, held):
        key = (id(ref), id(base), step)
        if key not in held:
            held[key] = ref[base + step, row : row + 8]
        return held[key]

    def along_z(self, source, places, row, held):
        fields, scaled = [], []
        for base, step in places:
            v = [self.load(ref, base, step, row, held) for ref in source]
            face = [self.load(ref, base, step, row, held) for ref in self.fz]
            fields.append((v, face))
            scaled.append([a * b for a, b in zip(face, v)])
        v_sum, w_sum = fields[0][0], scaled[0]
        for (v, _), w in zip(fields[1:], scaled[1:]):
            v_sum = [a + b for a, b in zip(v_sum, v)]
            w_sum = [a + b for a, b in zip(w_sum, w)]
        high, low = self.turn(v_sum, 1), self.turn(w_sum, -1)
        return [[f * h + l for f, h, l in zip(face, high, low)] for _, face in fields]

    def total(self, source, base, step, row, held, along_z):
        out = []
        for column in range(self.columns):
            ref, fx, fy = source[column], self.fx[column], self.fy[column]
            along_x = self.load(fx, base, step, row, held) * self.load(
                ref, base, step + 1, row, held
            ) + self.load(fx, base, step - 1, row, held) * self.load(
                ref, base, step - 1, row, held
            )
            low = slice(self.low(row), self.low(row) + 8)
            high = slice(self.high(row), self.high(row) + 8)
            plane = base + step
            along_y = (
                self.load(fy, base, step, row, held) * ref[plane, high]
                + fy[plane, low] * ref[plane, low]
            )
            g = self.load(self.g[column], base, step, row, held)
            out.append((g + along_x) + (along_y + along_z[column]))
        return out

    def relax(self, step, pairs, rows):
        source, inverse, target = (
            (self.r, self.ik, self.k),
            (self.k, self.ir, self.r),
            (self.r, self.ik, self.k),
        )[step]
        for row in rows:
            held = {}
            for places in pairs:
                sums = self.along_z(source, places, row, held)
                for (base, index), along_z in zip(places, sums):
                    values = self.total(source, base, index, row, held, along_z)
                    scale = self.at(inverse, base + index, row)
                    values = [value * factor for value, factor in zip(values, scale)]
                    if step == 2:
                        own = self.at(self.r, base + index, row)
                        values = [a + b for a, b in zip(values, own)]
                    self.put(target, base + index, row, values)

    @staticmethod
    def adjacent(base, count):
        return [((base, index), (base, index + 1)) for index in range(0, count, 2)]

    def rest(self, base, row, step=0, held=None):
        held = {} if held is None else held
        (along_z,) = self.along_z(self.k, ((base, step),), row, held)
        values = self.total(self.k, base, step, row, held, along_z)
        plane = base + step
        out = []
        for column, value in enumerate(values):
            here = (plane, slice(row, row + 8))
            value = value - self.d[column][here] * self.k[column][here]
            out.append(jnp.where(self.b[column][here] > 0.0, value, 0.0))
        return out


def halves(ref, rows):
    return ref[pl.ds(0, rows, stride=2), :] + ref[pl.ds(1, rows, stride=2), :]


def pack_kernel(
    f_ref, b_ref, low_ref, high_ref, main_ref, left_ref, right_ref, down_ref, up_ref
):
    lane = iota((BLOCK, 128), 1)
    even = lax.rem(lax.axis_index("gz"), 2) == 0

    def source(index):
        if index < F_HALO:
            return low_ref[index]
        if index < F_HALO + BLOCK:
            return f_ref[index - F_HALO]
        if index < F_PLANES:
            return high_ref[index - F_HALO - BLOCK]
        index -= F_PLANES
        if index < B_HALO:
            return low_ref[F_HALO + index]
        if index < B_HALO + BLOCK:
            return b_ref[index - B_HALO]
        return high_ref[F_HALO + index - B_HALO - BLOCK]

    for group in range(GROUPS):
        left = jnp.zeros((BLOCK, 128), F32)
        right = jnp.zeros((BLOCK, 128), F32)
        for slot in range(8):
            index = group * 8 + slot
            if index >= PLANES:
                break
            plane = source(index)
            main_ref[index] = plane
            count, start = COUNTS[index], OFFSETS[index]
            if count:
                down_ref[start : start + count] = plane[0:count]
                up_ref[start : start + count] = plane[BLOCK - count : BLOCK]
            turned = pltpu.roll(plane, 16 * slot, 1) if slot else plane
            left = jnp.where((lane >> 4) == slot, turned, left)
            right = jnp.where((lane >> 4) == ((slot - 1) & 7), turned, right)
        left_ref[group] = jnp.where(even, right, left)
        right_ref[group] = jnp.where(even, left, right)


def join_kernel(
    down_ref, up_ref, first_ref, second_ref, down_out, up_out, after_ref, before_ref
):
    even = lax.rem(lax.axis_index("gz"), 2) == 0
    for group in range(GROUPS):
        first, second = first_ref[group], second_ref[group]
        after_ref[group] = jnp.where(even, first, second)
        before_ref[group] = jnp.where(even, second, first)
    down_out[0:PACKED] = down_ref[...]
    up_out[0:PACKED] = up_ref[...]
    for side, strips in enumerate((after_ref, before_ref)):
        for group in range(GROUPS):
            count = STRIP_ROWS[group]
            start = STRIP_OFFSETS[group] + side * SIDE
            if count:
                down_out[start : start + count] = strips[group, 0:count]
                up_out[start : start + count] = strips[group, BLOCK - count : BLOCK]


def fine_kernel(
    low_ref, high_ref, main_ref, after_ref, before_ref, u0_ref, u1_ref, coarse_ref, *scratch
):
    count = len(Level.names)
    fine = Level(scratch[: 2 * count], 2, False)
    middle = Level(scratch[2 * count : 3 * count], 1, False)
    rest_main, rest_side, sum_main, sum_side, collect = scratch[3 * count :]

    blank = jnp.zeros((BLOCK, 128), F32)

    def unpack(after, before):
        even = ((iota(after.shape, 1) >> 4) & 1) == 0
        return jnp.where(even, after, before), jnp.where(even, before, after)

    at_y = lax.axis_index("gy")
    low_there = jnp.where(at_y > 0, 1.0, 0.0)
    high_there = jnp.where(at_y < lax.axis_size("gy") - 1, 1.0, 0.0)

    def place(target, plane, index, scale):
        low_scale, high_scale = low_there * scale, high_there * scale
        group, slot = index // 8, index % 8
        count, start = COUNTS[index], OFFSETS[index]
        main, side = target
        first, own, last = 8, 8 + BLOCK, 8 + 2 * BLOCK
        main[plane, first:own] = blank
        main[plane, last : last + BLOCK] = blank
        main[plane, own:last] = main_ref[index] * scale
        if count:
            main[plane, own - count : own] = low_ref[start : start + count] * low_scale
            main[plane, last : last + count] = high_ref[start : start + count] * high_scale

        def turned(pair, scale):
            value = pair[slot & 1]
            if slot:
                value = pltpu.roll(value, 128 - 16 * slot, 1)
            lane = iota(value.shape, 1)
            return jnp.where((lane < 16) | (lane >= 112), value, 0.0) * scale

        side[plane, own:last] = turned(unpack(after_ref[group], before_ref[group]), scale)
        rows = STRIP_ROWS[group]
        if rows < BLOCK:
            side[plane, first:own] = blank
            side[plane, last : last + BLOCK] = blank
        if rows:
            start = STRIP_OFFSETS[group]
            beyond = slice(start, start + rows), slice(start + SIDE, start + SIDE + rows)
            side[plane, own - rows : own] = turned(
                unpack(low_ref[beyond[0]], low_ref[beyond[1]]), low_scale
            )
            side[plane, last : last + rows] = turned(
                unpack(high_ref[beyond[0]], high_ref[beyond[1]]), high_scale
            )

    for index in range(F_PLANES):
        place(fine.g, index + 1, index, 2.0)
    for index in range(F_PLANES, PLANES):
        place(fine.b, index - F_PLANES, index, 1.0)

    fine.clear(B_PLANES, ROWS, (0, B_PLANES - 1))
    every = range(8, ROWS + 8, 8)
    fine.before(0, every)

    @pl.loop(1, B_PLANES - 1, step=4)
    def _(plane):
        for index in range(4):
            fine.setup(plane + index, every, index & 1)

    inner = range(16, ROWS, 8)
    for step in range(3):
        beside = 2 - step
        near = B_HALO - beside


        @pl.loop(near, near + BLOCK + 2 * beside, step=2)
        def _(plane):
            fine.relax(step, fine.adjacent(plane, 2), every)

        @pl.loop(near - 9, near, step=3)
        def _(plane):
            other = plane + BLOCK + 2 * beside + 9
            for base in (plane, other):
                fine.relax(step, [((base, index),) for index in range(3)], inner)

    for plane in range(BLOCK):
        u0_ref[plane] = fine.k[0][plane + B_HALO, 8 + BLOCK : 8 + 2 * BLOCK]

    @pl.loop(0, 16)
    def _(index):
        for row in inner:
            held = {}
            first = fine.rest(2 * index + 5, row, 0, held)
            second = fine.rest(2 * index + 5, row, 1, held)
            at = pl.ds(pl.multiple_of(32 * index + (row - 16), 8), 8)
            rest_main[at, :] = first[0] + second[0]
            rest_side[at, :] = first[1] + second[1]

    @pl.loop(0, 18)
    def _(index):
        for row in every:
            at = pl.ds(pl.multiple_of(48 * index + (row - 8), 8), 8)
            first, second = 2 * index + 3, 2 * index + 4
            here = slice(row, row + 8)
            sum_main[at, :] = fine.b[0][first, here] + fine.b[0][second, here]
            sum_side[at, :] = fine.b[1][first, here] + fine.b[1][second, here]

    to_main = pair_selector(128, 0, 128, 0, 64)
    to_side = pair_selector(128, 0, 128, 64, 64)
    g_next = split_matmul(halves(rest_main, 256), to_main)
    g_next = 0.5 * (g_next + split_matmul(halves(rest_side, 256), to_side))
    b_next = split_matmul(halves(sum_main, 432), to_main)
    b_next = 0.125 * (b_next + split_matmul(halves(sum_side, 432), to_side))

    middle.clear(20, 24, (1, 18))
    zero = jnp.zeros((8, 128), F32)
    for plane in range(2, 18):
        middle.g[0][plane, 8:16] = zero
        middle.g[0][plane, 24:32] = zero
        middle.g[0][plane, 12:28] = g_next[16 * (plane - 2) : 16 * (plane - 1)]
    for plane in range(1, 19):
        middle.b[0][plane, 8:32] = b_next[24 * (plane - 1) : 24 * plane]
    middle.before(1, range(8, 32, 8))

    @pl.loop(2, 18, step=4)
    def _(plane):
        for index in range(4):
            middle.setup(plane + index, range(8, 32, 8), index & 1)

    for step in range(3):

        @pl.loop(2, 18, step=4)
        def _(plane):
            middle.relax(step, middle.adjacent(plane, 4), range(8, 32, 8))

    for plane in range(8):
        u1_ref[plane] = middle.k[0][plane + 6, 16:24]
    for index in range(4):
        at = 32 * index
        (first,) = middle.rest(2 * index + 6, 16)
        (second,) = middle.rest(2 * index + 7, 16)
        collect[at : at + 8] = 0.5 * (first + second)
        first, second = middle.b[0][2 * index + 6, 14:26], middle.b[0][2 * index + 7, 14:26]
        collect[at + 8 : at + 20] = 0.125 * (first + second)
        collect[at + 20 : at + 32] = jnp.zeros((12, 128), F32)
    out = jnp.zeros((16, 128), F32)
    for index in range(4):
        rows = collect[pl.ds(32 * index, 16, stride=2), :]
        rows = rows + collect[pl.ds(32 * index + 1, 16, stride=2), :]
        out = out + split_matmul(rows, pair_selector(128, 0, 128, 32 * index, 32))
    for index in range(16):
        coarse_ref[index] = out


def squeeze_kernel(gathered_ref, out_ref):
    for row in range(10):
        value = gathered_ref[pl.ds(row, 16, stride=16), :]
        for index in range(4):
            out_ref[index, 16 * row : 16 * row + 16] = value


def line_kernel(gathered_ref, out_ref, up_ref, down_ref):
    group = iota((16, 128), 1) >> 5
    for row in range(10):
        here = slice(16 * row, 16 * row + 16)
        pieces = [gathered_ref[position, here] for position in range(4)]
        for part in range(4):
            value = pieces[part]
            for position in range(4):
                if position != part:
                    moved = pltpu.roll(pieces[position], (32 * (position - part)) % 128, 1)
                    value = jnp.where(group == position, moved, value)
            start = 64 * row + 16 * part
            out_ref[start : start + 16] = value
            if row < 9:
                up_ref[start : start + 16] = value
            if row != 4:
                start -= 64 * (row > 4)
                down_ref[start : start + 16] = value


class Blocks(Level):
    starts = tuple(32 * block + 8 for block in range(4))

    def __init__(self, refs):
        super().__init__(refs, 1, True)
        self.parity = self.lane & 1

    def low(self, row):
        return row - 32 if row >= self.starts[1] else row + 95

    def high(self, row):
        return row + 32 if row < self.starts[3] else row - 95


def column_kernel(low_ref, own_ref, high_ref, u2_ref, coarse_ref, *scratch):
    column = Blocks(scratch)
    at_y = lax.axis_index("gy")
    low_there = jnp.where(at_y > 0, 1.0, 0.0)
    high_there = jnp.where(at_y < lax.axis_size("gy") - 1, 1.0, 0.0)
    (b,), (g,) = column.b, column.g

    def put(target, plane, source, index, scale=None):
        for block, start in enumerate(column.starts):
            at = 64 * index + 16 * block
            value = source[at : at + 16]
            if scale is not None:
                value = value * scale
            target[plane, start : start + 16] = value

    for index in range(4):
        put(g, 1 + index, low_ref, index, low_there)
        put(g, 5 + index, own_ref, index)
        put(g, 9 + index, high_ref, index, high_there)
        put(b, 5 + index, own_ref, 5 + index)
    for index in range(5):
        put(b, index, low_ref, 4 + index, low_there)
        put(b, 9 + index, high_ref, 4 + index, high_there)

    zero = jnp.zeros((8, 128), F32)
    for refs in (column.b, column.fy, column.r, column.k):
        for plane in range(14):
            refs[0][plane, 24:32] = zero
            refs[0][plane, 96:104] = zero
    halves_of = [range(start, start + 16, 8) for start in column.starts]
    rows = [row for half in halves_of for row in half]
    for refs in (column.r, column.k):
        for plane in (0, 13):
            for row in rows:
                refs[0][plane, row : row + 8] = zero
    column.before(0, rows)

    @pl.loop(1, 13, step=2)
    def _(plane):
        for index in range(2):
            for block, half in enumerate(halves_of):
                column.setup(plane + index, half, (index + block) & 1)

    for step in range(3):

        @pl.loop(2 + step, 12 - step, step=2)
        def _(plane):
            column.relax(step, column.adjacent(plane, 2), rows)

    at_x = lax.axis_index("gx")
    for index, start in enumerate(column.starts):
        for plane in range(4):
            u2_ref[index, plane : plane + 1] = column.k[0][plane + 5, pl.ds(start + at_x, 1), :]
        u2_ref[index, 4:8] = jnp.zeros((4, 128), F32)

    halve = [pair_selector(128, 0, 128, 64 * part, 64) for part in range(2)]
    g_out, b_out = [], []
    for plane in (5, 7):
        g_value = jnp.zeros((16, 128), F32)
        b_value = jnp.zeros((16, 128), F32)
        for part in range(2):
            g_parts, b_parts = [], []
            for offset in (0, 8):
                g_sum = b_sum = None
                for block in (2 * part, 2 * part + 1):
                    row = column.starts[block] + offset
                    for step in range(2):
                        (value,) = column.rest(plane, row, step)
                        weight = b[plane + step, row : row + 8]
                        g_sum = value if g_sum is None else g_sum + value
                        b_sum = weight if b_sum is None else b_sum + weight
                g_parts.append(0.5 * g_sum)
                b_parts.append(0.125 * b_sum)
            g_value = g_value + split_matmul(jnp.concatenate(g_parts, axis=0), halve[part])
            b_value = b_value + split_matmul(jnp.concatenate(b_parts, axis=0), halve[part])
        g_out.append(g_value)
        b_out.append(b_value)
    for index in range(8):
        for part, value in enumerate(g_out + b_out):
            coarse_ref[index, 16 * part : 16 * part + 16] = value


def coarse_kernel(
    gathered_ref, u0_ref, u1_ref, u2_ref, out_ref,
    r3, rs, k3, ks, inner_3, outer_3, fy3, fz3, d3, ir3, ik3, b3, bs,
    r4, k4, fx4, fy4, fz4, ir4, ik4, g4, b4,
    g_rows, b_rows, pair_3, pair_4, twice_3, twice_2, twice_1, twice_0, level_1,
):
    at_x = lax.axis_index("gx")
    at_y = lax.axis_index("gy")
    at_z = lax.axis_index("gz")
    lane = iota((8, 128), 1)
    row8 = iota((8, 128), 0)
    zero = jnp.zeros((8, 128), F32)

    cell = lane & 63
    parity = ((lane >> 6) + row8 + cell) & 1
    first_half = lane < 64
    for index in range(8):
        for part in range(2):
            rows = pl.ds(2 * index + part, 16, stride=16)
            g_rows[rows, :] = gathered_ref[index, 16 * part : 16 * part + 16]
            b_rows[rows, :] = gathered_ref[index, 16 * part + 32 : 16 * part + 48]
    for ref in (r3, rs, k3, ks, b3, bs):
        for plane in (0, 17):
            ref[plane] = jnp.zeros((32, 128), F32)
    for plane in range(1, 17):
        for ref in (r3, k3, b3, fy3):
            ref[plane, 0:8] = zero
            ref[plane, 24:32] = zero
        for row in (8, 16):
            value = b_rows[16 * plane + row - 24 : 16 * plane + row - 16]
            b3[plane, row : row + 8] = value
            bs[plane, row : row + 8] = pltpu.roll(value, 64, 1)

    def outer(ref, plane, here):
        return jnp.where(first_half, ref[plane - 1, here], ref[plane + 1, here])

    for plane in range(1, 17):
        for row in (8, 16):
            here = slice(row, row + 8)
            b = b3[plane, here]
            partner, other = bs[plane, here], outer(bs, plane, here)
            y_high = b3[plane, row + 1 : row + 9]
            z_low = jnp.where(cell > 0, pltpu.roll(b, 1, 1), 0.0)
            z_high = jnp.where(cell < 63, pltpu.roll(b, 127, 1), 0.0)
            total = (6.0 * b + (partner + other)) + (
                (b3[plane, row - 1 : row + 7] + y_high) + (z_low + z_high)
            )
            inside = b > 0.0
            inverse = 1.0 / jnp.where(inside, total, 1.0)
            reds = jnp.where(inside & (parity == 0), inverse, 0.0)
            inner_3[plane, here] = b + partner
            outer_3[plane, here] = b + other
            fy3[plane, here] = b + y_high
            fz3[plane, here] = jnp.where(cell < 63, b + z_high, 0.0)
            d3[plane, here] = total
            ir3[plane, here] = reds
            ik3[plane, here] = jnp.where(inside & (parity == 1), inverse, 0.0)
            value = g_rows[16 * plane + row - 24 : 16 * plane + row - 16] * reds
            r3[plane, here] = value
            rs[plane, here] = pltpu.roll(value, 64, 1)

    def total_3(ref, swapped, plane, row):
        here, low, high = slice(row, row + 8), slice(row - 1, row + 7), slice(row + 1, row + 9)
        v, face = ref[plane, here], fz3[plane, here]
        along_x = inner_3[plane, here] * swapped[plane, here]
        along_x = along_x + outer_3[plane, here] * outer(swapped, plane, here)
        along_y = fy3[plane, here] * ref[plane, high] + fy3[plane, low] * ref[plane, low]
        along_z = face * pltpu.roll(v, 127, 1) + pltpu.roll(face * v, 1, 1)
        g = g_rows[16 * plane + row - 24 : 16 * plane + row - 16]
        return (g + along_x) + (along_y + along_z)

    for step in range(3):
        source, inverse, target = (
            ((r3, rs), ik3, (k3, ks)),
            ((k3, ks), ir3, (r3, rs)),
            ((r3, rs), ik3, (k3, ks)),
        )[step]
        for plane in range(1, 17):
            for row in (8, 16):
                here = slice(row, row + 8)
                value = total_3(*source, plane, row) * inverse[plane, here]
                if step == 2:
                    value = value + r3[plane, here]
                target[0][plane, here] = value
                target[1][plane, here] = pltpu.roll(value, 64, 1)

    for plane in range(1, 17):
        for row in (8, 16):
            here = slice(row, row + 8)
            value = total_3(k3, ks, plane, row) - d3[plane, here] * k3[plane, here]
            at = slice(16 * (plane - 1) + row - 8, 16 * (plane - 1) + row)
            pair_3[at] = value + pltpu.roll(value, 64, 1)
            pair_4[at] = b3[plane, here] + bs[plane, here]
    halve = pair_selector(128, 0, 128, 0, 32)
    g4[...] = 0.5 * split_matmul(halves(pair_3, 128), halve).reshape(16, 8, 128)
    b4[0] = zero
    b4[17] = zero
    b4[1:17] = 0.125 * split_matmul(halves(pair_4, 128), halve).reshape(16, 8, 128)

    parity = (row8 + lane) & 1
    for ref in (r4, k4):
        ref[0] = zero
        ref[17] = zero
    fx4[0] = b4[1]
    for plane in range(1, 17):
        b = b4[plane]
        x_high = b4[plane + 1]
        y_low = jnp.where(row8 > 0, pltpu.roll(b, 1, 0), 0.0)
        y_high = jnp.where(row8 < 7, pltpu.roll(b, 7, 0), 0.0)
        z_high = pltpu.roll(b, 127, 1)
        total = (6.0 * b + (b4[plane - 1] + x_high)) + (
            (y_low + y_high) + (pltpu.roll(b, 1, 1) + z_high)
        )
        inside = b > 0.0
        inverse = 1.0 / jnp.where(inside, total, 1.0)
        reds = jnp.where(inside & (parity == (plane - 1) & 1), inverse, 0.0)
        fx4[plane] = b + x_high
        fy4[plane] = jnp.where(row8 < 7, b + y_high, 0.0)
        fz4[plane] = jnp.where(lane < 31, b + z_high, 0.0)
        ir4[plane] = reds
        ik4[plane] = jnp.where(inside & (parity != (plane - 1) & 1), inverse, 0.0)
        r4[plane] = g4[plane - 1] * reds

    def half_4(source, inverse, target):
        for first in range(1, 17, 2):
            pair = (first, first + 1)
            v = source[first] + source[first + 1]
            y_face = fy4[first] * source[first] + fy4[first + 1] * source[first + 1]
            z_face = fz4[first] * source[first] + fz4[first + 1] * source[first + 1]
            y_high, y_low = pltpu.roll(v, 7, 0), pltpu.roll(y_face, 1, 0)
            z_high, z_low = pltpu.roll(v, 127, 1), pltpu.roll(z_face, 1, 1)
            for plane in pair:
                along_x = fx4[plane] * source[plane + 1] + fx4[plane - 1] * source[plane - 1]
                along_y = fy4[plane] * y_high + y_low
                along_z = fz4[plane] * z_high + z_low
                value = (g4[plane - 1] + along_x) + (along_y + along_z)
                target[plane] = value * inverse[plane]

    half_4(r4, ik4, k4)

    @pl.loop(1, COARSE_SWEEPS)
    def _(sweep):
        half_4(k4, ir4, r4)
        half_4(r4, ik4, k4)

    source = iota((128, 128), 0)
    target = iota((128, 128), 1)
    spread = selector_of((source < 32) & (((target & 63) >> 1) == source))
    value = split_matmul(r4[at_x + 1] + k4[at_x + 1], spread)
    twice_3[pl.ds(0, 8, stride=2), :] = value
    twice_3[pl.ds(1, 8, stride=2), :] = value
    value = k3[at_x + 1, 8:24] + twice_3[...]
    value = pltpu.roll(value, lax.rem(16 - 2 * at_y, 16), 0)
    value = pltpu.roll(value, lax.rem(128 - 16 * at_z, 128), 1)
    level_2 = []
    for part in range(2):
        fine = split_matmul(value, spread_selector(64 * part, 0, 16))[0:8]
        twice_2[pl.ds(0, 8, stride=2), :] = fine
        twice_2[pl.ds(1, 8, stride=2), :] = fine
        for index in range(2):
            own = u2_ref[2 * part + index]
            own = pltpu.roll(own, lax.rem(128 - 32 * at_z, 128), 1)
            level_2.append(own + twice_2[0:8])
    fine = split_matmul(jnp.concatenate(level_2, axis=0), spread_selector(0, 0, 32))
    twice_1[pl.ds(0, 32, stride=2), :] = fine
    twice_1[pl.ds(1, 32, stride=2), :] = fine
    for index in range(8):
        start = 16 * (index // 2)
        level_1[8 * index : 8 * index + 8] = u1_ref[index] + twice_1[start : start + 8]
    fine = split_matmul(level_1[...], spread_selector(0, 0, 64))
    twice_0[pl.ds(0, 64, stride=2), :] = fine
    twice_0[pl.ds(1, 64, stride=2), :] = fine
    for index in range(16):
        start = 16 * (index // 2)
        out_ref[index] = u0_ref[index] + twice_0[start : start + 16]


def call(kernel, megabytes, outs, scratch, *operands):
    whole = pl.BlockSpec(memory_space=pltpu.VMEM)
    return pl.pallas_call(
        kernel,
        out_shape=[jax.ShapeDtypeStruct(shape, F32) for shape in outs],
        in_specs=[whole] * len(operands),
        out_specs=[whole] * len(outs),
        scratch_shapes=[pltpu.VMEM(shape, F32) for shape in scratch],
        compiler_params=pltpu.CompilerParams(vmem_limit_bytes=megabytes << 20),
    )(*operands)


def shift(value, axis, step):
    count = lax.axis_size(axis)
    pairs = [(i, i + step) for i in range(count) if 0 <= i + step < count]
    return lax.ppermute(value, axis, pairs)


def around(value, axis, step):
    count = lax.axis_size(axis)
    return lax.ppermute(value, axis, [(i, (i + step) % count) for i in range(count)])


def swap(value, axis, first):
    count = lax.axis_size(axis)
    lower = range(first, count - 1, 2)
    pairs = [(i, i + 1) for i in lower] + [(i + 1, i) for i in lower]
    return lax.ppermute(value, axis, pairs)


def on_device(right_side, conductivity):
    f, b = right_side, conductivity
    upper = jnp.concatenate([f[BLOCK - F_HALO :], b[BLOCK - B_HALO :]], axis=0)
    lower = jnp.concatenate([f[:F_HALO], b[:B_HALO]], axis=0)
    low, high = shift(upper, "gx", 1), shift(lower, "gx", -1)

    strip = (GROUPS, BLOCK, 128)
    packed = (PACKED, 128)
    main, left, right, down, up = call(
        pack_kernel, 4, [(PLANES, BLOCK, 128), strip, strip, packed, packed], [], f, b, low, high
    )
    first, second = swap(left, "gz", 0), swap(right, "gz", 1)
    down, up, after, before = call(
        join_kernel, 4, [(PAYLOAD, 128)] * 2 + [strip] * 2, [], down, up, first, second
    )
    low, high = around(up, "gy", 1), around(down, "gy", -1)

    u0, u1, coarse = call(
        fine_kernel,
        40,
        [(BLOCK, BLOCK, 128), (8, 8, 128), (16, 16, 128)],
        Level.scratch(2, B_PLANES, ROWS)
        + Level.scratch(1, 20, 24)
        + [(512, 128)] * 2
        + [(864, 128)] * 2
        + [(128, 128)],
        low, high, main, after, before,
    )

    column = lax.all_to_all(coarse, "gx", 0, 0, tiled=True)
    (column,) = call(squeeze_kernel, 2, [(4, 160, 128)], [], column.reshape(256, 128))
    column = lax.all_to_all(column, "gz", 0, 0, tiled=True)
    column, up, down = call(line_kernel, 4, [(640, 128), (576, 128), (576, 128)], [], column)
    low, high = around(up, "gy", 1), around(down, "gy", -1)
    u2, coarse = call(
        column_kernel,
        13,
        [(4, 8, 128), (8, 64, 128)],
        Level.scratch(1, 14, 112),
        low, column, high,
    )

    whole = lax.all_to_all(coarse, "gy", 0, 0, tiled=True)
    (out,) = call(
        coarse_kernel,
        8,
        [(BLOCK, BLOCK, 128)],
        [(18, 32, 128)] * 13
        + [(18, 8, 128)] * 7
        + [(16, 8, 128), (18, 8, 128)]
        + [(256, 128)] * 4
        + [(16, 128), (16, 128), (64, 128), (128, 128), (64, 128)],
        whole, u0, u1, u2,
    )
    return out


def solution(mesh):
    spec = P("gx", "gy", "gz")
    return jax.shard_map(
        on_device, mesh=mesh, in_specs=(spec, spec), out_specs=spec, check_vma=False
    )
```
